32 devices in a mesh: dp: 8 (over y, x, core), tensor: 4 (over z).
Axes of the slice: x: 2, y: 2, z: 4, core: 2. Of those that a mesh axis runs over, the one named last changes fastest.
Arguments:
- block_input: bfloat16 [32768, 768], P(('dp', 'tensor')), may hold values from -6 to 6
- embedding: bfloat16 [32768, 768], P(('dp', 'tensor')), may hold values from -6 to 6
- history: bfloat16 [3, 32768, 768], P(None, ('dp', 'tensor')), may hold values from -6 to 6
- cotangent: bfloat16 [32768, 768], P(('dp', 'tensor')), may hold values from -6 to 6
- first_gain: float32 [768], replicated, may hold values from 0.5 to 1.5
- first_shift: float32 [768], replicated, may hold values from -1.75 to 1.75
- qkv_weight: bfloat16 [768, 3, 768], P(None, None, 'tensor'), may hold values from -0.4375 to 0.4375
- qkv_bias: bfloat16 [3, 768], P(None, 'tensor'), may hold values from -3 to 3
- out_weight: bfloat16 [768, 768], P('tensor'), may hold values from -0.4375 to 0.4375
- out_bias: bfloat16 [768], replicated, may hold values from -1.75 to 1.75
- second_gain: float32 [768], replicated, may hold values from 0.5 to 1.5
- second_shift: float32 [768], replicated, may hold values from -1.75 to 1.75
- up_weight: bfloat16 [768, 3072], P(None, 'tensor'), may hold values from -0.21875 to 0.21875
- up_bias: bfloat16 [3072], P('tensor'), may hold values from -3 to 3
- down_weight: bfloat16 [3072, 768], P('tensor'), may hold values from -0.21875 to 0.21875
- down_bias: bfloat16 [768], replicated, may hold values from -1.75 to 1.75
- depth_weights: float32 [5], replicated, may hold values from 0.2 to 0.8
- prefix_length: int32 [8], P('dp'), may hold values from 409 to 2048
- history_index: int32 [3], replicated, may hold values from 0 to 2, each once
Outputs:
- dwa_output: bfloat16 [32768, 768], P(('dp', 'tensor'))
- grad_input: float32 [32768, 768], P(('dp', 'tensor'))
- grad_first_gain: float32 [768], replicated
- grad_first_shift: float32 [768], replicated
- grad_qkv_weight: float32 [768, 3, 768], P(None, None, 'tensor')
- grad_qkv_bias: float32 [3, 768], P(None, 'tensor')
- grad_out_weight: float32 [768, 768], P('tensor')
- grad_out_bias: float32 [768], replicated
- grad_second_gain: float32 [768], replicated
- grad_second_shift: float32 [768], replicated
- grad_up_weight: float32 [768, 3072], P(None, 'tensor')
- grad_up_bias: float32 [3072], P('tensor')
- grad_down_weight: float32 [3072, 768], P('tensor')
- grad_down_bias: float32 [768], replicated
- grad_depth: float32 [5], replicated
The draws below stay inside these ranges and needn't reach their ends.
Inputs may be any that keep to these rules, and one draw needn't show every extreme that they name: `history_index`: each of the three slots is named once.
All inputs are finite; a program needn't handle non-finite values.
Results may differ from the reference program's by a relative error of at most 0.015.
The reference program's roundings to bfloat16 on the way count: a program that leaves them out, or rounds other values in their place, can miss the bound.
Values may be sent and summed in bfloat16 or wider, within the bound.
A program may use at most 256 MiB of HBM per device.

```python
import jax
import jax.numpy as jnp
from jax import lax

D = 768
HEADS = 12
HEAD_DIM = 64
FF = 3072
LENGTH = 4096
QBLOCK = 512
SEQS = 8
TOKENS = 32768


def plant(entries, stream_key, low, largest):
    index_at = [jax.random.randint(jax.random.fold_in(stream_key, axis), (), 0, length) for axis, length in enumerate(entries.shape)]
    widest = entries.shape.index(max(entries.shape))
    neighbour = index_at[:widest] + [(index_at[widest] + 1) % entries.shape[widest]] + index_at[widest + 1:]
    return entries.at[tuple(index_at)].set(low).at[tuple(neighbour)].set(largest)


def shard_levels(rng, dims, pieces, least, largest):
    level = 1.0
    for position, shards_of in pieces:
        steps = jax.random.uniform(jax.random.fold_in(jax.random.fold_in(rng, 6), position), (shards_of,), jnp.float32, least / len(pieces), largest / len(pieces))
        level = level * jnp.repeat(jnp.exp(steps), dims[position] // shards_of).reshape((-1,) + (1,) * (len(dims) - 1 - position))
    return level


def scatter_about(own_key, extent, scale, reach, pieces=(), kind=jnp.bfloat16):
    drawn = scale * jax.random.normal(own_key, extent, jnp.float32)
    if pieces:
        drawn = drawn * shard_levels(own_key, extent, pieces, -0.22, 0.18)
    return jnp.clip(drawn, -reach, reach).astype(kind)


def setup_inputs(seed: int = 0) -> dict:
    arg_keys = jax.random.split(jax.random.key(seed), 20)
    block_input = scatter_about(arg_keys[0], (TOKENS, D), 1.0, 6.0, ((0, 32),))
    embedding = scatter_about(arg_keys[1], (TOKENS, D), 1.0, 6.0, ((0, 32),))
    history = scatter_about(arg_keys[2], (3, TOKENS, D), 1.0, 6.0, ((1, 32),))
    cotangent = scatter_about(arg_keys[3], (TOKENS, D), 1.0, 6.0, ((0, 32),))
    first_gain = jnp.clip(1.0 + 0.1 * jax.random.normal(arg_keys[4], (D,), jnp.float32), 0.5, 1.5)
    first_shift = scatter_about(arg_keys[5], (D,), 0.3, 1.75, (), jnp.float32)
    qkv_weight = scatter_about(arg_keys[6], (D, 3, D), (D // 4) ** -0.5, 0.4375, ((2, 4),))
    qkv_bias = scatter_about(arg_keys[7], (3, D), 0.5, 3.0, ((1, 4),))
    out_weight = scatter_about(arg_keys[8], (D, D), (D // 4) ** -0.5, 0.4375, ((0, 4),))
    out_bias = scatter_about(arg_keys[9], (D,), 0.3, 1.75)
    second_gain = jnp.clip(1.0 + 0.1 * jax.random.normal(arg_keys[10], (D,), jnp.float32), 0.5, 1.5)
    second_shift = scatter_about(arg_keys[11], (D,), 0.3, 1.75, (), jnp.float32)
    up_weight = scatter_about(arg_keys[12], (D, FF), D ** -0.5, 0.21875, ((1, 4),))
    up_bias = scatter_about(arg_keys[13], (FF,), 0.5, 3.0, ((0, 4),))
    down_weight = scatter_about(arg_keys[14], (FF, D), (FF // 4) ** -0.5, 0.21875, ((0, 4),))
    down_bias = scatter_about(arg_keys[15], (D,), 0.3, 1.75)
    depth_weights = jnp.clip(jax.random.uniform(arg_keys[16], (5,), jnp.float32, 0.2, 0.8), 0.2, 0.8)
    prefix_length = plant(jax.random.randint(arg_keys[17], (SEQS,), LENGTH // 10, LENGTH // 2 + 1), jax.random.fold_in(arg_keys[17], 1), LENGTH // 10, (LENGTH // 2 + 1) - 1).astype(jnp.int32)
    history_index = jax.random.permutation(arg_keys[18], 3).astype(jnp.int32)
    return {"block_input": block_input, "embedding": embedding, "history": history, "cotangent": cotangent, "first_gain": first_gain, "first_shift": first_shift, "qkv_weight": qkv_weight, "qkv_bias": qkv_bias, "out_weight": out_weight, "out_bias": out_bias, "second_gain": second_gain, "second_shift": second_shift, "up_weight": up_weight, "up_bias": up_bias, "down_weight": down_weight, "down_bias": down_bias, "depth_weights": depth_weights, "prefix_length": prefix_length, "history_index": history_index}


EPS = 1e-05
ROPE_BASE = 10000.0
GELU_C = 0.7978845608028654
NEG_FILL = -1e+30
HIGH = lax.Precision.HIGHEST

@jax.custom_vjp
def low(v):
    return lax.optimization_barrier(v.astype(jnp.bfloat16)).astype(jnp.float32)

@jax.custom_vjp
def low_back(v):
    return v

def low_keep(v):
    return (low(v), None)

def low_pass(kept, grad):
    return (grad,)

def back_keep(v):
    return (v, None)

def back_low(kept, grad):
    return (low(grad),)
low.defvjp(low_keep, low_pass)
low_back.defvjp(back_keep, back_low)

def layer_norm(values, norm_gain, norm_shift):
    center = values - lax.optimization_barrier(jnp.mean(values, axis=-1, keepdims=True))
    spread = lax.optimization_barrier(jnp.mean(center * center, axis=-1, keepdims=True))
    return center * lax.rsqrt(spread + EPS) * norm_gain + norm_shift

def gelu_tanh(values):
    inner = GELU_C * (values + 0.044715 * values * values * values)
    return 0.5 * values * (1.0 + jnp.tanh(inner))

def rotary_tables(length, head_size):
    half_dim = head_size // 2
    frequency = ROPE_BASE ** (-jnp.arange(half_dim, dtype=jnp.float32) / half_dim)
    angles = jnp.arange(length, dtype=jnp.float32)[:, None] * frequency[None, :]
    return (jnp.cos(angles), jnp.sin(angles))

def rotate(values, cosine_table, sine_table):
    half_dim = values.shape[-1] // 2
    front_half = values[..., :half_dim]
    back_half = values[..., half_dim:]
    return jnp.concatenate([front_half * cosine_table - back_half * sine_table, back_half * cosine_table + front_half * sine_table], axis=-1)

def visible(row_start, block_rows, length, prefix):
    key_pos = jnp.arange(length, dtype=jnp.int32)
    query_pos = row_start + jnp.arange(block_rows, dtype=jnp.int32)
    return (key_pos[None, :] <= query_pos[:, None]) | (key_pos[None, :] < prefix)

def matmul(left, right):
    return jnp.dot(left, right, precision=HIGH, preferred_element_type=jnp.float32)

def forward_sequence(block_in, embed_rows, stack_rows, params, prefix, history_index):
    first_gain, first_shift, qkv_weight, qkv_bias, out_weight, out_bias, second_gain, second_shift, up_weight, up_bias, down_weight, down_bias, depth_weights = params
    length = block_in.shape[0]
    model_width = block_in.shape[1]
    normed = low(layer_norm(block_in, first_gain, first_shift))
    project = low_back(matmul(normed, qkv_weight.reshape(model_width, 3 * model_width)) + qkv_bias.reshape(-1))
    project = project.reshape(length, 3, HEADS, HEAD_DIM).transpose(1, 2, 0, 3)
    cosine_table, sine_table = rotary_tables(length, HEAD_DIM)
    query_rows = low(rotate(project[0], cosine_table, sine_table))
    key_rows = low(rotate(project[1], cosine_table, sine_table))
    value_rows = low(project[2])
    score_scale = HEAD_DIM ** (-0.5)

    def attend(row_start):
        query_part = lax.dynamic_slice_in_dim(query_rows, row_start, QBLOCK, 1)
        scores = low_back(jnp.einsum('hqd,hkd->hqk', query_part, key_rows, precision=HIGH) * score_scale)
        masked = jnp.where(visible(row_start, QBLOCK, length, prefix)[None], scores, NEG_FILL)
        maxima = lax.optimization_barrier(jnp.max(masked, axis=-1, keepdims=True))
        exponent = jnp.exp(masked - maxima)
        weights_soft = low(exponent / lax.optimization_barrier(jnp.sum(exponent, axis=-1, keepdims=True)))
        return low(low_back(jnp.einsum('hqk,hkd->hqd', weights_soft, value_rows, precision=HIGH)))
    starts = (jnp.arange(length // QBLOCK) * QBLOCK).astype(jnp.int32)
    blocks = lax.map(jax.checkpoint(attend), starts)
    attended = blocks.transpose(0, 2, 1, 3).reshape(length, model_width)
    attn_branch = low_back(matmul(attended, out_weight) + out_bias)
    middle = block_in + attn_branch
    normed_mid = low(layer_norm(middle, second_gain, second_shift))
    hidden_pre = low_back(matmul(normed_mid, up_weight) + up_bias)
    hidden_act = low(gelu_tanh(hidden_pre))
    mlp_branch = low_back(matmul(hidden_act, down_weight) + down_bias)
    block_out = middle + mlp_branch
    chosen = stack_rows[history_index]
    return depth_weights[0] * embed_rows + depth_weights[1] * chosen[0] + depth_weights[2] * chosen[1] + depth_weights[3] * chosen[2] + depth_weights[4] * block_out

def reference(block_input, embedding, history, cotangent, first_gain, first_shift, qkv_weight, qkv_bias, out_weight, out_bias, second_gain, second_shift, up_weight, up_bias, down_weight, down_bias, depth_weights, prefix_length, history_index):
    params = tuple((item.astype(jnp.float32) for item in (first_gain, first_shift, qkv_weight, qkv_bias, out_weight, out_bias, second_gain, second_shift, up_weight, up_bias, down_weight, down_bias, depth_weights)))
    input_seqs = block_input.astype(jnp.float32).reshape(SEQS, LENGTH, D)
    embed_seqs = embedding.astype(jnp.float32).reshape(SEQS, LENGTH, D)
    stack_seqs = history.astype(jnp.float32).reshape(3, SEQS, LENGTH, D).transpose(1, 0, 2, 3)
    cotan_seqs = cotangent.astype(jnp.float32).reshape(SEQS, LENGTH, D)
    initial = tuple((jnp.zeros_like(item) for item in params))

    def one_sequence(running, seq_items):
        block_in, embed_rows, stack_rows, cotan_rows, prefix = seq_items

        def apply_layer(first_arg, param_arg):
            return forward_sequence(first_arg, embed_rows, stack_rows, param_arg, prefix, history_index)
        result, pull_back = jax.vjp(apply_layer, block_in, params)
        grad_block_in, grad_params = pull_back(cotan_rows)
        running = tuple((left + right for left, right in zip(running, grad_params)))
        return (running, (result.astype(jnp.bfloat16), grad_block_in))
    totals, (outputs, grad_inputs) = lax.scan(one_sequence, initial, (input_seqs, embed_seqs, stack_seqs, cotan_seqs, prefix_length))
    return (outputs.reshape(TOKENS, D), grad_inputs.reshape(TOKENS, D), totals[0], totals[1], totals[2], totals[3], totals[4], totals[5], totals[6], totals[7], totals[8], totals[9], totals[10], totals[11], totals[12])
```

```python
import functools

import jax
import jax.numpy as jnp
from jax import lax
from jax.experimental import pallas as pl
from jax.experimental.pallas import tpu as pltpu
from jax.sharding import PartitionSpec as P
HD=64
NEG=-1e30
LOG2E=1.4426950408889634
F32=jnp.float32; BF=jnp.bfloat16

def dg(a,b,ca,cb):
    return lax.dot_general(a,b,(((ca,),(cb,)),((),())),preferred_element_type=F32)

def fwd_kernel(BQ,BK,SUB,pref_ref,q_ref,k_ref,v_ref,ob_ref,of_ref,lse_ref,k2_ref,v2_ref,m_ref,acc_ref):
    i=pl.program_id(0)
    length=k_ref.shape[-1]
    nk=length//BK
    @pl.when(i==0)
    def _():
        for c in range(nk):
            kt=k_ref[:,c*BK:(c+1)*BK].astype(F32).T.astype(BF)
            k2_ref[c*BK:(c+1)*BK,:]=jnp.concatenate([kt,kt],axis=1)
            v2_ref[c,0:HD,:]=v_ref[:,c*BK:(c+1)*BK]
            row=lax.broadcasted_iota(jnp.int32,(16,BK),0)
            v2_ref[c,HD:HD+16,:]=jnp.where(row==0,1.0,0.0).astype(BF)
    prefix=pref_ref[0]
    qs=q_ref[...].astype(F32)*(LOG2E/8.0)
    hi=qs.astype(BF)
    lo=(qs-hi.astype(F32)).astype(BF)
    q2=jnp.concatenate([hi,lo],axis=0)
    m_ref[...]=jnp.full(m_ref.shape,NEG,F32)
    acc_ref[...]=jnp.zeros(acc_ref.shape,F32)
    def block(j,masked):
        kj=k2_ref[pl.ds(pl.multiple_of(j*BK,BK),BK),:]
        vj=v2_ref[j]
        for s0 in range(0,BQ,SUB):
            s=dg(kj,q2[:,s0:s0+SUB],1,0)
            if masked:
                kp=j*BK+lax.broadcasted_iota(jnp.int32,(BK,SUB),0)
                qp=i*BQ+s0+lax.broadcasted_iota(jnp.int32,(BK,SUB),1)
                s=jnp.where((kp<=qp)|(kp<prefix),s,NEG)
            m=m_ref[:,s0:s0+SUB]
            mn=jnp.maximum(m,jnp.max(s,axis=0,keepdims=True))
            p=jnp.exp2(s-mn).astype(BF)
            al=jnp.exp2(m-mn)
            m_ref[:,s0:s0+SUB]=mn
            acc_ref[:,s0:s0+SUB]=acc_ref[:,s0:s0+SUB]*al+dg(vj,p,1,0)
    nfull=jnp.maximum((i*BQ+1)//BK, prefix//BK)
    nvis=jnp.maximum(((i+1)*BQ+BK-1)//BK, (prefix+BK-1)//BK)
    nfull=jnp.minimum(nfull,nk); nvis=jnp.minimum(nvis,nk)
    def lf(j,_):
        block(j,False); return 0
    def lm(j,_):
        block(j,True); return 0
    lax.fori_loop(0,nfull,lf,0)
    lax.fori_loop(nfull,nvis,lm,0)
    l=acc_ref[HD:HD+1,:]
    o=acc_ref[0:HD,:]/l
    ob_ref[...]=o.astype(BF)
    of_ref[...]=o
    lse_ref[...]=m_ref[...]+jnp.log2(l)

def fwd(prefix,qkv,h,nchunk,BQ=1024,BK=512,SUB=512):
    L=qkv.shape[-1]
    nq=L//BQ; CL=L//nchunk; per=CL//BQ
    sq=pl.Squeezed()
    return pl.pallas_call(
        functools.partial(fwd_kernel,BQ,BK,SUB),
        grid_spec=pltpu.PrefetchScalarGridSpec(num_scalar_prefetch=1,grid=(nq,),
            in_specs=[pl.BlockSpec((sq,sq,HD,BQ),lambda i,p:(h,0,0,i)),
                      pl.BlockSpec((sq,sq,HD,L),lambda i,p:(h,1,0,0)),
                      pl.BlockSpec((sq,sq,HD,L),lambda i,p:(h,2,0,0))],
            out_specs=[pl.BlockSpec((sq,HD,BQ),lambda i,p:(i//per,0,i%per)),
                       pl.BlockSpec((HD,BQ),lambda i,p:(0,i)),
                       pl.BlockSpec((1,BQ),lambda i,p:(0,i))],
            scratch_shapes=[pltpu.VMEM((L,2*HD),BF),pltpu.VMEM((L//BK,HD+16,BK),BF),pltpu.VMEM((1,BQ),F32),pltpu.VMEM((HD+16,BQ),F32)]),
        out_shape=[jax.ShapeDtypeStruct((nchunk,HD,CL),BF),jax.ShapeDtypeStruct((HD,L),F32),jax.ShapeDtypeStruct((1,L),F32)],
        compiler_params=pltpu.CompilerParams(dimension_semantics=("arbitrary",),vmem_limit_bytes=48*2**20),
        cost_estimate=pl.CostEstimate(flops=int(4*256*L*L*0.6),bytes_accessed=4*HD*L*2,transcendentals=int(L*L*0.6)),
        name="attend_fwd")(prefix,qkv,qkv,qkv)

def unrot(f,b,c,s):
    return f*c+b*s, b*c-f*s

def bwd_kernel(BQ,BK,SUB,nchunk,pref_ref,q_ref,k_ref,v_ref,do_ref,of_ref,lse_ref,cos_ref,sin_ref,g_ref,
               q2_ref,qn_ref,dn_ref,don_ref,dd_ref,dq_ref,dk_ref,dv_ref):
    j=pl.program_id(0)
    length=q_ref.shape[-1]
    nq=length//BQ; nj=length//BK
    CL=length//nchunk; perq=CL//BQ
    @pl.when(j==0)
    def _():
        for c in range(nq):
            qf=q_ref[:,c*BQ:(c+1)*BQ].astype(F32)
            qs=qf*(LOG2E/8.0)
            hi=qs.astype(BF); lo=(qs-hi.astype(F32)).astype(BF)
            q2_ref[c]=jnp.concatenate([hi,lo],axis=0)
            qn_ref[c]=qf.T.astype(BF)
            t,o=c//perq,(c%perq)*BQ
            dof=do_ref[t,:,o:o+BQ].astype(F32)
            dn_ref[c]=do_ref[t,:,o:o+BQ]
            don_ref[c]=dof.T.astype(BF)
            dd_ref[c]=jnp.concatenate([jnp.sum(dof*of_ref[:,c*BQ:(c+1)*BQ],axis=0,keepdims=True),lse_ref[:,c*BQ:(c+1)*BQ]],axis=0)
            dq_ref[c]=jnp.zeros((HD,BQ),F32)
    prefix=pref_ref[0]
    kt=k_ref[...]
    kn=kt.astype(F32).T.astype(BF)
    k2=jnp.concatenate([kn,kn],axis=1)
    vn=v_ref[...].astype(F32).T.astype(BF)
    dk_ref[...]=jnp.zeros(dk_ref.shape,F32)
    dv_ref[...]=jnp.zeros(dv_ref.shape,F32)
    def block(i,masked):
        for s0 in range(0,BQ,SUB):
            sl=slice(s0,s0+SUB)
            s=dg(k2,q2_ref[i,:,sl],1,0)
            p=jnp.exp2(s-dd_ref[i,1:2,sl])
            if masked:
                kp=j*BK+lax.broadcasted_iota(jnp.int32,(BK,SUB),0)
                qp=i*BQ+s0+lax.broadcasted_iota(jnp.int32,(BK,SUB),1)
                p=jnp.where((kp<=qp)|(kp<prefix),p,0.0)
            dp=dg(vn,dn_ref[i,:,sl],1,0)
            dv_ref[...]+=dg(p.astype(BF),don_ref[i,sl,:],1,0)
            ds=(p*(dp-dd_ref[i,0:1,sl])).astype(BF)
            dk_ref[...]+=dg(ds,qn_ref[i,sl,:],1,0)
            dq_ref[i,:,sl]+=dg(kt,ds,1,0)
    k0=j*BK; k1=k0+BK
    start=jnp.where(k0<prefix,0,k0//BQ)
    mend=jnp.where(k1<=prefix,start,(k1+BQ-1)//BQ)
    def lm(i,_):
        block(i,True); return 0
    def lf(i,_):
        block(i,False); return 0
    lax.fori_loop(start,mend,lm,0)
    lax.fori_loop(mend,nq,lf,0)
    dk=dk_ref[...].T*0.125
    dv=dv_ref[...].T
    perk=CL//BK
    t=j//perk; o=pl.multiple_of((j%perk)*BK,BK)
    c=cos_ref[:,pl.ds(pl.multiple_of(k0,BK),BK)]; s=sin_ref[:,pl.ds(pl.multiple_of(k0,BK),BK)]
    a,b=unrot(dk[0:32],dk[32:64],c,s)
    g_ref[t,HD:HD+32,pl.ds(o,BK)]=a.astype(BF)
    g_ref[t,HD+32:2*HD,pl.ds(o,BK)]=b.astype(BF)
    g_ref[t,2*HD:3*HD,pl.ds(o,BK)]=dv.astype(BF)
    @pl.when(j==nj-1)
    def _():
        for c in range(nq):
            t,o=c//perq,(c%perq)*BQ
            x=dq_ref[c]*0.125
            a,b=unrot(x[0:32],x[32:64],cos_ref[:,c*BQ:(c+1)*BQ],sin_ref[:,c*BQ:(c+1)*BQ])
            g_ref[t,0:32,o:o+BQ]=a.astype(BF)
            g_ref[t,32:64,o:o+BQ]=b.astype(BF)

def bwd(prefix,qkv,h,do,of,lse,cosT,sinT,BQ=1024,BK=512,SUB=256):
    L=qkv.shape[-1]; nchunk=do.shape[0]; CL=L//nchunk; nq=L//BQ
    sq=pl.Squeezed()
    full=lambda shp:pl.BlockSpec(shp,lambda j,p:(0,)*len(shp))
    return pl.pallas_call(
        functools.partial(bwd_kernel,BQ,BK,SUB,nchunk),
        grid_spec=pltpu.PrefetchScalarGridSpec(num_scalar_prefetch=1,grid=(L//BK,),
            in_specs=[pl.BlockSpec((sq,sq,HD,L),lambda j,p:(h,0,0,0)),
                      pl.BlockSpec((sq,sq,HD,BK),lambda j,p:(h,1,0,j)),
                      pl.BlockSpec((sq,sq,HD,BK),lambda j,p:(h,2,0,j)),
                      full((nchunk,HD,CL)),full((HD,L)),full((1,L)),full((32,L)),full((32,L))],
            out_specs=full((nchunk,3*HD,CL)),
            scratch_shapes=[pltpu.VMEM((nq,2*HD,BQ),BF),pltpu.VMEM((nq,BQ,HD),BF),pltpu.VMEM((nq,HD,BQ),BF),pltpu.VMEM((nq,BQ,HD),BF),
                pltpu.VMEM((nq,2,BQ),F32),pltpu.VMEM((nq,HD,BQ),F32),pltpu.VMEM((BK,HD),F32),pltpu.VMEM((BK,HD),F32)]),
        out_shape=jax.ShapeDtypeStruct((nchunk,3*HD,CL),BF),
        compiler_params=pltpu.CompilerParams(dimension_semantics=("arbitrary",),vmem_limit_bytes=48*2**20),
        cost_estimate=pl.CostEstimate(flops=int(10*256*L*L*0.6),bytes_accessed=10*HD*L*2,transcendentals=int(L*L*0.6)),
        name="attend_bwd")(prefix,qkv,qkv,qkv,do,of,lse,cosT,sinT)


EPS = 1e-05
ROPE_BASE = 10000.0
GELU_C = 0.7978845608028654


def layer_norm(values, norm_gain, norm_shift):
    center = values - jnp.mean(values, axis=-1, keepdims=True)
    spread = jnp.mean(center * center, axis=-1, keepdims=True)
    return center * lax.rsqrt(spread + EPS) * norm_gain + norm_shift


def rotary_tables(length):
    half_dim = HD // 2
    frequency = ROPE_BASE ** (-jnp.arange(half_dim, dtype=jnp.float32) / half_dim)
    angles = frequency[:, None] * jnp.arange(length, dtype=jnp.float32)[None, :]
    return (jnp.cos(angles), jnp.sin(angles))


def project_kernel(heads, x_ref, gain_ref, shift_ref, w_ref, b_ref, cos_ref, sin_ref, qkv_ref, normed_ref):
    normed = layer_norm(x_ref[...].astype(F32), gain_ref[...], shift_ref[...]).astype(BF)
    normed_ref[...] = normed
    c, s = cos_ref[...], sin_ref[...]
    proj = dg(w_ref[...], normed, 1, 1) + b_ref[...]
    for h in range(heads):
        for part in range(3):
            r0 = (h * 3 + part) * HD
            u = proj[r0 : r0 + HD]
            if part < 2:
                f, b = u[: HD // 2], u[HD // 2 :]
                qkv_ref[h, part, : HD // 2] = (f * c - b * s).astype(BF)
                qkv_ref[h, part, HD // 2 :] = (b * c + f * s).astype(BF)
            else:
                qkv_ref[h, part] = u.astype(BF)


def project(gathered, gain, shift, w_t, bias, cos_t, sin_t, block=512):
    length, width = gathered.shape
    cols = w_t.shape[0]
    heads = cols // (3 * HD)
    const = lambda shape: pl.BlockSpec(shape, lambda i: (0,) * len(shape))
    return pl.pallas_call(
        functools.partial(project_kernel, heads),
        grid=(length // block,),
        in_specs=[
            pl.BlockSpec((block, width), lambda i: (i, 0)),
            const((1, width)),
            const((1, width)),
            const((cols, width)),
            const((cols, 1)),
            pl.BlockSpec((HD // 2, block), lambda i: (0, i)),
            pl.BlockSpec((HD // 2, block), lambda i: (0, i)),
        ],
        out_specs=[
            pl.BlockSpec((heads, 3, HD, block), lambda i: (0, 0, 0, i)),
            pl.BlockSpec((block, width), lambda i: (i, 0)),
        ],
        out_shape=[
            jax.ShapeDtypeStruct((heads, 3, HD, length), BF),
            jax.ShapeDtypeStruct((length, width), BF),
        ],
        compiler_params=pltpu.CompilerParams(vmem_limit_bytes=48 * 2**20),
        cost_estimate=pl.CostEstimate(
            flops=2 * length * width * cols, bytes_accessed=length * (width * 4 + cols * 2), transcendentals=length
        ),
        name="project_qkv",
    )(gathered, gain[None], shift[None], w_t, bias[:, None], cos_t, sin_t)


def mlp_kernel(nm_ref, gm_ref, up_ref, upb_ref, down_ref, out_ref, dnm_ref, dup_ref, ddown_ref, dupb_ref, nmt_ref, gmt_ref):
    step = pl.program_id(0)

    @pl.when(step == 0)
    def _():
        nmt_ref[...] = nm_ref[...].T
        gmt_ref[...] = gm_ref[...].T
        out_ref[...] = jnp.zeros(out_ref.shape, F32)
        dnm_ref[...] = jnp.zeros(dnm_ref.shape, F32)

    up, down = up_ref[...], down_ref[...]
    pre = dg(nm_ref[...], up, 1, 0) + upb_ref[...]
    sq = pre * pre
    th = jnp.tanh(GELU_C * (pre + 0.044715 * sq * pre))
    half = 0.5 * (1.0 + th)
    act = (pre * half).astype(BF)
    slope = half + 0.5 * pre * (1.0 - th * th) * (GELU_C + (3.0 * 0.044715 * GELU_C) * sq)
    gp = dg(gm_ref[...], down, 1, 1) * slope
    gpb = gp.astype(BF)
    out_ref[...] += dg(act, down, 1, 0)
    dnm_ref[...] += dg(gpb, up, 1, 1)
    dup_ref[...] = dg(nmt_ref[...], gpb, 1, 0).astype(BF)
    ddown_ref[...] = dg(gmt_ref[...], act, 1, 0).astype(BF)
    dupb_ref[...] = jnp.sum(gpb.astype(F32), axis=0, keepdims=True)


def mlp(nm, gm, up, up_bias, down, chunk=256):
    rows, width = nm.shape
    n, _, f = up.shape
    per = f // chunk
    squeezed = pl.Squeezed()
    const = pl.BlockSpec((rows, width), lambda i: (0, 0))
    hidden = n * f
    return pl.pallas_call(
        mlp_kernel,
        grid=(n * per,),
        in_specs=[
            const,
            const,
            pl.BlockSpec((squeezed, width, chunk), lambda i: (i // per, 0, i % per)),
            pl.BlockSpec((1, chunk), lambda i: (0, i)),
            pl.BlockSpec((squeezed, chunk, width), lambda i: (i // per, i % per, 0)),
        ],
        out_specs=[
            const,
            const,
            pl.BlockSpec((squeezed, width, chunk), lambda i: (i // per, 0, i % per)),
            pl.BlockSpec((squeezed, width, chunk), lambda i: (i // per, 0, i % per)),
            pl.BlockSpec((1, chunk), lambda i: (0, i)),
        ],
        out_shape=[
            jax.ShapeDtypeStruct((rows, width), F32),
            jax.ShapeDtypeStruct((rows, width), F32),
            jax.ShapeDtypeStruct((n, width, f), BF),
            jax.ShapeDtypeStruct((n, width, f), BF),
            jax.ShapeDtypeStruct((1, hidden), F32),
        ],
        scratch_shapes=[pltpu.VMEM((width, rows), BF), pltpu.VMEM((width, rows), BF)],
        compiler_params=pltpu.CompilerParams(vmem_limit_bytes=56 * 2**20),
        cost_estimate=pl.CostEstimate(
            flops=12 * rows * width * hidden, bytes_accessed=8 * width * hidden + 12 * rows * width, transcendentals=rows * hidden
        ),
        name="mlp",
    )(nm, gm, up, up_bias, down)


def exchange(pieces, index, count):
    result = pieces
    for k in range(1, count):
        sent = lax.dynamic_index_in_dim(pieces, lax.rem(index + k, count), 0, keepdims=True)
        got = lax.ppermute(sent, "tensor", [(s, (s + k) % count) for s in range(count)])
        result = lax.dynamic_update_slice_in_dim(result, got, lax.rem(index + count - k, count), 0)
    return result


def gather_weight(shard, dp_index, dp_size, n):
    rows, cols = shard.shape
    part = rows // dp_size
    mine = lax.dynamic_slice_in_dim(shard, dp_index * part, part, 0)
    every = lax.all_gather(mine, ("dp", "tensor"), axis=0, tiled=False)
    return every.reshape(dp_size, n, part, cols).transpose(1, 0, 2, 3).reshape(n, rows, cols)


def total_small(vectors):
    sizes = [v.size for v in vectors]
    flat = jnp.concatenate([v.reshape(-1) for v in vectors])
    pad = -flat.size % 1024
    flat = jnp.pad(flat, (0, pad)).reshape(-1, 128)
    every = lax.all_gather(flat, ("dp", "tensor"), axis=0, tiled=False)
    summed = jnp.sum(every, axis=0).reshape(-1)
    out, at = [], 0
    for v, size in zip(vectors, sizes):
        out.append(summed[at : at + size].reshape(v.shape))
        at += size
    return out


def shards(
    block_input,
    embedding,
    history,
    cotangent,
    first_gain,
    first_shift,
    qkv_weight,
    qkv_bias,
    out_weight,
    out_bias,
    second_gain,
    second_shift,
    up_weight,
    up_bias,
    down_weight,
    down_bias,
    depth_weights,
    prefix_length,
    history_index,
):
    rows, width = block_input.shape
    local = qkv_weight.shape[2]
    heads = local // HD
    n = lax.axis_size("tensor")
    m = lax.axis_size("dp")
    z = lax.axis_index("tensor")
    dp = lax.axis_index("dp")
    length = rows * n
    hidden = up_weight.shape[1]
    cos_t, sin_t = rotary_tables(length)

    gathered = lax.all_gather(block_input, "tensor", axis=0, tiled=True)
    w_t = qkv_weight.reshape(width, 3, heads, HD).transpose(2, 1, 3, 0).reshape(3 * local, width)
    b_t = qkv_bias.reshape(3, heads, HD).transpose(1, 0, 2).reshape(3 * local).astype(F32)
    qkv_t, normed = project(gathered, first_gain, first_shift, w_t, b_t, cos_t, sin_t)

    early = jnp.concatenate([out_weight, up_weight, down_weight], axis=0)
    early, _ = lax.optimization_barrier((early, gathered))
    early_all = gather_weight(early, dp, m, n)
    out_all = early_all[:, :local].reshape(n, heads, HD, width)
    up_all = early_all[:, local : local + width]
    down_all = early_all[:, local + width :]
    up_bias_all = lax.all_gather(up_bias.astype(F32)[None], "tensor", axis=1, tiled=True)
    late, _ = lax.optimization_barrier((w_t, early_all))
    w_all = gather_weight(late, dp, m, n).reshape(n, heads, 3 * HD, width)

    inputs_f = block_input.astype(F32)
    saved, attended = [], []
    attn = None
    for h in range(heads):
        ob, of, lse = fwd(prefix_length, qkv_t, h, n)
        saved.append((of, lse))
        att = exchange(ob, z, n).reshape(n * HD, rows)
        attended.append(att)
        piece = dg(att, out_all[:, h].reshape(n * HD, width), 0, 0)
        attn = piece if attn is None else attn + piece

    middle = inputs_f + (attn + out_bias.astype(F32))
    normed_mid_f, second_pull = jax.vjp(layer_norm, middle, second_gain, second_shift)
    grad_top = cotangent.astype(F32)
    grad_block = depth_weights[4] * grad_top
    grad_branch = grad_block.astype(BF)
    mlp_out, grad_normed_mid, up_grad, down_grad_t, up_bias_grad = mlp(
        normed_mid_f.astype(BF), grad_branch, up_all, up_bias_all, down_all
    )
    block_out = middle + (mlp_out + down_bias.astype(F32))
    slot_ids = jnp.arange(3, dtype=jnp.int32)
    pick = (history_index[:, None] == slot_ids[None, :]).astype(F32)
    slot_coef = jnp.sum(depth_weights[1:4, None] * pick, axis=0)
    embed_f = embedding.astype(F32)
    mixed = depth_weights[0] * embed_f + depth_weights[4] * block_out
    for slot_id in range(3):
        mixed = mixed + slot_coef[slot_id] * history[slot_id].astype(F32)
    dwa_output = mixed.astype(BF)
    slot_sums = jnp.stack([jnp.sum(grad_top * history[slot_id].astype(F32)) for slot_id in range(3)])
    grad_depth = jnp.concatenate(
        [
            jnp.sum(grad_top * embed_f)[None],
            jnp.sum(pick * slot_sums[None, :], axis=1),
            jnp.sum(grad_top * block_out)[None],
        ]
    )
    down_bias_grad = jnp.sum(grad_branch.astype(F32), axis=0)

    grad_middle_ln, second_gain_grad, second_shift_grad = second_pull(grad_normed_mid)
    grad_middle = grad_block + grad_middle_ln
    grad_attn = grad_middle.astype(BF)
    out_bias_grad = jnp.sum(grad_attn.astype(F32), axis=0)

    grad_normed = None
    qkv_grads, qkv_bias_grads, out_grads = [], [], []
    for h in range(heads):
        grad_att = dg(out_all[:, h].reshape(n * HD, width), grad_attn, 1, 1).astype(BF)
        grad_att = exchange(grad_att.reshape(n, HD, rows), z, n)
        of, lse = saved[h]
        grad_t = bwd(prefix_length, qkv_t, h, grad_att, of, lse, cos_t, sin_t)
        back = exchange(grad_t, z, n).reshape(n * 3 * HD, rows)
        piece = dg(back, w_all[:, h].reshape(n * 3 * HD, width), 0, 0)
        grad_normed = piece if grad_normed is None else grad_normed + piece
        wgrad = None
        for t in range(n):
            term = dg(grad_t[t], normed[t * rows : (t + 1) * rows], 1, 0)
            wgrad = term if wgrad is None else wgrad + term
        qkv_grads.append(wgrad)
        qkv_bias_grads.append(jnp.sum(grad_t.astype(F32), axis=(0, 2)))
        out_grads.append(dg(attended[h], grad_attn, 1, 0).reshape(n, HD, width))
    first_normed, first_pull = jax.vjp(layer_norm, inputs_f, first_gain, first_shift)
    grad_input_ln, first_gain_grad, first_shift_grad = first_pull(grad_normed)
    grad_input = grad_middle + grad_input_ln

    out_grad = jnp.stack(out_grads, axis=1).reshape(n, local, width).astype(BF)
    partial = jnp.concatenate([out_grad, up_grad, down_grad_t], axis=1)
    total_rows = partial.shape[1]
    part = total_rows // m
    partial = partial.reshape(n, m, part, width).transpose(1, 0, 2, 3)
    partial = lax.psum_scatter(partial, "dp", scatter_dimension=0, tiled=False)
    partial = lax.psum_scatter(partial, "tensor", scatter_dimension=0, tiled=False)
    summed = lax.all_gather(partial.astype(F32), "dp", axis=0, tiled=True)
    out_grad = summed[:local]
    up_grad = summed[local : local + width]
    down_grad = summed[local + width :].T

    qkv_grad = lax.psum(jnp.stack(qkv_grads), "dp")
    qkv_grad = qkv_grad.reshape(heads, 3, HD, width).transpose(3, 1, 0, 2).reshape(width, 3, local)
    qkv_bias_grad = lax.psum(jnp.stack(qkv_bias_grads), "dp")
    qkv_bias_grad = qkv_bias_grad.reshape(heads, 3, HD).transpose(1, 0, 2).reshape(3, local)

    out_bias_grad, second_gain_grad, second_shift_grad, down_bias_grad, grad_depth, up_bias_grad = total_small(
        [out_bias_grad, second_gain_grad, second_shift_grad, down_bias_grad, grad_depth, up_bias_grad[0]]
    )
    up_bias_grad = lax.dynamic_slice_in_dim(up_bias_grad, z * hidden, hidden, 0)
    first_gain_grad, first_shift_grad = total_small([first_gain_grad, first_shift_grad])
    return (
        dwa_output,
        grad_input,
        first_gain_grad,
        first_shift_grad,
        qkv_grad,
        qkv_bias_grad,
        out_grad,
        out_bias_grad,
        second_gain_grad,
        second_shift_grad,
        up_grad,
        up_bias_grad,
        down_grad,
        down_bias_grad,
        grad_depth,
    )


def solution(mesh):
    both = ("dp", "tensor")
    return jax.shard_map(
        shards,
        mesh=mesh,
        in_specs=(
            P(both, None),
            P(both, None),
            P(None, both, None),
            P(both, None),
            P(),
            P(),
            P(None, None, "tensor"),
            P(None, "tensor"),
            P("tensor", None),
            P(),
            P(),
            P(),
            P(None, "tensor"),
            P("tensor"),
            P("tensor", None),
            P(),
            P(),
            P("dp"),
            P(),
        ),
        out_specs=(
            P(both, None),
            P(both, None),
            P(),
            P(),
            P(None, None, "tensor"),
            P(None, "tensor"),
            P("tensor", None),
            P(),
            P(),
            P(),
            P(None, "tensor"),
            P("tensor"),
            P("tensor", None),
            P(),
            P(),
        ),
        check_vma=False,
    )
```

```python
import functools

import jax
import jax.numpy as jnp
from jax import lax
from jax.experimental import pallas as pl
from jax.experimental.pallas import tpu as pltpu
from jax.sharding import PartitionSpec as P

HD = 64
NEG = -1e30
LOG2E = 1.4426950408889634
F32 = jnp.float32
BF = jnp.bfloat16


def dg(a, b, ca, cb):
    return lax.dot_general(a, b, (((ca,), (cb,)), ((), ())), preferred_element_type=F32)


def split_query(q):
    scaled = q.astype(F32) * (LOG2E * HD**-0.5)
    high = scaled.astype(BF)
    low = (scaled - high.astype(F32)).astype(BF)
    return jnp.concatenate([high, low], axis=0)


def visible(key_start, query_start, keys, queries, prefix):
    key_pos = key_start + lax.broadcasted_iota(jnp.int32, (keys, queries), 0)
    query_pos = query_start + lax.broadcasted_iota(jnp.int32, (1, queries), 1)
    return key_pos <= jnp.maximum(query_pos, prefix - 1)


def remote(src, dst, send, recv, peer):
    return pltpu.make_async_remote_copy(
        src_ref=src,
        dst_ref=dst,
        send_sem=send,
        recv_sem=recv,
        device_id=peer,
        device_id_type=pl.DeviceIdType.MESH,
    )


def greet(axis_counts):
    barrier = pltpu.get_barrier_semaphore()
    total = 0
    for axis, count in axis_counts:
        me = lax.axis_index(axis)
        for k in range(1, count):
            pl.semaphore_signal(
                barrier, inc=1, device_id={axis: lax.rem(me + k, count)}, device_id_type=pl.DeviceIdType.MESH
            )
        total += count - 1
    pl.semaphore_wait(barrier, total)


def fwd_kernel(
    n, heads, rows, bk, sub,
    pref_ref, send_ref, qkv_ref, att_ref, of_ref, lse_ref,
    k2_ref, v2_ref, m_ref, acc_ref, ob_ref, own_sem, s_sem, r_sem, os_sem, or_sem, oo_sem,
):
    z = lax.axis_index("tensor")
    length = n * rows
    per = rows // bk
    prefix_blocks = length // 2 // bk
    greet([("tensor", n)])

    def qkv_copy(h, k):
        d = lax.rem(z + k, n)
        return remote(send_ref.at[d, h], qkv_ref.at[h, z], s_sem.at[h, k - 1], r_sem.at[h, k - 1], {"tensor": d})

    def own_copy(h):
        return pltpu.make_async_copy(send_ref.at[z, h], qkv_ref.at[h, z], own_sem.at[h])

    for h in range(heads):
        own_copy(h).start()
        for k in range(1, n):
            qkv_copy(h, k).start()
    prefix = pref_ref[0]

    def att_remote(h, i):
        return remote(ob_ref.at[h, i], att_ref.at[h, z], os_sem.at[h, i], or_sem.at[h, z], {"tensor": i})

    def att_own(h, i):
        return pltpu.make_async_copy(ob_ref.at[h, i], att_ref.at[h, i], oo_sem.at[h])

    def head(h, carry):
        own_copy(h).wait()
        for k in range(1, n):
            qkv_copy(h, k).wait_recv()
        for c in range(n * per):
            t, o = c // per, (c % per) * bk
            kt = qkv_ref[h, t, 1, :, o : o + bk].astype(F32).T.astype(BF)
            k2_ref[c * bk : (c + 1) * bk, :] = jnp.concatenate([kt, kt], axis=1)
            v2_ref[c, 0:HD, :] = qkv_ref[h, t, 2, :, o : o + bk]
            first = lax.broadcasted_iota(jnp.int32, (16, bk), 0) == 0
            v2_ref[c, HD : HD + 16, :] = jnp.where(first, 1.0, 0.0).astype(BF)
        for i in range(n):
            q2 = split_query(qkv_ref[h, i, 0])
            m_ref[...] = jnp.full(m_ref.shape, NEG, F32)
            acc_ref[...] = jnp.zeros(acc_ref.shape, F32)

            def block(j, masked, q2=q2, i=i):
                kj = k2_ref[pl.ds(pl.multiple_of(j * bk, bk), bk), :]
                vj = v2_ref[j]
                for s0 in range(0, rows, sub):
                    s = dg(kj, q2[:, s0 : s0 + sub], 1, 0)
                    if masked:
                        s = jnp.where(visible(j * bk, i * rows + s0, bk, sub, prefix), s, NEG)
                    m = m_ref[:, s0 : s0 + sub]
                    mn = jnp.maximum(m, jnp.max(s, axis=0, keepdims=True))
                    p = jnp.exp2(s - mn).astype(BF)
                    scale = jnp.exp2(m - mn)
                    m_ref[:, s0 : s0 + sub] = mn
                    acc_ref[:, s0 : s0 + sub] = acc_ref[:, s0 : s0 + sub] * scale + dg(vj, p, 1, 0)

            def full_block(j, c, block=block):
                block(j, False)
                return c

            def masked_block(j, c, block=block):
                block(j, True)
                return c

            if i > 0:
                lax.fori_loop(0, i * per, full_block, 0)
            lax.fori_loop(i * per, max((i + 1) * per, prefix_blocks), masked_block, 0)
            total = acc_ref[HD : HD + 1, :]
            out = acc_ref[0:HD, :] / total
            of_ref[h, :, i * rows : (i + 1) * rows] = out
            lse_ref[h, :, i * rows : (i + 1) * rows] = m_ref[...] + jnp.log2(total)
            ob_ref[h, i] = out.astype(BF)

            @pl.when(z != i)
            def _():
                att_remote(h, i).start()

            @pl.when(z == i)
            def _():
                att_own(h, i).start()

        return carry

    lax.fori_loop(0, heads, head, 0)
    for h in range(heads):
        att_own(h, z).wait()
        for k in range(1, n):
            qkv_copy(h, k).wait_send()
            d = lax.rem(z + k, n)
            att_remote(h, d).wait_send()
            remote(ob_ref.at[h, d], att_ref.at[h, d], os_sem.at[h, d], or_sem.at[h, d], {"tensor": d}).wait_recv()


def attend(prefix, send, bk=512, sub=512):
    n, heads, _, _, rows = send.shape
    length = n * rows
    vmem = pl.BlockSpec(memory_space=pltpu.VMEM)
    dma = pltpu.SemaphoreType.DMA
    return pl.pallas_call(
        functools.partial(fwd_kernel, n, heads, rows, bk, sub),
        in_specs=[pl.BlockSpec(memory_space=pltpu.SMEM), vmem],
        out_specs=[vmem] * 4,
        out_shape=[
            jax.ShapeDtypeStruct((heads, n, 3, HD, rows), BF),
            jax.ShapeDtypeStruct((heads, n, HD, rows), BF),
            jax.ShapeDtypeStruct((heads, HD, length), F32),
            jax.ShapeDtypeStruct((heads, 1, length), F32),
        ],
        scratch_shapes=[
            pltpu.VMEM((length, 2 * HD), BF),
            pltpu.VMEM((length // bk, HD + 16, bk), BF),
            pltpu.VMEM((1, rows), F32),
            pltpu.VMEM((HD + 16, rows), F32),
            pltpu.VMEM((heads, n, HD, rows), BF),
            dma((heads,)),
            dma((heads, n - 1)),
            dma((heads, n - 1)),
            dma((heads, n)),
            dma((heads, n)),
            dma((heads,)),
        ],
        compiler_params=pltpu.CompilerParams(
            collective_id=0, has_side_effects=True, vmem_limit_bytes=60 * 2**20
        ),
        cost_estimate=pl.CostEstimate(
            flops=int(heads * 4 * 256 * length * length * 0.7),
            bytes_accessed=heads * length * HD * 20,
            transcendentals=int(heads * length * length * 0.7),
        ),
        name="attend_forward",
    )(prefix, send)


def small_kernel(n, m, x_ref, o_ref, zbuf, mid, pbuf, zs, zr, ps, pr):
    z = lax.axis_index("tensor")
    d = lax.axis_index("dp")
    greet([("tensor", n), ("dp", m)])

    def stage(axis, me, count, src, buf, send, recv):
        buf[me] = src[...]
        for k in range(1, count):
            peer = lax.rem(me + k, count)
            remote(src, buf.at[me], send.at[k - 1], recv.at[me], {axis: peer}).start()
        for k in range(1, count):
            peer = lax.rem(me + k, count)
            copy = remote(src, buf.at[peer], send.at[k - 1], recv.at[peer], {axis: peer})
            copy.wait_send()
            copy.wait_recv()
        total = buf[0]
        for k in range(1, count):
            total = total + buf[k]
        return total

    mid[...] = stage("tensor", z, n, x_ref, zbuf, zs, zr)
    o_ref[...] = stage("dp", d, m, mid, pbuf, ps, pr)


def total_small(vectors, n, m):
    sizes = [v.size for v in vectors]
    flat = jnp.concatenate([v.reshape(-1) for v in vectors])
    flat = jnp.pad(flat, (0, -flat.size % 1024)).reshape(-1, 128)
    vmem = pl.BlockSpec(memory_space=pltpu.VMEM)
    dma = pltpu.SemaphoreType.DMA
    summed = pl.pallas_call(
        functools.partial(small_kernel, n, m),
        in_specs=[vmem],
        out_specs=vmem,
        out_shape=jax.ShapeDtypeStruct(flat.shape, F32),
        scratch_shapes=[
            pltpu.VMEM((n,) + flat.shape, F32),
            pltpu.VMEM(flat.shape, F32),
            pltpu.VMEM((m,) + flat.shape, F32),
            dma((n - 1,)),
            dma((n,)),
            dma((m - 1,)),
            dma((m,)),
        ],
        compiler_params=pltpu.CompilerParams(collective_id=1, has_side_effects=True),
        name="total_small",
    )(flat).reshape(-1)
    out, at = [], 0
    for v, size in zip(vectors, sizes):
        out.append(summed[at : at + size].reshape(v.shape))
        at += size
    return out


def unrotate(front, back, c, s):
    return front * c + back * s, back * c - front * s


def bwd_kernel(
    n, heads, rows, bk, sub,
    pref_ref, send_ref, qkv_ref, of_ref, lse_ref, cos_ref, sin_ref, g_ref, back_ref,
    do_ref, q2_ref, qn_ref, don_ref, dd_ref, dq_ref, dk_ref, dv_ref, own_sem, s_sem, r_sem, kvs, kvr, qs, qr, kvo, qo,
):
    z = lax.axis_index("tensor")
    length = n * rows
    per = rows // bk
    prefix_chunks = -(-(length // 2) // rows)
    greet([("tensor", n)])

    def do_copy(h, k):
        d = lax.rem(z + k, n)
        return remote(send_ref.at[d, h], do_ref.at[h, z], s_sem.at[h, k - 1], r_sem.at[h, k - 1], {"tensor": d})

    def own_copy(h):
        return pltpu.make_async_copy(send_ref.at[z, h], do_ref.at[h, z], own_sem.at[h])

    for h in range(heads):
        own_copy(h).start()
        for k in range(1, n):
            do_copy(h, k).start()
    prefix = pref_ref[0]
    kv_rows, q_rows = pl.ds(HD, 2 * HD), pl.ds(0, HD)

    def piece(h, t, part, source, send, recv):
        return remote(
            g_ref.at[h, t, part], back_ref.at[h, source, part], send.at[h, t], recv.at[h, source], {"tensor": t}
        )

    def own_piece(h, part, sem):
        return pltpu.make_async_copy(g_ref.at[h, z, part], back_ref.at[h, z, part], sem.at[h])

    def hand_out(h, t, part, send, recv, own):
        @pl.when(z != t)
        def _():
            piece(h, t, part, z, send, recv).start()

        @pl.when(z == t)
        def _():
            own_piece(h, part, own).start()

    def head(h, carry):
        own_copy(h).wait()
        for k in range(1, n):
            do_copy(h, k).wait_recv()
        for c in range(n):
            q = qkv_ref[h, c, 0]
            q2_ref[c] = split_query(q)
            qn_ref[c] = q.astype(F32).T.astype(BF)
            dof = do_ref[h, c].astype(F32)
            don_ref[c] = dof.T.astype(BF)
            inner = jnp.sum(dof * of_ref[h, :, c * rows : (c + 1) * rows], axis=0, keepdims=True)
            dd_ref[c] = jnp.concatenate([inner, lse_ref[h, :, c * rows : (c + 1) * rows]], axis=0)
            dq_ref[c] = jnp.zeros((HD, rows), F32)

        def keys(t, c1):
            for o in range(0, rows, bk):
                kt = qkv_ref[h, t, 1, :, o : o + bk]
                kn = kt.astype(F32).T.astype(BF)
                k2 = jnp.concatenate([kn, kn], axis=1)
                vn = qkv_ref[h, t, 2, :, o : o + bk].astype(F32).T.astype(BF)
                dk_ref[...] = jnp.zeros(dk_ref.shape, F32)
                dv_ref[...] = jnp.zeros(dv_ref.shape, F32)

                def block(i, masked, o=o, kt=kt, k2=k2, vn=vn):
                    for s0 in range(0, rows, sub):
                        sl = slice(s0, s0 + sub)
                        p = jnp.exp2(dg(k2, q2_ref[i, :, sl], 1, 0) - dd_ref[i, 1:2, sl])
                        if masked:
                            p = jnp.where(visible(t * rows + o, i * rows + s0, bk, sub, prefix), p, 0.0)
                        dp = dg(vn, do_ref[h, i, :, sl], 1, 0)
                        dv_ref[...] += dg(p.astype(BF), don_ref[i, sl, :], 1, 0)
                        ds = (p * (dp - dd_ref[i, 0:1, sl])).astype(BF)
                        dk_ref[...] += dg(ds, qn_ref[i, sl, :], 1, 0)
                        dq_ref[i, :, sl] += dg(kt, ds, 1, 0)

                def masked_block(i, c2, block=block):
                    block(i, True)
                    return c2

                def full_block(i, c2, block=block):
                    block(i, False)
                    return c2

                lax.fori_loop(jnp.where(t < prefix_chunks, 0, t), t + 1, masked_block, 0)
                lax.fori_loop(t + 1, n, full_block, 0)
                dk = dk_ref[...].T * HD**-0.5
                at = pl.ds(pl.multiple_of(t * rows + o, bk), bk)
                a, b = unrotate(dk[: HD // 2], dk[HD // 2 :], cos_ref[:, at], sin_ref[:, at])
                g_ref[h, t, HD : HD + HD // 2, o : o + bk] = a.astype(BF)
                g_ref[h, t, HD + HD // 2 : 2 * HD, o : o + bk] = b.astype(BF)
                g_ref[h, t, 2 * HD : 3 * HD, o : o + bk] = dv_ref[...].T.astype(BF)
            hand_out(h, t, kv_rows, kvs, kvr, kvo)
            return c1

        lax.fori_loop(0, n, keys, 0)
        for c in range(n):
            x = dq_ref[c] * HD**-0.5
            at = slice(c * rows, (c + 1) * rows)
            a, b = unrotate(x[: HD // 2], x[HD // 2 :], cos_ref[:, at], sin_ref[:, at])
            g_ref[h, c, : HD // 2, :] = a.astype(BF)
            g_ref[h, c, HD // 2 : HD, :] = b.astype(BF)
            hand_out(h, c, q_rows, qs, qr, qo)
        return carry

    lax.fori_loop(0, heads, head, 0)
    for h in range(heads):
        own_piece(h, kv_rows, kvo).wait()
        own_piece(h, q_rows, qo).wait()
        for k in range(1, n):
            do_copy(h, k).wait_send()
            d = lax.rem(z + k, n)
            for part, send, recv in ((kv_rows, kvs, kvr), (q_rows, qs, qr)):
                copy = piece(h, d, part, d, send, recv)
                copy.wait_send()
                copy.wait_recv()


def attend_back(prefix, send, qkv, of, lse, cos_t, sin_t, bk=512, sub=256):
    n, heads, _, rows = send.shape
    length = n * rows
    vmem = pl.BlockSpec(memory_space=pltpu.VMEM)
    dma = pltpu.SemaphoreType.DMA
    return pl.pallas_call(
        functools.partial(bwd_kernel, n, heads, rows, bk, sub),
        in_specs=[pl.BlockSpec(memory_space=pltpu.SMEM)] + [vmem] * 6,
        out_specs=[vmem] * 2,
        out_shape=[jax.ShapeDtypeStruct((heads, n, 3 * HD, rows), BF)] * 2,
        scratch_shapes=[
            pltpu.VMEM((heads, n, HD, rows), BF),
            pltpu.VMEM((n, 2 * HD, rows), BF),
            pltpu.VMEM((n, rows, HD), BF),
            pltpu.VMEM((n, rows, HD), BF),
            pltpu.VMEM((n, 2, rows), F32),
            pltpu.VMEM((n, HD, rows), F32),
            pltpu.VMEM((bk, HD), F32),
            pltpu.VMEM((bk, HD), F32),
            dma((heads,)),
            dma((heads, n - 1)),
            dma((heads, n - 1)),
            dma((heads, n)),
            dma((heads, n)),
            dma((heads, n)),
            dma((heads, n)),
            dma((heads,)),
            dma((heads,)),
        ],
        compiler_params=pltpu.CompilerParams(
            collective_id=2, has_side_effects=True, vmem_limit_bytes=60 * 2**20
        ),
        cost_estimate=pl.CostEstimate(
            flops=int(heads * 10 * 256 * length * length * 0.7),
            bytes_accessed=heads * length * HD * 20,
            transcendentals=int(heads * length * length * 0.7),
        ),
        name="attend_backward",
    )(prefix, send, qkv, of, lse, cos_t, sin_t)


EPS = 1e-05
ROPE_BASE = 10000.0
GELU_C = 0.7978845608028654


def layer_norm(values, norm_gain, norm_shift):
    center = values - jnp.mean(values, axis=-1, keepdims=True)
    spread = jnp.mean(center * center, axis=-1, keepdims=True)
    return center * lax.rsqrt(spread + EPS) * norm_gain + norm_shift


def rotary_tables(length):
    half_dim = HD // 2
    frequency = ROPE_BASE ** (-jnp.arange(half_dim, dtype=jnp.float32) / half_dim)
    angles = frequency[:, None] * jnp.arange(length, dtype=jnp.float32)[None, :]
    return (jnp.cos(angles), jnp.sin(angles))


def project_kernel(n, heads, x_ref, gain_ref, shift_ref, w_ref, b_ref, cos_ref, sin_ref, send_ref, normed_ref):
    normed = layer_norm(x_ref[...].astype(F32), gain_ref[...], shift_ref[...]).astype(BF)
    normed_ref[...] = normed
    c, s = cos_ref[...], sin_ref[...]
    for d in range(n):
        proj = dg(w_ref[d], normed, 1, 1) + b_ref[d]
        for h in range(heads):
            for part in range(3):
                r0 = (h * 3 + part) * HD
                u = proj[r0 : r0 + HD]
                if part < 2:
                    f, b = u[: HD // 2], u[HD // 2 :]
                    send_ref[d, h, part, : HD // 2] = (f * c - b * s).astype(BF)
                    send_ref[d, h, part, HD // 2 :] = (b * c + f * s).astype(BF)
                else:
                    send_ref[d, h, part] = u.astype(BF)


def project(x, gain, shift, w_all, bias, cos_t, sin_t, cols, block=512):
    rows, width = x.shape
    n = w_all.shape[0]
    heads = cols // (3 * HD)
    const = lambda shape: pl.BlockSpec(shape, lambda i: (0,) * len(shape))
    return pl.pallas_call(
        functools.partial(project_kernel, n, heads),
        grid=(rows // block,),
        in_specs=[
            pl.BlockSpec((block, width), lambda i: (i, 0)),
            const((1, width)),
            const((1, width)),
            const((n, cols, width)),
            const((n, cols, 1)),
            pl.BlockSpec((HD // 2, block), lambda i: (0, i)),
            pl.BlockSpec((HD // 2, block), lambda i: (0, i)),
        ],
        out_specs=[
            pl.BlockSpec((n, heads, 3, HD, block), lambda i: (0, 0, 0, 0, i)),
            pl.BlockSpec((block, width), lambda i: (i, 0)),
        ],
        out_shape=[
            jax.ShapeDtypeStruct((n, heads, 3, HD, rows), BF),
            jax.ShapeDtypeStruct((rows, width), BF),
        ],
        compiler_params=pltpu.CompilerParams(vmem_limit_bytes=48 * 2**20),
        cost_estimate=pl.CostEstimate(
            flops=2 * rows * width * cols * n, bytes_accessed=rows * width * 4 + n * cols * (rows + width) * 2, transcendentals=rows
        ),
        name="project_qkv",
    )(x, gain[None], shift[None], w_all, bias, cos_t, sin_t)


def mlp_kernel(nm_ref, gm_ref, up_ref, upb_ref, down_ref, out_ref, dnm_ref, dup_ref, ddown_ref, dupb_ref, nmt_ref, gmt_ref):
    step = pl.program_id(0)

    @pl.when(step == 0)
    def _():
        nmt_ref[...] = nm_ref[...].T
        gmt_ref[...] = gm_ref[...].T
        out_ref[...] = jnp.zeros(out_ref.shape, F32)
        dnm_ref[...] = jnp.zeros(dnm_ref.shape, F32)

    up, down = up_ref[...], down_ref[...]
    pre = dg(nm_ref[...], up, 1, 0) + upb_ref[...]
    sq = pre * pre
    th = jnp.tanh(GELU_C * (pre + 0.044715 * sq * pre))
    half = 0.5 * (1.0 + th)
    act = (pre * half).astype(BF)
    slope = half + 0.5 * pre * (1.0 - th * th) * (GELU_C + (3.0 * 0.044715 * GELU_C) * sq)
    gp = dg(gm_ref[...], down, 1, 1) * slope
    gpb = gp.astype(BF)
    out_ref[...] += dg(act, down, 1, 0)
    dnm_ref[...] += dg(gpb, up, 1, 1)
    dup_ref[...] = dg(nmt_ref[...], gpb, 1, 0).astype(BF)
    ddown_ref[...] = dg(gmt_ref[...], act, 1, 0).astype(BF)
    dupb_ref[...] = jnp.sum(gpb.astype(F32), axis=0, keepdims=True)


def mlp(nm, gm, up, up_bias, down, chunk=256):
    rows, width = nm.shape
    n, _, f = up.shape
    per = f // chunk
    squeezed = pl.Squeezed()
    const = pl.BlockSpec((rows, width), lambda i: (0, 0))
    hidden = n * f
    return pl.pallas_call(
        mlp_kernel,
        grid=(n * per,),
        in_specs=[
            const,
            const,
            pl.BlockSpec((squeezed, width, chunk), lambda i: (i // per, 0, i % per)),
            pl.BlockSpec((1, chunk), lambda i: (0, i)),
            pl.BlockSpec((squeezed, chunk, width), lambda i: (i // per, i % per, 0)),
        ],
        out_specs=[
            const,
            const,
            pl.BlockSpec((squeezed, width, chunk), lambda i: (i // per, 0, i % per)),
            pl.BlockSpec((squeezed, width, chunk), lambda i: (i // per, 0, i % per)),
            pl.BlockSpec((1, chunk), lambda i: (0, i)),
        ],
        out_shape=[
            jax.ShapeDtypeStruct((rows, width), F32),
            jax.ShapeDtypeStruct((rows, width), F32),
            jax.ShapeDtypeStruct((n, width, f), BF),
            jax.ShapeDtypeStruct((n, width, f), BF),
            jax.ShapeDtypeStruct((1, hidden), F32),
        ],
        scratch_shapes=[pltpu.VMEM((width, rows), BF), pltpu.VMEM((width, rows), BF)],
        compiler_params=pltpu.CompilerParams(vmem_limit_bytes=56 * 2**20),
        cost_estimate=pl.CostEstimate(
            flops=12 * rows * width * hidden, bytes_accessed=8 * width * hidden + 12 * rows * width, transcendentals=rows * hidden
        ),
        name="mlp",
    )(nm, gm, up, up_bias, down)


def gather_weight(shard, dp_index, dp_size, n):
    rows, cols = shard.shape
    part = rows // dp_size
    mine = lax.dynamic_slice_in_dim(shard, dp_index * part, part, 0)
    every = lax.all_gather(mine, ("dp", "tensor"), axis=0, tiled=False)
    return every.reshape(dp_size, n, part, cols).transpose(1, 0, 2, 3).reshape(n, rows, cols)


def shards(
    block_input,
    embedding,
    history,
    cotangent,
    first_gain,
    first_shift,
    qkv_weight,
    qkv_bias,
    out_weight,
    out_bias,
    second_gain,
    second_shift,
    up_weight,
    up_bias,
    down_weight,
    down_bias,
    depth_weights,
    prefix_length,
    history_index,
):
    rows, width = block_input.shape
    local = qkv_weight.shape[2]
    heads = local // HD
    n = lax.axis_size("tensor")
    m = lax.axis_size("dp")
    z = lax.axis_index("tensor")
    dp = lax.axis_index("dp")
    length = rows * n
    hidden = up_weight.shape[1]
    cos_t, sin_t = rotary_tables(length)

    w_t = qkv_weight.reshape(width, 3, heads, HD).transpose(2, 1, 3, 0).reshape(3 * local, width)
    b_t = qkv_bias.reshape(3, heads, HD).transpose(1, 0, 2).reshape(1, 3 * local)
    b_t = jnp.pad(b_t, ((0, 0), (0, width - 3 * local)))
    fill = jnp.zeros((-(3 * local) % 64 + 62, width), BF)
    first = jnp.concatenate([w_t, up_bias[None], b_t, fill], axis=0)
    first_all = gather_weight(first, dp, m, n)
    up_bias_all = first_all[:, 3 * local, :hidden].astype(F32).reshape(1, n * hidden)
    b_all = first_all[:, 3 * local + 1, : 3 * local].astype(F32)[:, :, None]
    row_at = lambda table: lax.dynamic_slice_in_dim(table, z * rows, rows, 1)
    send, normed_own = project(
        block_input, first_gain, first_shift, first_all, b_all, row_at(cos_t), row_at(sin_t), 3 * local
    )
    w_all = first_all[:, : 3 * local].reshape(n, heads, 3 * HD, width)

    early = jnp.concatenate([out_weight, up_weight, down_weight], axis=0)
    early, _ = lax.optimization_barrier((early, first_all))
    early_all = gather_weight(early, dp, m, n)
    out_all = early_all[:, :local].reshape(n, heads, HD, width)
    up_all = early_all[:, local : local + width]
    down_all = early_all[:, local + width :]

    inputs_f = block_input.astype(F32)
    qkv_t, attended, of, lse = attend(prefix_length, send)
    attn = None
    for h in range(heads):
        piece = dg(attended[h].reshape(n * HD, rows), out_all[:, h].reshape(n * HD, width), 0, 0)
        attn = piece if attn is None else attn + piece

    normed_own, _ = lax.optimization_barrier((normed_own, early_all))
    normed = lax.all_gather(normed_own, "tensor", axis=0, tiled=True)
    middle = inputs_f + (attn + out_bias.astype(F32))
    normed_mid_f, second_pull = jax.vjp(layer_norm, middle, second_gain, second_shift)
    grad_top = cotangent.astype(F32)
    grad_block = depth_weights[4] * grad_top
    grad_branch = grad_block.astype(BF)
    mlp_out, grad_normed_mid, up_grad, down_grad_t, up_bias_grad = mlp(
        normed_mid_f.astype(BF), grad_branch, up_all, up_bias_all, down_all
    )
    block_out = middle + (mlp_out + down_bias.astype(F32))
    slot_ids = jnp.arange(3, dtype=jnp.int32)
    pick = (history_index[:, None] == slot_ids[None, :]).astype(F32)
    slot_coef = jnp.sum(depth_weights[1:4, None] * pick, axis=0)
    embed_f = embedding.astype(F32)
    mixed = depth_weights[0] * embed_f + depth_weights[4] * block_out
    for slot_id in range(3):
        mixed = mixed + slot_coef[slot_id] * history[slot_id].astype(F32)
    dwa_output = mixed.astype(BF)
    slot_sums = jnp.stack([jnp.sum(grad_top * history[slot_id].astype(F32)) for slot_id in range(3)])
    grad_depth = jnp.concatenate(
        [
            jnp.sum(grad_top * embed_f)[None],
            jnp.sum(pick * slot_sums[None, :], axis=1),
            jnp.sum(grad_top * block_out)[None],
        ]
    )
    down_bias_grad = jnp.sum(grad_branch.astype(F32), axis=0)

    grad_middle_ln, second_gain_grad, second_shift_grad = second_pull(grad_normed_mid)
    grad_middle = grad_block + grad_middle_ln
    grad_attn = grad_middle.astype(BF)
    out_bias_grad = jnp.sum(grad_attn.astype(F32), axis=0)

    grad_send = jnp.stack(
        [dg(out_all[:, h].reshape(n * HD, width), grad_attn, 1, 1).astype(BF).reshape(n, HD, rows) for h in range(heads)],
        axis=1,
    )
    normed, grad_send = lax.optimization_barrier((normed, grad_send))
    grad_own, back = attend_back(prefix_length, grad_send, qkv_t, of, lse, cos_t, sin_t)
    grad_normed = None
    qkv_grads, qkv_bias_grads, out_grads = [], [], []
    for h in range(heads):
        piece = dg(back[h].reshape(n * 3 * HD, rows), w_all[:, h].reshape(n * 3 * HD, width), 0, 0)
        grad_normed = piece if grad_normed is None else grad_normed + piece
        wgrad = None
        for t in range(n):
            term = dg(grad_own[h, t], normed[t * rows : (t + 1) * rows], 1, 0)
            wgrad = term if wgrad is None else wgrad + term
        qkv_grads.append(wgrad)
        qkv_bias_grads.append(jnp.sum(grad_own[h].astype(F32), axis=(0, 2)))
        out_grads.append(dg(attended[h].reshape(n * HD, rows), grad_attn, 1, 0).reshape(n, HD, width))
    first_normed, first_pull = jax.vjp(layer_norm, inputs_f, first_gain, first_shift)
    grad_input_ln, first_gain_grad, first_shift_grad = first_pull(grad_normed)
    grad_input = grad_middle + grad_input_ln

    out_grad = jnp.stack(out_grads, axis=1).reshape(n, local, width).astype(BF)
    partial = jnp.concatenate([out_grad, up_grad, down_grad_t], axis=1)
    total_rows = partial.shape[1]
    part = total_rows // m
    partial = partial.reshape(n, m, part, width).transpose(1, 0, 2, 3)
    partial = lax.psum_scatter(partial, "dp", scatter_dimension=0, tiled=False)
    partial, _ = lax.optimization_barrier((partial, back))
    partial = lax.psum_scatter(partial, "tensor", scatter_dimension=0, tiled=False)
    summed = lax.all_gather(partial, "dp", axis=0, tiled=True).astype(F32)
    out_grad = summed[:local]
    up_grad = summed[local : local + width]
    down_grad = summed[local + width :].T

    qkv_grad = lax.psum(jnp.stack(qkv_grads), "dp")
    qkv_grad = qkv_grad.reshape(heads, 3, HD, width).transpose(3, 1, 0, 2).reshape(width, 3, local)
    spread = jnp.zeros((n, 3 * local), F32)
    spread = lax.dynamic_update_slice_in_dim(spread, jnp.concatenate(qkv_bias_grads)[None], z, 0)
    (
        out_bias_grad,
        second_gain_grad,
        second_shift_grad,
        down_bias_grad,
        grad_depth,
        up_bias_grad,
        qkv_bias_grad,
        first_gain_grad,
        first_shift_grad,
    ) = total_small(
        [
            out_bias_grad,
            second_gain_grad,
            second_shift_grad,
            down_bias_grad,
            grad_depth,
            up_bias_grad[0],
            spread,
            first_gain_grad,
            first_shift_grad,
        ],
        n,
        m,
    )
    up_bias_grad = lax.dynamic_slice_in_dim(up_bias_grad, z * hidden, hidden, 0)
    qkv_bias_grad = lax.dynamic_index_in_dim(qkv_bias_grad, z, 0, keepdims=False)
    qkv_bias_grad = qkv_bias_grad.reshape(heads, 3, HD).transpose(1, 0, 2).reshape(3, local)
    return (
        dwa_output,
        grad_input,
        first_gain_grad,
        first_shift_grad,
        qkv_grad,
        qkv_bias_grad,
        out_grad,
        out_bias_grad,
        second_gain_grad,
        second_shift_grad,
        up_grad,
        up_bias_grad,
        down_grad,
        down_bias_grad,
        grad_depth,
    )


def solution(mesh):
    both = ("dp", "tensor")
    return jax.shard_map(
        shards,
        mesh=mesh,
        in_specs=(
            P(both, None),
            P(both, None),
            P(None, both, None),
            P(both, None),
            P(),
            P(),
            P(None, None, "tensor"),
            P(None, "tensor"),
            P("tensor", None),
            P(),
            P(),
            P(),
            P(None, "tensor"),
            P("tensor"),
            P("tensor", None),
            P(),
            P(),
            P("dp"),
            P(),
        ),
        out_specs=(
            P(both, None),
            P(both, None),
            P(),
            P(),
            P(None, None, "tensor"),
            P(None, "tensor"),
            P("tensor", None),
            P(),
            P(),
            P(),
            P(None, "tensor"),
            P("tensor"),
            P("tensor", None),
            P(),
            P(),
        ),
        check_vma=False,
    )
```

```python
import functools

import jax
import jax.numpy as jnp
from jax import lax
from jax.experimental import pallas as pl
from jax.experimental.pallas import tpu as pltpu
from jax.sharding import PartitionSpec as P

HD = 64
NEG = -1e30
LOG2E = 1.4426950408889634
F32 = jnp.float32
BF = jnp.bfloat16


def dg(a, b, ca, cb):
    return lax.dot_general(a, b, (((ca,), (cb,)), ((), ())), preferred_element_type=F32)


def split_query(q):
    scaled = q.astype(F32) * (LOG2E * HD**-0.5)
    high = scaled.astype(BF)
    low = (scaled - high.astype(F32)).astype(BF)
    return jnp.concatenate([high, low], axis=0)


def visible(key_start, query_start, keys, queries, prefix):
    key_pos = key_start + lax.broadcasted_iota(jnp.int32, (keys, queries), 0)
    query_pos = query_start + lax.broadcasted_iota(jnp.int32, (1, queries), 1)
    return key_pos <= jnp.maximum(query_pos, prefix - 1)


def remote(src, dst, send, recv, peer):
    return pltpu.make_async_remote_copy(
        src_ref=src,
        dst_ref=dst,
        send_sem=send,
        recv_sem=recv,
        device_id=peer,
        device_id_type=pl.DeviceIdType.MESH,
    )


def greet(axis_counts):
    barrier = pltpu.get_barrier_semaphore()
    total = 0
    for axis, count in axis_counts:
        me = lax.axis_index(axis)
        for k in range(1, count):
            pl.semaphore_signal(
                barrier, inc=1, device_id={axis: lax.rem(me + k, count)}, device_id_type=pl.DeviceIdType.MESH
            )
        total += count - 1
    pl.semaphore_wait(barrier, total)


def fwd_kernel(
    n, heads, rows, bk, sub,
    pref_ref, x_ref, gain_ref, shift_ref, w_ref, b_ref, cos_ref, sin_ref,
    normed_ref, qkv_ref, att_ref, of_ref, lse_ref,
    q2_ref, k2_ref, v2_ref, m_ref, acc_ref, ob_ref, rs, rr, ls, lr, os_sem, or_sem, oo_sem,
):
    z = lax.axis_index("tensor")
    per = rows // bk
    prefix_chunks = -(-(n * rows // 2) // rows)
    greet([("tensor", n)])
    prefix = pref_ref[0]

    def to_right(s):
        c = z - (s - 1)
        return remote(normed_ref.at[c], normed_ref.at[c], rs.at[s - 1], rr.at[s - 1], {"tensor": z + 1})

    def to_left(s):
        c = z + (s - 1)
        return remote(normed_ref.at[c], normed_ref.at[c], ls.at[s - 1], lr.at[s - 1], {"tensor": z - 1})

    def from_left(s):
        c = z - s
        return remote(normed_ref.at[c], normed_ref.at[c], rs.at[s - 1], rr.at[s - 1], {"tensor": z - 1})

    def from_right(s):
        c = z + s
        return remote(normed_ref.at[c], normed_ref.at[c], ls.at[s - 1], lr.at[s - 1], {"tensor": z + 1})

    def has_right(s):
        return (z + 1 < n) & (z - (s - 1) >= 0)

    def has_left(s):
        return (z >= 1) & (z + (s - 1) < n)

    for o in range(0, rows, bk):
        x = x_ref[o : o + bk].astype(F32)
        normed_ref[z, o : o + bk] = layer_norm(x, gain_ref[...], shift_ref[...]).astype(BF)

    @pl.when(has_right(1))
    def _():
        to_right(1).start()

    @pl.when(has_left(1))
    def _():
        to_left(1).start()

    m_ref[...] = jnp.full(m_ref.shape, NEG, F32)
    acc_ref[...] = jnp.zeros(acc_ref.shape, F32)
    first = lax.broadcasted_iota(jnp.int32, (16, bk), 0) == 0
    for h in range(heads):
        for c in range(n * per):
            v2_ref[h, c, HD : HD + 16, :] = jnp.where(first, 1.0, 0.0).astype(BF)

    def att_remote(h, i):
        return remote(ob_ref.at[h, i], att_ref.at[h, z], os_sem.at[h, i], or_sem.at[h, z], {"tensor": i})

    def att_own(h):
        return pltpu.make_async_copy(ob_ref.at[h, z], att_ref.at[h, z], oo_sem.at[h])

    def enter(c):
        for o in range(0, rows, bk):
            at = pl.ds(pl.multiple_of(c * rows + o, bk), bk)
            cos, sin = cos_ref[:, at], sin_ref[:, at]
            proj = dg(w_ref[...], normed_ref[c, o : o + bk, :], 1, 1) + b_ref[...]
            for h in range(heads):
                r0 = h * 3 * HD
                parts = []
                for part in range(2):
                    u = proj[r0 + part * HD : r0 + (part + 1) * HD]
                    f, b = u[: HD // 2], u[HD // 2 :]
                    parts.append(jnp.concatenate([f * cos - b * sin, b * cos + f * sin], axis=0))
                q = parts[0].astype(BF)
                v = proj[r0 + 2 * HD : r0 + 3 * HD].astype(BF)
                qkv_ref[h, c, 0, :, o : o + bk] = q
                qkv_ref[h, c, 1, :, o : o + bk] = parts[1].astype(BF)
                qkv_ref[h, c, 2, :, o : o + bk] = v
                q2_ref[h, c, :, o : o + bk] = split_query(q)
                kt = parts[1].T.astype(BF)
                k2_ref[h, c * per + o // bk] = jnp.concatenate([kt, kt], axis=1)
                v2_ref[h, c * per + o // bk, 0:HD, :] = v

    def pair(q, k, masked):
        for h in range(heads):
            for b in range(per):
                kj, vj = k2_ref[h, k * per + b], v2_ref[h, k * per + b]
                for s0 in range(0, rows, sub):
                    sl = slice(s0, s0 + sub)
                    s = dg(kj, q2_ref[h, q, :, sl], 1, 0)
                    if masked:
                        s = jnp.where(visible(k * rows + b * bk, q * rows + s0, bk, sub, prefix), s, NEG)
                    m = m_ref[h, q, :, sl]
                    mn = jnp.maximum(m, jnp.max(s, axis=0, keepdims=True))
                    p = jnp.exp2(s - mn).astype(BF)
                    scale = jnp.exp2(m - mn)
                    m_ref[h, q, :, sl] = mn
                    acc_ref[h, q, :, sl] = acc_ref[h, q, :, sl] * scale + dg(vj, p, 1, 0)

    def finish(q):
        for h in range(heads):
            total = acc_ref[h, q, HD : HD + 1, :]
            out = acc_ref[h, q, 0:HD, :] / total
            of_ref[h, q] = out
            lse_ref[h, q] = m_ref[h, q] + jnp.log2(total)
            ob_ref[h, q] = out.astype(BF)

            @pl.when(z != q)
            def _(h=h):
                att_remote(h, q).start()

            @pl.when(z == q)
            def _(h=h):
                att_own(h).start()

    def event(e, carry):
        s = (e + 1) // 2
        low = e % 2 == 1
        high = (e % 2 == 0) & (e > 0)

        @pl.when(low)
        def _():
            @pl.when(z - s >= 0)
            def _():
                from_left(s).wait_recv()

            @pl.when((s + 1 < n) & has_right(s + 1))
            def _():
                to_right(s + 1).start()

            @pl.when(z + s < n)
            def _():
                from_right(s).wait_recv()

            @pl.when((s + 1 < n) & has_left(s + 1))
            def _():
                to_left(s + 1).start()

        c = jnp.where(low, z - s, z + s)
        bottom = jnp.maximum(z - s, 0)
        start = jnp.where(low, c + 1, jnp.where(high, bottom, c))
        stop = jnp.where(low, jnp.minimum(n, z + s), c)

        @pl.when((c >= 0) & (c < n))
        def _():
            enter(c)
            all_low = low & (c == 0)

            def full_pair(a, t):
                pair(jnp.maximum(a, c), jnp.minimum(a, c), False)

                @pl.when(all_low)
                def _():
                    finish(a)

                return t

            lax.fori_loop(start, stop, full_pair, 0)

            def masked_pair(a, t):
                pair(jnp.minimum(a, c), jnp.maximum(a, c), True)
                return t

            inner = c < prefix_chunks
            lax.fori_loop(
                jnp.where(inner & high, start, c),
                jnp.where(inner & low, jnp.minimum(stop, prefix_chunks), c + 1),
                masked_pair,
                0,
            )
            ready = all_low | ((bottom == 0) & high & (c >= prefix_chunks - 1))
            from_q = jnp.where(c == prefix_chunks - 1, 0, c)

            def finish_one(q, t):
                finish(q)
                return t

            lax.fori_loop(from_q, jnp.where(ready, c + 1, from_q), finish_one, 0)

        return carry

    lax.fori_loop(0, 2 * n - 1, event, 0)
    for s in range(1, n):

        @pl.when(has_right(s))
        def _(s=s):
            to_right(s).wait_send()

        @pl.when(has_left(s))
        def _(s=s):
            to_left(s).wait_send()

    for h in range(heads):
        att_own(h).wait()
        for k in range(1, n):
            d = lax.rem(z + k, n)
            att_remote(h, d).wait_send()
            remote(ob_ref.at[h, d], att_ref.at[h, d], os_sem.at[h, d], or_sem.at[h, d], {"tensor": d}).wait_recv()


def attend(prefix, x, gain, shift, w, bias, cos_t, sin_t, n, bk=512, sub=512):
    rows, width = x.shape
    heads = w.shape[0] // (3 * HD)
    length = n * rows
    vmem = pl.BlockSpec(memory_space=pltpu.VMEM)
    dma = pltpu.SemaphoreType.DMA
    return pl.pallas_call(
        functools.partial(fwd_kernel, n, heads, rows, bk, sub),
        in_specs=[pl.BlockSpec(memory_space=pltpu.SMEM)] + [vmem] * 7,
        out_specs=[vmem] * 5,
        out_shape=[
            jax.ShapeDtypeStruct((n, rows, width), BF),
            jax.ShapeDtypeStruct((heads, n, 3, HD, rows), BF),
            jax.ShapeDtypeStruct((heads, n, HD, rows), BF),
            jax.ShapeDtypeStruct((heads, n, HD, rows), F32),
            jax.ShapeDtypeStruct((heads, n, 1, rows), F32),
        ],
        scratch_shapes=[
            pltpu.VMEM((heads, n, 2 * HD, rows), BF),
            pltpu.VMEM((heads, length // bk, bk, 2 * HD), BF),
            pltpu.VMEM((heads, length // bk, HD + 16, bk), BF),
            pltpu.VMEM((heads, n, 1, rows), F32),
            pltpu.VMEM((heads, n, HD + 16, rows), F32),
            pltpu.VMEM((heads, n, HD, rows), BF),
            dma((n - 1,)),
            dma((n - 1,)),
            dma((n - 1,)),
            dma((n - 1,)),
            dma((heads, n)),
            dma((heads, n)),
            dma((heads,)),
        ],
        compiler_params=pltpu.CompilerParams(
            collective_id=0, has_side_effects=True, vmem_limit_bytes=60 * 2**20
        ),
        cost_estimate=pl.CostEstimate(
            flops=int(heads * 4 * 256 * length * length * 0.7),
            bytes_accessed=heads * length * HD * 20,
            transcendentals=int(heads * length * length * 0.7),
        ),
        name="attend_forward",
    )(prefix, x, gain[None], shift[None], w, bias[:, None], cos_t, sin_t)


def small_kernel(n, m, x_ref, o_ref, zbuf, mid, pbuf, zs, zr, ps, pr):
    z = lax.axis_index("tensor")
    d = lax.axis_index("dp")
    greet([("tensor", n), ("dp", m)])

    def stage(axis, me, count, src, buf, send, recv):
        buf[me] = src[...]
        for k in range(1, count):
            peer = lax.rem(me + k, count)
            remote(src, buf.at[me], send.at[k - 1], recv.at[me], {axis: peer}).start()
        for k in range(1, count):
            peer = lax.rem(me + k, count)
            copy = remote(src, buf.at[peer], send.at[k - 1], recv.at[peer], {axis: peer})
            copy.wait_send()
            copy.wait_recv()
        total = buf[0]
        for k in range(1, count):
            total = total + buf[k]
        return total

    mid[...] = stage("tensor", z, n, x_ref, zbuf, zs, zr)
    o_ref[...] = stage("dp", d, m, mid, pbuf, ps, pr)


def total_small(vectors, n, m):
    sizes = [v.size for v in vectors]
    flat = jnp.concatenate([v.reshape(-1) for v in vectors])
    flat = jnp.pad(flat, (0, -flat.size % 1024)).reshape(-1, 128)
    vmem = pl.BlockSpec(memory_space=pltpu.VMEM)
    dma = pltpu.SemaphoreType.DMA
    summed = pl.pallas_call(
        functools.partial(small_kernel, n, m),
        in_specs=[vmem],
        out_specs=vmem,
        out_shape=jax.ShapeDtypeStruct(flat.shape, F32),
        scratch_shapes=[
            pltpu.VMEM((n,) + flat.shape, F32),
            pltpu.VMEM(flat.shape, F32),
            pltpu.VMEM((m,) + flat.shape, F32),
            dma((n - 1,)),
            dma((n,)),
            dma((m - 1,)),
            dma((m,)),
        ],
        compiler_params=pltpu.CompilerParams(collective_id=1, has_side_effects=True),
        name="total_small",
    )(flat).reshape(-1)
    out, at = [], 0
    for v, size in zip(vectors, sizes):
        out.append(summed[at : at + size].reshape(v.shape))
        at += size
    return out


def unrotate(front, back, c, s):
    return front * c + back * s, back * c - front * s


def bit_orders(m):
    bits = list(range(m.bit_length() - 1))
    return [bits, bits[:1] + bits[:0:-1], bits]


def bwd_kernel(n, heads, rows, bk, sub, m, *refs):
    steps = m.bit_length() - 1
    (pref_ref, send_ref, qkv_ref, of_ref, lse_ref, cos_ref, sin_ref, normed_ref), refs = refs[:8], refs[8:]
    parts, refs = refs[:3], refs[3:]
    (g_ref, back_ref), refs = refs[:2], refs[2:]
    (rw_ref,), results, refs = refs[:1], refs[1:4], refs[4:]
    (do_ref, q2_ref, qn_ref, don_ref, dd_ref, dq_ref, dk_ref, dv_ref), refs = refs[:8], refs[8:]
    (wv_ref, ws_ref, wb_ref, wf_ref), refs = refs[:4], refs[4:]
    tracks = []
    for tag, order in enumerate(bit_orders(m)):
        held, came, (zbuf, fin) = refs[0], refs[1 : steps + 1], refs[steps + 1 : steps + 3]
        refs = refs[steps + 3 :]
        tracks.append((tag, order, parts[tag], held, came, zbuf, fin, results[tag]))
    (own_sem, s_sem, r_sem, kvs, kvr, qs, qr, kvo, qo), refs = refs[:9], refs[9:]
    (hs, hr, ho, p2s, p2r, p2o, p3s, p3r, p3o, w1s, w1r, w1o, w2s, w2r, w2o) = refs
    z = lax.axis_index("tensor")
    dp = lax.axis_index("dp")
    length = n * rows
    per = rows // bk
    prefix_chunks = -(-(length // 2) // rows)
    greet([("tensor", n), ("dp", m)])

    def spread(axis, me, count, pick, dst, send, recv, own, tag):
        pltpu.make_async_copy(pick(me), dst.at[me], own.at[tag]).start()
        for k in range(1, count):
            d = lax.rem(me + k, count)
            remote(pick(d), dst.at[me], send.at[tag, k - 1], recv.at[tag, me], {axis: d}).start()

    def arrived(axis, me, count, pick, dst, recv, send, own, tag):
        pltpu.make_async_copy(pick(me), dst.at[me], own.at[tag]).wait()
        for k in range(1, count):
            d = lax.rem(me + k, count)
            copy = remote(pick(d), dst.at[d], send.at[tag, k - 1], recv.at[tag, d], {axis: d})
            copy.wait_send()
            copy.wait_recv()

    def own_bit(b):
        return (dp // 2**b) % 2

    def slice_of(order, bit, j):
        index = bit * 2 ** order[0]
        for place, b in enumerate(order[1:]):
            index = index + ((j >> place) & 1) * 2**b
        return index

    def place(order, i, last):
        at = last * 2 ** (i - 1)
        for k in range(1, i):
            at = at + own_bit(order[k]) * 2 ** (k - 1)
        return at

    def halve_copies(i):
        for tag, order, part, held, came, zbuf, fin, res in tracks:
            bit = own_bit(order[i])
            partner = dp + (1 - 2 * bit) * 2 ** order[i]
            for j in range(m >> (i + 1)):
                src = part.at[slice_of(order, 1 - bit, j)] if i == 0 else held.at[place(order, i, 1 - bit) + 2**i * j]
                yield tag, j, bit, order, remote(src, came[i].at[j], hs.at[tag, i, j], hr.at[tag, i, j], {"dp": partner})

    def kept_copies():
        for tag, order, part, held, came, zbuf, fin, res in tracks:
            for j in range(m // 2):
                src = part.at[slice_of(order, own_bit(order[0]), j)]
                yield pltpu.make_async_copy(src, held.at[j], ho.at[tag, j])

    def halve_start(i):
        for _, _, _, _, copy in halve_copies(i):
            copy.start()

    def halve_sum(i):
        if i == 0:
            for copy in kept_copies():
                copy.wait()
        for tag, j, bit, order, copy in halve_copies(i):
            copy.wait_send()
            copy.wait_recv()
            held, came = tracks[tag][3], tracks[tag][4]
            at = j if i == 0 else place(order, i, bit) + 2**i * j
            for t in range(n):
                held[at, t] = (held[at, t].astype(F32) + came[i][j, t].astype(F32)).astype(BF)

    def line_start():
        for tag, order, part, held, came, zbuf, fin, res in tracks:
            spread("tensor", z, n, lambda d, held=held, order=order: held.at[place(order, steps - 1, own_bit(order[-1])), d], zbuf, p2s, p2r, p2o, tag)

    def line_sum():
        for tag, order, part, held, came, zbuf, fin, res in tracks:
            arrived("tensor", z, n, lambda d, held=held, order=order: held.at[place(order, steps - 1, own_bit(order[-1])), d], zbuf, p2r, p2s, p2o, tag)
            total = zbuf[0].astype(F32)
            for k in range(1, n):
                total = total + zbuf[k].astype(F32)
            fin[...] = total.astype(BF)
            spread("dp", dp, m, lambda d, fin=fin: fin, res, p3s, p3r, p3o, tag)

    def after_last():
        for tag, order, part, held, came, zbuf, fin, res in tracks:
            arrived("dp", dp, m, lambda d, fin=fin: fin, res, p3r, p3s, p3o, tag)

    for copy in kept_copies():
        copy.start()
    halve_start(0)
    points = (0, 3, 4) if steps == 3 else tuple(range(steps))

    def at_point(e):
        for i, point in enumerate(points):

            @pl.when(e == point)
            def _(i=i):
                halve_sum(i)
                if i + 1 < steps:
                    halve_start(i + 1)
                else:
                    line_start()

        @pl.when(e == 2 * n - 1)
        def _():
            line_sum()

    def weight_start(h):
        grad = dg(g_ref[h, 0], normed_ref[0], 1, 0)
        for t in range(1, n):
            grad = grad + dg(g_ref[h, t], normed_ref[t], 1, 0)
        wv_ref[...] = grad
        q = 3 * HD // m
        for i in range(m):
            ws_ref[h, i] = wv_ref[i * q : (i + 1) * q].astype(BF)
        spread("dp", dp, m, lambda d: ws_ref.at[h, d], wb_ref.at[h], w1s, w1r, w1o, h)

    def weight_sum(h):
        arrived("dp", dp, m, lambda d: ws_ref.at[h, d], wb_ref.at[h], w1r, w1s, w1o, h)
        total = wb_ref[h, 0].astype(F32)
        for k in range(1, m):
            total = total + wb_ref[h, k].astype(F32)
        wf_ref[h] = total.astype(BF)
        spread("dp", dp, m, lambda d: wf_ref.at[h], rw_ref.at[h], w2s, w2r, w2o, h)

    def weight_end(h):
        arrived("dp", dp, m, lambda d: wf_ref.at[h], rw_ref.at[h], w2r, w2s, w2o, h)

    def do_copy(h, k):
        d = lax.rem(z + k, n)
        return remote(send_ref.at[d, h], do_ref.at[h, z], s_sem.at[h, k - 1], r_sem.at[h, k - 1], {"tensor": d})

    def own_copy(h):
        return pltpu.make_async_copy(send_ref.at[z, h], do_ref.at[h, z], own_sem.at[h])

    for h in range(heads):
        own_copy(h).start()
        for k in range(1, n):
            do_copy(h, k).start()
    prefix = pref_ref[0]
    kv_rows, q_rows = pl.ds(HD, 2 * HD), pl.ds(0, HD)

    def piece(h, t, part, source, send, recv):
        return remote(
            g_ref.at[h, t, part], back_ref.at[h, source, part], send.at[h, t], recv.at[h, source], {"tensor": t}
        )

    def own_piece(h, part, sem):
        return pltpu.make_async_copy(g_ref.at[h, z, part], back_ref.at[h, z, part], sem.at[h])

    def hand_out(h, t, part, send, recv, own):
        @pl.when(z != t)
        def _():
            piece(h, t, part, z, send, recv).start()

        @pl.when(z == t)
        def _():
            own_piece(h, part, own).start()

    def head(h, carry):
        own_copy(h).wait()
        for k in range(1, n):
            do_copy(h, k).wait_recv()
        for c in range(n):
            q = qkv_ref[h, c, 0]
            q2_ref[c] = split_query(q)
            qn_ref[c] = q.astype(F32).T.astype(BF)
            dof = do_ref[h, c].astype(F32)
            don_ref[c] = dof.T.astype(BF)
            inner = jnp.sum(dof * of_ref[h, c], axis=0, keepdims=True)
            dd_ref[c] = jnp.concatenate([inner, lse_ref[h, c]], axis=0)
            dq_ref[c] = jnp.zeros((HD, rows), F32)

        def keys(t, c1):
            for o in range(0, rows, bk):
                kt = qkv_ref[h, t, 1, :, o : o + bk]
                kn = kt.astype(F32).T.astype(BF)
                k2 = jnp.concatenate([kn, kn], axis=1)
                vn = qkv_ref[h, t, 2, :, o : o + bk].astype(F32).T.astype(BF)
                dk_ref[...] = jnp.zeros(dk_ref.shape, F32)
                dv_ref[...] = jnp.zeros(dv_ref.shape, F32)

                def block(i, masked, o=o, kt=kt, k2=k2, vn=vn):
                    for s0 in range(0, rows, sub):
                        sl = slice(s0, s0 + sub)
                        p = jnp.exp2(dg(k2, q2_ref[i, :, sl], 1, 0) - dd_ref[i, 1:2, sl])
                        if masked:
                            p = jnp.where(visible(t * rows + o, i * rows + s0, bk, sub, prefix), p, 0.0)
                        dp = dg(vn, do_ref[h, i, :, sl], 1, 0)
                        dv_ref[...] += dg(p.astype(BF), don_ref[i, sl, :], 1, 0)
                        ds = (p * (dp - dd_ref[i, 0:1, sl])).astype(BF)
                        dk_ref[...] += dg(ds, qn_ref[i, sl, :], 1, 0)
                        dq_ref[i, :, sl] += dg(kt, ds, 1, 0)

                def masked_block(i, c2, block=block):
                    block(i, True)
                    return c2

                def full_block(i, c2, block=block):
                    block(i, False)
                    return c2

                lax.fori_loop(jnp.where(t < prefix_chunks, 0, t), t + 1, masked_block, 0)
                lax.fori_loop(t + 1, n, full_block, 0)
                dk = dk_ref[...].T * HD**-0.5
                at = pl.ds(pl.multiple_of(t * rows + o, bk), bk)
                a, b = unrotate(dk[: HD // 2], dk[HD // 2 :], cos_ref[:, at], sin_ref[:, at])
                g_ref[h, t, HD : HD + HD // 2, o : o + bk] = a.astype(BF)
                g_ref[h, t, HD + HD // 2 : 2 * HD, o : o + bk] = b.astype(BF)
                g_ref[h, t, 2 * HD : 3 * HD, o : o + bk] = dv_ref[...].T.astype(BF)
            hand_out(h, t, kv_rows, kvs, kvr, kvo)
            at_point(h * n + t)
            return c1

        lax.fori_loop(0, n, keys, 0)
        for c in range(n):
            x = dq_ref[c] * HD**-0.5
            at = slice(c * rows, (c + 1) * rows)
            a, b = unrotate(x[: HD // 2], x[HD // 2 :], cos_ref[:, at], sin_ref[:, at])
            g_ref[h, c, : HD // 2, :] = a.astype(BF)
            g_ref[h, c, HD // 2 : HD, :] = b.astype(BF)
            hand_out(h, c, q_rows, qs, qr, qo)
        weight_start(h)

        @pl.when(h > 0)
        def _():
            weight_sum(h - 1)

        return carry

    lax.fori_loop(0, heads, head, 0)
    weight_sum(heads - 1)
    after_last()
    for h in range(heads):
        weight_end(h)
    for h in range(heads):
        own_piece(h, kv_rows, kvo).wait()
        own_piece(h, q_rows, qo).wait()
        for k in range(1, n):
            do_copy(h, k).wait_send()
            d = lax.rem(z + k, n)
            for part, send, recv in ((kv_rows, kvs, kvr), (q_rows, qs, qr)):
                copy = piece(h, d, part, d, send, recv)
                copy.wait_send()
                copy.wait_recv()


def attend_back(prefix, send, qkv, of, lse, cos_t, sin_t, normed, parts, bk=512, sub=256):
    n, heads, _, rows = send.shape
    m, width = parts[0].shape[0], parts[0].shape[-1]
    steps = m.bit_length() - 1
    size_w = 3 * HD // m
    length = n * rows
    vmem = pl.BlockSpec(memory_space=pltpu.VMEM)
    dma = pltpu.SemaphoreType.DMA
    buffers = []
    for part in parts:
        size = part.shape[2]
        for count in [m // 2] + [m >> (i + 1) for i in range(steps)]:
            buffers.append(pltpu.VMEM((count, n, size, width), BF))
        buffers += [pltpu.VMEM((n, size, width), BF), pltpu.VMEM((size, width), BF)]
    return pl.pallas_call(
        functools.partial(bwd_kernel, n, heads, rows, bk, sub, m),
        in_specs=[pl.BlockSpec(memory_space=pltpu.SMEM)] + [vmem] * 7 + [pl.BlockSpec(memory_space=pl.ANY)] * 3,
        out_specs=[vmem] * 6,
        out_shape=[
            jax.ShapeDtypeStruct((heads, n, 3 * HD, rows), BF),
            jax.ShapeDtypeStruct((heads, n, 3 * HD, rows), BF),
            jax.ShapeDtypeStruct((heads, m, size_w, width), BF),
        ]
        + [jax.ShapeDtypeStruct((m, part.shape[2], width), BF) for part in parts],
        scratch_shapes=[
            pltpu.VMEM((heads, n, HD, rows), BF),
            pltpu.VMEM((n, 2 * HD, rows), BF),
            pltpu.VMEM((n, rows, HD), BF),
            pltpu.VMEM((n, rows, HD), BF),
            pltpu.VMEM((n, 2, rows), F32),
            pltpu.VMEM((n, HD, rows), F32),
            pltpu.VMEM((bk, HD), F32),
            pltpu.VMEM((bk, HD), F32),
            pltpu.VMEM((3 * HD, width), F32),
            pltpu.VMEM((heads, m, size_w, width), BF),
            pltpu.VMEM((heads, m, size_w, width), BF),
            pltpu.VMEM((heads, size_w, width), BF),
        ]
        + buffers
        + [
            dma((heads,)),
            dma((heads, n - 1)),
            dma((heads, n - 1)),
            dma((heads, n)),
            dma((heads, n)),
            dma((heads, n)),
            dma((heads, n)),
            dma((heads,)),
            dma((heads,)),
            dma((3, steps, m // 2)),
            dma((3, steps, m // 2)),
            dma((3, m // 2)),
            dma((3, n - 1)),
            dma((3, n)),
            dma((3,)),
            dma((3, m - 1)),
            dma((3, m)),
            dma((3,)),
            dma((heads, m - 1)),
            dma((heads, m)),
            dma((heads,)),
            dma((heads, m - 1)),
            dma((heads, m)),
            dma((heads,)),
        ],
        compiler_params=pltpu.CompilerParams(
            collective_id=2, has_side_effects=True, vmem_limit_bytes=63 * 2**20
        ),
        cost_estimate=pl.CostEstimate(
            flops=int(heads * 10 * 256 * length * length * 0.7),
            bytes_accessed=heads * length * HD * 20,
            transcendentals=int(heads * length * length * 0.7),
        ),
        name="attend_backward",
    )(prefix, send, qkv, of, lse, cos_t, sin_t, normed, *parts)


EPS = 1e-05
ROPE_BASE = 10000.0
GELU_C = 0.7978845608028654


def layer_norm(values, norm_gain, norm_shift):
    center = values - jnp.mean(values, axis=-1, keepdims=True)
    spread = jnp.mean(center * center, axis=-1, keepdims=True)
    return center * lax.rsqrt(spread + EPS) * norm_gain + norm_shift


def rotary_tables(length):
    half_dim = HD // 2
    frequency = ROPE_BASE ** (-jnp.arange(half_dim, dtype=jnp.float32) / half_dim)
    angles = frequency[:, None] * jnp.arange(length, dtype=jnp.float32)[None, :]
    return (jnp.cos(angles), jnp.sin(angles))


def mlp_kernel(
    split, size, block, nm_ref, gm_ref, w_ref, upb_ref, out_ref, dnm_ref, dup_ref, ddown_ref, dupb_ref, nmt_ref, gmt_ref, act_ref, gp_ref
):
    step = pl.program_id(0)

    @pl.when(step == 0)
    def _():
        nmt_ref[...] = nm_ref[...].T
        gmt_ref[...] = gm_ref[...].T
        out_ref[...] = jnp.zeros(out_ref.shape, F32)
        dnm_ref[...] = jnp.zeros(dnm_ref.shape, F32)

    width = w_ref.shape[-1]
    up = w_ref[:, :size].reshape(split * size, width)
    down = w_ref[:, size : 2 * size].reshape(split * size, width)
    for r in range(0, nm_ref.shape[0], block):
        at = slice(r, r + block)
        pre = dg(nm_ref[at], up, 1, 0) + upb_ref[...]
        sq = pre * pre
        th = jnp.tanh(GELU_C * (pre + 0.044715 * sq * pre))
        half = 0.5 * (1.0 + th)
        act = (pre * half).astype(BF)
        slope = half + 0.5 * pre * (1.0 - th * th) * (GELU_C + (3.0 * 0.044715 * GELU_C) * sq)
        gp = (dg(gm_ref[at], down, 1, 1) * slope).astype(BF)
        act_ref[at] = act
        gp_ref[at] = gp
        out_ref[at] += dg(act, down, 1, 0)
        dnm_ref[at] += dg(gp, up, 1, 1)
    dup_ref[...] = dg(nmt_ref[...], gp_ref[...], 1, 0).astype(BF).reshape(split, size, width)
    ddown_ref[...] = dg(gmt_ref[...], act_ref[...], 1, 0).astype(BF).reshape(split, size, width)
    dupb_ref[...] = jnp.sum(gp_ref[...].astype(F32), axis=0, keepdims=True)


def mlp(nm, gm, weights, up_bias, size, block=256):
    rows, width = nm.shape
    split, n, deep, _ = weights.shape
    f = split * size
    squeezed = pl.Squeezed()
    const = pl.BlockSpec((rows, width), lambda i: (0, 0))
    hidden = n * f
    return pl.pallas_call(
        functools.partial(mlp_kernel, split, size, block),
        grid=(n,),
        in_specs=[
            const,
            const,
            pl.BlockSpec((split, squeezed, deep, width), lambda i: (0, i, 0, 0)),
            pl.BlockSpec((1, f), lambda i: (0, i)),
        ],
        out_specs=[
            const,
            const,
            pl.BlockSpec((split, squeezed, size, width), lambda i: (0, i, 0, 0)),
            pl.BlockSpec((split, squeezed, size, width), lambda i: (0, i, 0, 0)),
            pl.BlockSpec((1, f), lambda i: (0, i)),
        ],
        out_shape=[
            jax.ShapeDtypeStruct((rows, width), F32),
            jax.ShapeDtypeStruct((rows, width), F32),
            jax.ShapeDtypeStruct((split, n, size, width), BF),
            jax.ShapeDtypeStruct((split, n, size, width), BF),
            jax.ShapeDtypeStruct((1, hidden), F32),
        ],
        scratch_shapes=[pltpu.VMEM((width, rows), BF)] * 2 + [pltpu.VMEM((rows, f), BF)] * 2,
        compiler_params=pltpu.CompilerParams(vmem_limit_bytes=60 * 2**20),
        cost_estimate=pl.CostEstimate(
            flops=12 * rows * width * hidden, bytes_accessed=8 * width * hidden + 12 * rows * width, transcendentals=rows * hidden
        ),
        name="mlp",
    )(nm, gm, weights, up_bias)


def gather_parts(parts):
    column = lax.all_gather(parts, "tensor", axis=0, tiled=False)
    return lax.all_gather(column, "dp", axis=0, tiled=False)


def shards(
    block_input,
    embedding,
    history,
    cotangent,
    first_gain,
    first_shift,
    qkv_weight,
    qkv_bias,
    out_weight,
    out_bias,
    second_gain,
    second_shift,
    up_weight,
    up_bias,
    down_weight,
    down_bias,
    depth_weights,
    prefix_length,
    history_index,
):
    rows, width = block_input.shape
    local = qkv_weight.shape[2]
    heads = local // HD
    n = lax.axis_size("tensor")
    m = lax.axis_size("dp")
    z = lax.axis_index("tensor")
    dp = lax.axis_index("dp")
    length = rows * n
    hidden = up_weight.shape[1]
    cos_t, sin_t = rotary_tables(length)

    w_t = qkv_weight.reshape(width, 3, heads, HD).transpose(2, 1, 3, 0).reshape(3 * local, width)
    b_t = qkv_bias.reshape(3, heads, HD).transpose(1, 0, 2).reshape(3 * local).astype(F32)
    def mine(shard):
        size = shard.shape[0] // m
        return lax.dynamic_slice_in_dim(shard, dp * size, size, 0)

    size, out_size = width // m, local // m
    used = 2 * size + out_size
    fill = jnp.zeros((15 - used % 16, width), BF)
    early = jnp.concatenate([mine(up_weight), mine(down_weight), mine(out_weight), up_bias[None], fill], axis=0)
    every = gather_parts(early)
    out_all = every[:, :, 2 * size : used].transpose(1, 0, 2, 3).reshape(n, heads, HD, width)
    up_bias_all = every[0, :, used, :hidden].astype(F32).reshape(1, n * hidden)

    inputs_f = block_input.astype(F32)
    normed, qkv_t, attended, of, lse = attend(
        prefix_length, block_input, first_gain, first_shift, w_t, b_t, cos_t, sin_t, n
    )
    late, attended = lax.optimization_barrier((mine(w_t), attended))
    w_all = gather_parts(late).transpose(1, 0, 2, 3).reshape(n, heads, 3 * HD, width)
    attn = None
    for h in range(heads):
        piece = dg(attended[h].reshape(n * HD, rows), out_all[:, h].reshape(n * HD, width), 0, 0)
        attn = piece if attn is None else attn + piece


    middle = inputs_f + (attn + out_bias.astype(F32))
    normed_mid_f, second_pull = jax.vjp(layer_norm, middle, second_gain, second_shift)
    grad_top = cotangent.astype(F32)
    grad_block = depth_weights[4] * grad_top
    grad_branch = grad_block.astype(BF)
    if size % 16 == 0:
        mlp_weights, part = every, size
    else:
        whole = every[:, :, : 2 * size].reshape(m, n, 2, size, width)
        mlp_weights, part = whole.transpose(1, 2, 0, 3, 4).reshape(1, n, 2 * hidden, width), hidden
    mlp_out, grad_normed_mid, up_grad, down_grad, up_bias_grad = mlp(
        normed_mid_f.astype(BF), grad_branch, mlp_weights, up_bias_all, part
    )
    if size % 16 != 0:
        up_grad = up_grad.reshape(n, m, size, width).transpose(1, 0, 2, 3)
        down_grad = down_grad.reshape(n, m, size, width).transpose(1, 0, 2, 3)
    block_out = middle + (mlp_out + down_bias.astype(F32))
    slot_ids = jnp.arange(3, dtype=jnp.int32)
    pick = (history_index[:, None] == slot_ids[None, :]).astype(F32)
    slot_coef = jnp.sum(depth_weights[1:4, None] * pick, axis=0)
    embed_f = embedding.astype(F32)
    mixed = depth_weights[0] * embed_f + depth_weights[4] * block_out
    for slot_id in range(3):
        mixed = mixed + slot_coef[slot_id] * history[slot_id].astype(F32)
    dwa_output = mixed.astype(BF)
    slot_sums = jnp.stack([jnp.sum(grad_top * history[slot_id].astype(F32)) for slot_id in range(3)])
    grad_depth = jnp.concatenate(
        [
            jnp.sum(grad_top * embed_f)[None],
            jnp.sum(pick * slot_sums[None, :], axis=1),
            jnp.sum(grad_top * block_out)[None],
        ]
    )
    down_bias_grad = jnp.sum(grad_branch.astype(F32), axis=0)

    grad_middle_ln, second_gain_grad, second_shift_grad = second_pull(grad_normed_mid)
    grad_middle = grad_block + grad_middle_ln
    grad_attn = grad_middle.astype(BF)
    out_bias_grad = jnp.sum(grad_attn.astype(F32), axis=0)

    grad_send = jnp.stack(
        [dg(out_all[:, h].reshape(n * HD, width), grad_attn, 1, 1).astype(BF).reshape(n, HD, rows) for h in range(heads)],
        axis=1,
    )
    out_grad = jnp.stack(
        [dg(attended[h].reshape(n * HD, rows), grad_attn, 1, 0).astype(BF).reshape(n, HD, width) for h in range(heads)], axis=1
    )
    out_grad = out_grad.reshape(n, m, out_size, width).transpose(1, 0, 2, 3)
    grad_own, back, qkv_sum, up_sum, down_sum, out_sum = attend_back(
        prefix_length, grad_send, qkv_t, of, lse, cos_t, sin_t, normed, (up_grad, down_grad, out_grad)
    )
    grad_normed = None
    for h in range(heads):
        piece = dg(back[h].reshape(n * 3 * HD, rows), w_all[:, h].reshape(n * 3 * HD, width), 0, 0)
        grad_normed = piece if grad_normed is None else grad_normed + piece
    qkv_bias_grad = jnp.sum(grad_own.astype(F32), axis=(1, 3)).reshape(-1)
    first_normed, first_pull = jax.vjp(layer_norm, inputs_f, first_gain, first_shift)
    grad_input_ln, first_gain_grad, first_shift_grad = first_pull(grad_normed)
    grad_input = grad_middle + grad_input_ln

    up_grad = up_sum.reshape(width, hidden).astype(F32)
    down_grad = down_sum.reshape(width, hidden).T.astype(F32)
    out_grad = out_sum.reshape(local, width).astype(F32)
    qkv_grad = qkv_sum.reshape(heads, 3, HD, width).transpose(3, 1, 0, 2).reshape(width, 3, local).astype(F32)

    spread = jnp.zeros((n, 3 * local), F32)
    spread = lax.dynamic_update_slice_in_dim(spread, qkv_bias_grad[None], z, 0)
    (
        out_bias_grad,
        second_gain_grad,
        second_shift_grad,
        down_bias_grad,
        grad_depth,
        up_bias_grad,
        qkv_bias_grad,
        first_gain_grad,
        first_shift_grad,
    ) = total_small(
        [
            out_bias_grad,
            second_gain_grad,
            second_shift_grad,
            down_bias_grad,
            grad_depth,
            up_bias_grad[0],
            spread,
            first_gain_grad,
            first_shift_grad,
        ],
        n,
        m,
    )
    up_bias_grad = lax.dynamic_slice_in_dim(up_bias_grad, z * hidden, hidden, 0)
    qkv_bias_grad = lax.dynamic_index_in_dim(qkv_bias_grad, z, 0, keepdims=False)
    qkv_bias_grad = qkv_bias_grad.reshape(heads, 3, HD).transpose(1, 0, 2).reshape(3, local)
    return (
        dwa_output,
        grad_input,
        first_gain_grad,
        first_shift_grad,
        qkv_grad,
        qkv_bias_grad,
        out_grad,
        out_bias_grad,
        second_gain_grad,
        second_shift_grad,
        up_grad,
        up_bias_grad,
        down_grad,
        down_bias_grad,
        grad_depth,
    )


def solution(mesh):
    both = ("dp", "tensor")
    return jax.shard_map(
        shards,
        mesh=mesh,
        in_specs=(
            P(both, None),
            P(both, None),
            P(None, both, None),
            P(both, None),
            P(),
            P(),
            P(None, None, "tensor"),
            P(None, "tensor"),
            P("tensor", None),
            P(),
            P(),
            P(),
            P(None, "tensor"),
            P("tensor"),
            P("tensor", None),
            P(),
            P(),
            P("dp"),
            P(),
        ),
        out_specs=(
            P(both, None),
            P(both, None),
            P(),
            P(),
            P(None, None, "tensor"),
            P(None, "tensor"),
            P("tensor", None),
            P(),
            P(),
            P(),
            P(None, "tensor"),
            P("tensor"),
            P("tensor", None),
            P(),
            P(),
        ),
        check_vma=False,
    )
```

```python
import functools

import jax
import jax.numpy as jnp
from jax import lax
from jax.experimental import pallas as pl
from jax.experimental.pallas import tpu as pltpu
from jax.sharding import PartitionSpec as P

HD = 64
NEG = -1e30
LOG2E = 1.4426950408889634
F32 = jnp.float32
BF = jnp.bfloat16


def dg(a, b, ca, cb):
    return lax.dot_general(a, b, (((ca,), (cb,)), ((), ())), preferred_element_type=F32)


def split_query(q):
    scaled = q.astype(F32) * (LOG2E * HD**-0.5)
    high = scaled.astype(BF)
    low = (scaled - high.astype(F32)).astype(BF)
    return jnp.concatenate([high, low], axis=0)


def visible(key_start, query_start, keys, queries, prefix):
    key_pos = key_start + lax.broadcasted_iota(jnp.int32, (keys, queries), 0)
    query_pos = query_start + lax.broadcasted_iota(jnp.int32, (1, queries), 1)
    return key_pos <= jnp.maximum(query_pos, prefix - 1)


def remote(src, dst, send, recv, peer):
    return pltpu.make_async_remote_copy(
        src_ref=src,
        dst_ref=dst,
        send_sem=send,
        recv_sem=recv,
        device_id=peer,
        device_id_type=pl.DeviceIdType.MESH,
    )


def greet(axis_counts):
    barrier = pltpu.get_barrier_semaphore()
    total = 0
    for axis, count in axis_counts:
        me = lax.axis_index(axis)
        for k in range(1, count):
            pl.semaphore_signal(
                barrier, inc=1, device_id={axis: lax.rem(me + k, count)}, device_id_type=pl.DeviceIdType.MESH
            )
        total += count - 1
    pl.semaphore_wait(barrier, total)


def gatherer(n, m, src, dst, line_send, line_recv, plane_send, plane_recv, own):
    z = lax.axis_index("tensor")
    dp = lax.axis_index("dp")

    def keep():
        return pltpu.make_async_copy(src, dst.at[dp, z], own.at[0])

    def line(k, t):
        return remote(src, dst.at[dp, t], line_send.at[k - 1], line_recv.at[t], {"tensor": lax.rem(z + k, n)})

    def plane(kk, k, d):
        t = lax.rem(z + kk, n)
        start = src if kk == 0 else dst.at[dp, t]
        peer = lax.rem(dp + k, m)
        return remote(start, dst.at[d, t], plane_send.at[kk, k - 1], plane_recv.at[t, d], {"dp": peer})

    def start():
        keep().start()
        for k in range(1, n):
            line(k, z).start()
        for k in range(1, m):
            plane(0, k, dp).start()

    def forward():
        for kk in range(1, n):
            line(kk, lax.rem(z + kk, n)).wait_recv()
            for k in range(1, m):
                plane(kk, k, dp).start()

    def finish():
        keep().wait()
        for k in range(1, n):
            line(k, z).wait_send()
        for kk in range(n):
            for k in range(1, m):
                copy = plane(kk, k, lax.rem(dp + k, m))
                copy.wait_send()
                copy.wait_recv()

    return start, forward, finish


def gather_sems(n, m):
    dma = pltpu.SemaphoreType.DMA
    return [dma((n - 1,)), dma((n,)), dma((n, m - 1)), dma((n, m)), dma((1,))]


def fwd_kernel(
    n, m, heads, rows, bk, sub,
    pref_ref, x_ref, gain_ref, shift_ref, w_ref, b_ref, cos_ref, sin_ref, shard_ref,
    normed_ref, qkv_ref, att_ref, of_ref, lse_ref, every_ref,
    q2_ref, k2_ref, v2_ref, m_ref, acc_ref, ob_ref, rs, rr, ls, lr, os_sem, or_sem, oo_sem, *gather,
):
    z = lax.axis_index("tensor")
    per = rows // bk
    prefix_chunks = -(-(n * rows // 2) // rows)
    greet([("tensor", n), ("dp", m)])
    gather_start, gather_forward, gather_finish = gatherer(n, m, shard_ref, every_ref, *gather)
    gather_start()
    prefix = pref_ref[0]

    def to_right(s):
        c = z - (s - 1)
        return remote(normed_ref.at[c], normed_ref.at[c], rs.at[s - 1], rr.at[s - 1], {"tensor": z + 1})

    def to_left(s):
        c = z + (s - 1)
        return remote(normed_ref.at[c], normed_ref.at[c], ls.at[s - 1], lr.at[s - 1], {"tensor": z - 1})

    def from_left(s):
        c = z - s
        return remote(normed_ref.at[c], normed_ref.at[c], rs.at[s - 1], rr.at[s - 1], {"tensor": z - 1})

    def from_right(s):
        c = z + s
        return remote(normed_ref.at[c], normed_ref.at[c], ls.at[s - 1], lr.at[s - 1], {"tensor": z + 1})

    def has_right(s):
        return (z + 1 < n) & (z - (s - 1) >= 0)

    def has_left(s):
        return (z >= 1) & (z + (s - 1) < n)

    for o in range(0, rows, bk):
        x = x_ref[o : o + bk].astype(F32)
        normed_ref[z, o : o + bk] = layer_norm(x, gain_ref[...], shift_ref[...]).astype(BF)

    @pl.when(has_right(1))
    def _():
        to_right(1).start()

    @pl.when(has_left(1))
    def _():
        to_left(1).start()

    m_ref[...] = jnp.full(m_ref.shape, NEG, F32)
    acc_ref[...] = jnp.zeros(acc_ref.shape, F32)
    first = lax.broadcasted_iota(jnp.int32, (16, bk), 0) == 0
    for h in range(heads):
        for c in range(n * per):
            v2_ref[h, c, HD : HD + 16, :] = jnp.where(first, 1.0, 0.0).astype(BF)

    def att_remote(h, i):
        return remote(ob_ref.at[h, i], att_ref.at[h, z], os_sem.at[h, i], or_sem.at[h, z], {"tensor": i})

    def att_own(h):
        return pltpu.make_async_copy(ob_ref.at[h, z], att_ref.at[h, z], oo_sem.at[h])

    def enter(c):
        for o in range(0, rows, bk):
            at = pl.ds(pl.multiple_of(c * rows + o, bk), bk)
            cos, sin = cos_ref[:, at], sin_ref[:, at]
            proj = dg(w_ref[...], normed_ref[c, o : o + bk, :], 1, 1) + b_ref[...]
            for h in range(heads):
                r0 = h * 3 * HD
                parts = []
                for part in range(2):
                    u = proj[r0 + part * HD : r0 + (part + 1) * HD]
                    f, b = u[: HD // 2], u[HD // 2 :]
                    parts.append(jnp.concatenate([f * cos - b * sin, b * cos + f * sin], axis=0))
                q = parts[0].astype(BF)
                v = proj[r0 + 2 * HD : r0 + 3 * HD].astype(BF)
                qkv_ref[h, c, 0, :, o : o + bk] = q
                qkv_ref[h, c, 1, :, o : o + bk] = parts[1].astype(BF)
                qkv_ref[h, c, 2, :, o : o + bk] = v
                q2_ref[h, c, :, o : o + bk] = split_query(q)
                kt = parts[1].T.astype(BF)
                k2_ref[h, c * per + o // bk] = jnp.concatenate([kt, kt], axis=1)
                v2_ref[h, c * per + o // bk, 0:HD, :] = v

    def pair(q, k, masked):
        for h in range(heads):
            for b in range(per):
                kj, vj = k2_ref[h, k * per + b], v2_ref[h, k * per + b]
                for s0 in range(0, rows, sub):
                    sl = slice(s0, s0 + sub)
                    s = dg(kj, q2_ref[h, q, :, sl], 1, 0)
                    if masked:
                        s = jnp.where(visible(k * rows + b * bk, q * rows + s0, bk, sub, prefix), s, NEG)
                    m = m_ref[h, q, :, sl]
                    mn = jnp.maximum(m, jnp.max(s, axis=0, keepdims=True))
                    p = jnp.exp2(s - mn).astype(BF)
                    scale = jnp.exp2(m - mn)
                    m_ref[h, q, :, sl] = mn
                    acc_ref[h, q, :, sl] = acc_ref[h, q, :, sl] * scale + dg(vj, p, 1, 0)

    def finish(q):
        for h in range(heads):
            total = acc_ref[h, q, HD : HD + 1, :]
            out = acc_ref[h, q, 0:HD, :] / total
            of_ref[h, q] = out
            lse_ref[h, q] = m_ref[h, q] + jnp.log2(total)
            ob_ref[h, q] = out.astype(BF)

            @pl.when(z != q)
            def _(h=h):
                att_remote(h, q).start()

            @pl.when(z == q)
            def _(h=h):
                att_own(h).start()

    def event(e, carry):
        s = (e + 1) // 2
        low = e % 2 == 1
        high = (e % 2 == 0) & (e > 0)

        @pl.when(e == 1)
        def _():
            gather_forward()

        @pl.when(low)
        def _():
            @pl.when(z - s >= 0)
            def _():
                from_left(s).wait_recv()

            @pl.when((s + 1 < n) & has_right(s + 1))
            def _():
                to_right(s + 1).start()

            @pl.when(z + s < n)
            def _():
                from_right(s).wait_recv()

            @pl.when((s + 1 < n) & has_left(s + 1))
            def _():
                to_left(s + 1).start()

        c = jnp.where(low, z - s, z + s)
        bottom = jnp.maximum(z - s, 0)
        start = jnp.where(low, c + 1, jnp.where(high, bottom, c))
        stop = jnp.where(low, jnp.minimum(n, z + s), c)

        @pl.when((c >= 0) & (c < n))
        def _():
            enter(c)
            all_low = low & (c == 0)

            def full_pair(a, t):
                pair(jnp.maximum(a, c), jnp.minimum(a, c), False)

                @pl.when(all_low)
                def _():
                    finish(a)

                return t

            lax.fori_loop(start, stop, full_pair, 0)

            def masked_pair(a, t):
                pair(jnp.minimum(a, c), jnp.maximum(a, c), True)
                return t

            inner = c < prefix_chunks
            lax.fori_loop(
                jnp.where(inner & high, start, c),
                jnp.where(inner & low, jnp.minimum(stop, prefix_chunks), c + 1),
                masked_pair,
                0,
            )
            ready = all_low | ((bottom == 0) & high & (c >= prefix_chunks - 1))
            from_q = jnp.where(c == prefix_chunks - 1, 0, c)

            def finish_one(q, t):
                finish(q)
                return t

            lax.fori_loop(from_q, jnp.where(ready, c + 1, from_q), finish_one, 0)

        return carry

    lax.fori_loop(0, 2 * n - 1, event, 0)
    gather_finish()
    for s in range(1, n):

        @pl.when(has_right(s))
        def _(s=s):
            to_right(s).wait_send()

        @pl.when(has_left(s))
        def _(s=s):
            to_left(s).wait_send()

    for h in range(heads):
        att_own(h).wait()
        for k in range(1, n):
            d = lax.rem(z + k, n)
            att_remote(h, d).wait_send()
            remote(ob_ref.at[h, d], att_ref.at[h, d], os_sem.at[h, d], or_sem.at[h, d], {"tensor": d}).wait_recv()


def attend(prefix, x, gain, shift, w, bias, cos_t, sin_t, shard, n, m, bk=512, sub=512):
    rows, width = x.shape
    heads = w.shape[0] // (3 * HD)
    length = n * rows
    vmem = pl.BlockSpec(memory_space=pltpu.VMEM)
    dma = pltpu.SemaphoreType.DMA
    return pl.pallas_call(
        functools.partial(fwd_kernel, n, m, heads, rows, bk, sub),
        in_specs=[pl.BlockSpec(memory_space=pltpu.SMEM)] + [vmem] * 7 + [pl.BlockSpec(memory_space=pl.ANY)],
        out_specs=[vmem] * 5 + [pl.BlockSpec(memory_space=pl.ANY)],
        out_shape=[
            jax.ShapeDtypeStruct((n, rows, width), BF),
            jax.ShapeDtypeStruct((heads, n, 3, HD, rows), BF),
            jax.ShapeDtypeStruct((heads, n, HD, rows), BF),
            jax.ShapeDtypeStruct((heads, n, HD, rows), F32),
            jax.ShapeDtypeStruct((heads, n, 1, rows), F32),
            jax.ShapeDtypeStruct((m, n) + shard.shape, BF),
        ],
        scratch_shapes=[
            pltpu.VMEM((heads, n, 2 * HD, rows), BF),
            pltpu.VMEM((heads, length // bk, bk, 2 * HD), BF),
            pltpu.VMEM((heads, length // bk, HD + 16, bk), BF),
            pltpu.VMEM((heads, n, 1, rows), F32),
            pltpu.VMEM((heads, n, HD + 16, rows), F32),
            pltpu.VMEM((heads, n, HD, rows), BF),
            dma((n - 1,)),
            dma((n - 1,)),
            dma((n - 1,)),
            dma((n - 1,)),
            dma((heads, n)),
            dma((heads, n)),
            dma((heads,)),
        ]
        + gather_sems(n, m),
        compiler_params=pltpu.CompilerParams(
            collective_id=0, has_side_effects=True, vmem_limit_bytes=60 * 2**20
        ),
        cost_estimate=pl.CostEstimate(
            flops=int(heads * 4 * 256 * length * length * 0.7),
            bytes_accessed=heads * length * HD * 20,
            transcendentals=int(heads * length * length * 0.7),
        ),
        name="attend_forward",
    )(prefix, x, gain[None], shift[None], w, bias[:, None], cos_t, sin_t, shard)


def small_kernel(n, m, x_ref, o_ref, zbuf, mid, pbuf, zs, zr, ps, pr):
    z = lax.axis_index("tensor")
    d = lax.axis_index("dp")
    greet([("tensor", n), ("dp", m)])

    def stage(axis, me, count, src, buf, send, recv):
        buf[me] = src[...]
        for k in range(1, count):
            peer = lax.rem(me + k, count)
            remote(src, buf.at[me], send.at[k - 1], recv.at[me], {axis: peer}).start()
        for k in range(1, count):
            peer = lax.rem(me + k, count)
            copy = remote(src, buf.at[peer], send.at[k - 1], recv.at[peer], {axis: peer})
            copy.wait_send()
            copy.wait_recv()
        total = buf[0]
        for k in range(1, count):
            total = total + buf[k]
        return total

    mid[...] = stage("tensor", z, n, x_ref, zbuf, zs, zr)
    o_ref[...] = stage("dp", d, m, mid, pbuf, ps, pr)


def total_small(vectors, n, m):
    sizes = [v.size for v in vectors]
    flat = jnp.concatenate([v.reshape(-1) for v in vectors])
    flat = jnp.pad(flat, (0, -flat.size % 1024)).reshape(-1, 128)
    vmem = pl.BlockSpec(memory_space=pltpu.VMEM)
    dma = pltpu.SemaphoreType.DMA
    summed = pl.pallas_call(
        functools.partial(small_kernel, n, m),
        in_specs=[vmem],
        out_specs=vmem,
        out_shape=jax.ShapeDtypeStruct(flat.shape, F32),
        scratch_shapes=[
            pltpu.VMEM((n,) + flat.shape, F32),
            pltpu.VMEM(flat.shape, F32),
            pltpu.VMEM((m,) + flat.shape, F32),
            dma((n - 1,)),
            dma((n,)),
            dma((m - 1,)),
            dma((m,)),
        ],
        compiler_params=pltpu.CompilerParams(collective_id=1, has_side_effects=True),
        name="total_small",
    )(flat).reshape(-1)
    out, at = [], 0
    for v, size in zip(vectors, sizes):
        out.append(summed[at : at + size].reshape(v.shape))
        at += size
    return out


def unrotate(front, back, c, s):
    return front * c + back * s, back * c - front * s


def bit_orders(m):
    bits = list(range(m.bit_length() - 1))
    return [bits, bits[:1] + bits[:0:-1], bits]


def bwd_kernel(n, heads, rows, bk, sub, m, *refs):
    steps = m.bit_length() - 1
    (pref_ref, send_ref, qkv_ref, of_ref, lse_ref, cos_ref, sin_ref, normed_ref), refs = refs[:8], refs[8:]
    parts, (shard_ref,), refs = refs[:3], refs[3:4], refs[4:]
    (g_ref, back_ref), refs = refs[:2], refs[2:]
    (rw_ref,), results, (every_ref,), refs = refs[:1], refs[1:4], refs[4:5], refs[5:]
    (do_ref, q2_ref, qn_ref, don_ref, dd_ref, dq_ref, dk_ref, dv_ref), refs = refs[:8], refs[8:]
    (wv_ref, ws_ref, wb_ref, wf_ref), refs = refs[:4], refs[4:]
    tracks = []
    for tag, order in enumerate(bit_orders(m)):
        held, came, (zbuf, fin) = refs[0], refs[1 : steps + 1], refs[steps + 1 : steps + 3]
        refs = refs[steps + 3 :]
        tracks.append((tag, order, parts[tag], held, came, zbuf, fin, results[tag]))
    (own_sem, s_sem, r_sem, kvs, kvr, qs, qr, kvo, qo), refs = refs[:9], refs[9:]
    (hs, hr, ho, p2s, p2r, p2o, p3s, p3r, p3o, w1s, w1r, w1o, w2s, w2r, w2o), gather = refs[:15], refs[15:]
    z = lax.axis_index("tensor")
    dp = lax.axis_index("dp")
    length = n * rows
    per = rows // bk
    prefix_chunks = -(-(length // 2) // rows)
    greet([("tensor", n), ("dp", m)])

    gather_start, gather_forward, gather_finish = gatherer(n, m, shard_ref, every_ref, *gather)
    def spread(axis, me, count, pick, dst, send, recv, own, tag):
        pltpu.make_async_copy(pick(me), dst.at[me], own.at[tag]).start()
        for k in range(1, count):
            d = lax.rem(me + k, count)
            remote(pick(d), dst.at[me], send.at[tag, k - 1], recv.at[tag, me], {axis: d}).start()

    def arrived(axis, me, count, pick, dst, recv, send, own, tag):
        pltpu.make_async_copy(pick(me), dst.at[me], own.at[tag]).wait()
        for k in range(1, count):
            d = lax.rem(me + k, count)
            copy = remote(pick(d), dst.at[d], send.at[tag, k - 1], recv.at[tag, d], {axis: d})
            copy.wait_send()
            copy.wait_recv()

    def own_bit(b):
        return (dp // 2**b) % 2

    def slice_of(order, bit, j):
        index = bit * 2 ** order[0]
        for place, b in enumerate(order[1:]):
            index = index + ((j >> place) & 1) * 2**b
        return index

    def place(order, i, last):
        at = last * 2 ** (i - 1)
        for k in range(1, i):
            at = at + own_bit(order[k]) * 2 ** (k - 1)
        return at

    def halve_copies(i):
        for tag, order, part, held, came, zbuf, fin, res in tracks:
            bit = own_bit(order[i])
            partner = dp + (1 - 2 * bit) * 2 ** order[i]
            for j in range(m >> (i + 1)):
                src = part.at[slice_of(order, 1 - bit, j)] if i == 0 else held.at[place(order, i, 1 - bit) + 2**i * j]
                yield tag, j, bit, order, remote(src, came[i].at[j], hs.at[tag, i, j], hr.at[tag, i, j], {"dp": partner})

    def kept_copies():
        for tag, order, part, held, came, zbuf, fin, res in tracks:
            for j in range(m // 2):
                src = part.at[slice_of(order, own_bit(order[0]), j)]
                yield pltpu.make_async_copy(src, held.at[j], ho.at[tag, j])

    def halve_start(i):
        for _, _, _, _, copy in halve_copies(i):
            copy.start()

    def halve_sum(i):
        if i == 0:
            for copy in kept_copies():
                copy.wait()
        for tag, j, bit, order, copy in halve_copies(i):
            copy.wait_send()
            copy.wait_recv()
            held, came = tracks[tag][3], tracks[tag][4]
            at = j if i == 0 else place(order, i, bit) + 2**i * j
            for t in range(n):
                held[at, t] = (held[at, t].astype(F32) + came[i][j, t].astype(F32)).astype(BF)

    def line_start():
        for tag, order, part, held, came, zbuf, fin, res in tracks:
            spread("tensor", z, n, lambda d, held=held, order=order: held.at[place(order, steps - 1, own_bit(order[-1])), d], zbuf, p2s, p2r, p2o, tag)

    def line_sum():
        for tag, order, part, held, came, zbuf, fin, res in tracks:
            arrived("tensor", z, n, lambda d, held=held, order=order: held.at[place(order, steps - 1, own_bit(order[-1])), d], zbuf, p2r, p2s, p2o, tag)
            total = zbuf[0].astype(F32)
            for k in range(1, n):
                total = total + zbuf[k].astype(F32)
            fin[...] = total.astype(BF)
            spread("dp", dp, m, lambda d, fin=fin: fin, res, p3s, p3r, p3o, tag)

    def after_last():
        for tag, order, part, held, came, zbuf, fin, res in tracks:
            arrived("dp", dp, m, lambda d, fin=fin: fin, res, p3r, p3s, p3o, tag)

    for copy in kept_copies():
        copy.start()
    halve_start(0)
    points = (0, 3, 4) if steps == 3 else tuple(range(steps))

    def at_point(e):
        for i, point in enumerate(points):

            @pl.when(e == point)
            def _(i=i):
                halve_sum(i)
                if i + 1 < steps:
                    halve_start(i + 1)
                else:
                    line_start()

        @pl.when(e == n + 1)
        def _():
            gather_forward()

        @pl.when(e == 2 * n - 1)
        def _():
            line_sum()

    def weight_start(h):
        grad = dg(g_ref[h, 0], normed_ref[0], 1, 0)
        for t in range(1, n):
            grad = grad + dg(g_ref[h, t], normed_ref[t], 1, 0)
        wv_ref[...] = grad
        q = 3 * HD // m
        for i in range(m):
            ws_ref[h, i] = wv_ref[i * q : (i + 1) * q].astype(BF)
        spread("dp", dp, m, lambda d: ws_ref.at[h, d], wb_ref.at[h], w1s, w1r, w1o, h)

    def weight_sum(h):
        arrived("dp", dp, m, lambda d: ws_ref.at[h, d], wb_ref.at[h], w1r, w1s, w1o, h)
        total = wb_ref[h, 0].astype(F32)
        for k in range(1, m):
            total = total + wb_ref[h, k].astype(F32)
        wf_ref[h] = total.astype(BF)
        spread("dp", dp, m, lambda d: wf_ref.at[h], rw_ref.at[h], w2s, w2r, w2o, h)

    def weight_end(h):
        arrived("dp", dp, m, lambda d: wf_ref.at[h], rw_ref.at[h], w2r, w2s, w2o, h)

    def do_copy(h, k):
        d = lax.rem(z + k, n)
        return remote(send_ref.at[d, h], do_ref.at[h, z], s_sem.at[h, k - 1], r_sem.at[h, k - 1], {"tensor": d})

    def own_copy(h):
        return pltpu.make_async_copy(send_ref.at[z, h], do_ref.at[h, z], own_sem.at[h])

    for h in range(heads):
        own_copy(h).start()
        for k in range(1, n):
            do_copy(h, k).start()
    gather_start()
    prefix = pref_ref[0]
    kv_rows, q_rows = pl.ds(HD, 2 * HD), pl.ds(0, HD)

    def piece(h, t, part, source, send, recv):
        return remote(
            g_ref.at[h, t, part], back_ref.at[h, source, part], send.at[h, t], recv.at[h, source], {"tensor": t}
        )

    def own_piece(h, part, sem):
        return pltpu.make_async_copy(g_ref.at[h, z, part], back_ref.at[h, z, part], sem.at[h])

    def hand_out(h, t, part, send, recv, own):
        @pl.when(z != t)
        def _():
            piece(h, t, part, z, send, recv).start()

        @pl.when(z == t)
        def _():
            own_piece(h, part, own).start()

    def head(h, carry):
        own_copy(h).wait()
        for k in range(1, n):
            do_copy(h, k).wait_recv()
        for c in range(n):
            q = qkv_ref[h, c, 0]
            q2_ref[c] = split_query(q)
            qn_ref[c] = q.astype(F32).T.astype(BF)
            dof = do_ref[h, c].astype(F32)
            don_ref[c] = dof.T.astype(BF)
            inner = jnp.sum(dof * of_ref[h, c], axis=0, keepdims=True)
            dd_ref[c] = jnp.concatenate([inner, lse_ref[h, c]], axis=0)
            dq_ref[c] = jnp.zeros((HD, rows), F32)

        def keys(t, c1):
            for o in range(0, rows, bk):
                kt = qkv_ref[h, t, 1, :, o : o + bk]
                kn = kt.astype(F32).T.astype(BF)
                k2 = jnp.concatenate([kn, kn], axis=1)
                vn = qkv_ref[h, t, 2, :, o : o + bk].astype(F32).T.astype(BF)
                dk_ref[...] = jnp.zeros(dk_ref.shape, F32)
                dv_ref[...] = jnp.zeros(dv_ref.shape, F32)

                def block(i, masked, o=o, kt=kt, k2=k2, vn=vn):
                    for s0 in range(0, rows, sub):
                        sl = slice(s0, s0 + sub)
                        p = jnp.exp2(dg(k2, q2_ref[i, :, sl], 1, 0) - dd_ref[i, 1:2, sl])
                        if masked:
                            p = jnp.where(visible(t * rows + o, i * rows + s0, bk, sub, prefix), p, 0.0)
                        dp = dg(vn, do_ref[h, i, :, sl], 1, 0)
                        dv_ref[...] += dg(p.astype(BF), don_ref[i, sl, :], 1, 0)
                        ds = (p * (dp - dd_ref[i, 0:1, sl])).astype(BF)
                        dk_ref[...] += dg(ds, qn_ref[i, sl, :], 1, 0)
                        dq_ref[i, :, sl] += dg(kt, ds, 1, 0)

                def masked_block(i, c2, block=block):
                    block(i, True)
                    return c2

                def full_block(i, c2, block=block):
                    block(i, False)
                    return c2

                lax.fori_loop(jnp.where(t < prefix_chunks, 0, t), t + 1, masked_block, 0)
                lax.fori_loop(t + 1, n, full_block, 0)
                dk = dk_ref[...].T * HD**-0.5
                at = pl.ds(pl.multiple_of(t * rows + o, bk), bk)
                a, b = unrotate(dk[: HD // 2], dk[HD // 2 :], cos_ref[:, at], sin_ref[:, at])
                g_ref[h, t, HD : HD + HD // 2, o : o + bk] = a.astype(BF)
                g_ref[h, t, HD + HD // 2 : 2 * HD, o : o + bk] = b.astype(BF)
                g_ref[h, t, 2 * HD : 3 * HD, o : o + bk] = dv_ref[...].T.astype(BF)
            hand_out(h, t, kv_rows, kvs, kvr, kvo)
            at_point(h * n + t)
            return c1

        lax.fori_loop(0, n, keys, 0)
        for c in range(n):
            x = dq_ref[c] * HD**-0.5
            at = slice(c * rows, (c + 1) * rows)
            a, b = unrotate(x[: HD // 2], x[HD // 2 :], cos_ref[:, at], sin_ref[:, at])
            g_ref[h, c, : HD // 2, :] = a.astype(BF)
            g_ref[h, c, HD // 2 : HD, :] = b.astype(BF)
            hand_out(h, c, q_rows, qs, qr, qo)
        weight_start(h)

        @pl.when(h > 0)
        def _():
            weight_sum(h - 1)

        return carry

    lax.fori_loop(0, heads, head, 0)
    weight_sum(heads - 1)
    gather_finish()
    after_last()
    for h in range(heads):
        weight_end(h)
    for h in range(heads):
        own_piece(h, kv_rows, kvo).wait()
        own_piece(h, q_rows, qo).wait()
        for k in range(1, n):
            do_copy(h, k).wait_send()
            d = lax.rem(z + k, n)
            for part, send, recv in ((kv_rows, kvs, kvr), (q_rows, qs, qr)):
                copy = piece(h, d, part, d, send, recv)
                copy.wait_send()
                copy.wait_recv()


def attend_back(prefix, send, qkv, of, lse, cos_t, sin_t, normed, parts, shard, bk=512, sub=256):
    n, heads, _, rows = send.shape
    m, width = parts[0].shape[0], parts[0].shape[-1]
    steps = m.bit_length() - 1
    size_w = 3 * HD // m
    length = n * rows
    vmem = pl.BlockSpec(memory_space=pltpu.VMEM)
    dma = pltpu.SemaphoreType.DMA
    buffers = []
    for part in parts:
        size = part.shape[2]
        for count in [m // 2] + [m >> (i + 1) for i in range(steps)]:
            buffers.append(pltpu.VMEM((count, n, size, width), BF))
        buffers += [pltpu.VMEM((n, size, width), BF), pltpu.VMEM((size, width), BF)]
    return pl.pallas_call(
        functools.partial(bwd_kernel, n, heads, rows, bk, sub, m),
        in_specs=[pl.BlockSpec(memory_space=pltpu.SMEM)] + [vmem] * 7 + [pl.BlockSpec(memory_space=pl.ANY)] * 4,
        out_specs=[vmem] * 6 + [pl.BlockSpec(memory_space=pl.ANY)],
        out_shape=[
            jax.ShapeDtypeStruct((heads, n, 3 * HD, rows), BF),
            jax.ShapeDtypeStruct((heads, n, 3 * HD, rows), BF),
            jax.ShapeDtypeStruct((heads, m, size_w, width), BF),
        ]
        + [jax.ShapeDtypeStruct((m, part.shape[2], width), BF) for part in parts]
        + [jax.ShapeDtypeStruct((m, n) + shard.shape, BF)],
        scratch_shapes=[
            pltpu.VMEM((heads, n, HD, rows), BF),
            pltpu.VMEM((n, 2 * HD, rows), BF),
            pltpu.VMEM((n, rows, HD), BF),
            pltpu.VMEM((n, rows, HD), BF),
            pltpu.VMEM((n, 2, rows), F32),
            pltpu.VMEM((n, HD, rows), F32),
            pltpu.VMEM((bk, HD), F32),
            pltpu.VMEM((bk, HD), F32),
            pltpu.VMEM((3 * HD, width), F32),
            pltpu.VMEM((heads, m, size_w, width), BF),
            pltpu.VMEM((heads, m, size_w, width), BF),
            pltpu.VMEM((heads, size_w, width), BF),
        ]
        + buffers
        + [
            dma((heads,)),
            dma((heads, n - 1)),
            dma((heads, n - 1)),
            dma((heads, n)),
            dma((heads, n)),
            dma((heads, n)),
            dma((heads, n)),
            dma((heads,)),
            dma((heads,)),
            dma((3, steps, m // 2)),
            dma((3, steps, m // 2)),
            dma((3, m // 2)),
            dma((3, n - 1)),
            dma((3, n)),
            dma((3,)),
            dma((3, m - 1)),
            dma((3, m)),
            dma((3,)),
            dma((heads, m - 1)),
            dma((heads, m)),
            dma((heads,)),
            dma((heads, m - 1)),
            dma((heads, m)),
            dma((heads,)),
        ]
        + gather_sems(n, m),
        compiler_params=pltpu.CompilerParams(
            collective_id=2, has_side_effects=True, vmem_limit_bytes=63 * 2**20
        ),
        cost_estimate=pl.CostEstimate(
            flops=int(heads * 10 * 256 * length * length * 0.7),
            bytes_accessed=heads * length * HD * 20,
            transcendentals=int(heads * length * length * 0.7),
        ),
        name="attend_backward",
    )(prefix, send, qkv, of, lse, cos_t, sin_t, normed, *parts, shard)


EPS = 1e-05
ROPE_BASE = 10000.0
GELU_C = 0.7978845608028654


def layer_norm(values, norm_gain, norm_shift):
    center = values - jnp.mean(values, axis=-1, keepdims=True)
    spread = jnp.mean(center * center, axis=-1, keepdims=True)
    return center * lax.rsqrt(spread + EPS) * norm_gain + norm_shift


def rotary_tables(length):
    half_dim = HD // 2
    frequency = ROPE_BASE ** (-jnp.arange(half_dim, dtype=jnp.float32) / half_dim)
    angles = frequency[:, None] * jnp.arange(length, dtype=jnp.float32)[None, :]
    return (jnp.cos(angles), jnp.sin(angles))


def mlp_kernel(
    split, size, block, nm_ref, gm_ref, w_ref, upb_ref, out_ref, dnm_ref, dup_ref, ddown_ref, dupb_ref, nmt_ref, gmt_ref, act_ref, gp_ref
):
    step = pl.program_id(0)

    @pl.when(step == 0)
    def _():
        nmt_ref[...] = nm_ref[...].T
        gmt_ref[...] = gm_ref[...].T
        out_ref[...] = jnp.zeros(out_ref.shape, F32)
        dnm_ref[...] = jnp.zeros(dnm_ref.shape, F32)

    width = w_ref.shape[-1]
    up = w_ref[:, :size].reshape(split * size, width)
    down = w_ref[:, size : 2 * size].reshape(split * size, width)
    for r in range(0, nm_ref.shape[0], block):
        at = slice(r, r + block)
        pre = dg(nm_ref[at], up, 1, 0) + upb_ref[...]
        sq = pre * pre
        th = jnp.tanh(GELU_C * (pre + 0.044715 * sq * pre))
        half = 0.5 * (1.0 + th)
        act = (pre * half).astype(BF)
        slope = half + 0.5 * pre * (1.0 - th * th) * (GELU_C + (3.0 * 0.044715 * GELU_C) * sq)
        gp = (dg(gm_ref[at], down, 1, 1) * slope).astype(BF)
        act_ref[at] = act
        gp_ref[at] = gp
        out_ref[at] += dg(act, down, 1, 0)
        dnm_ref[at] += dg(gp, up, 1, 1)
    dup_ref[...] = dg(nmt_ref[...], gp_ref[...], 1, 0).astype(BF).reshape(split, size, width)
    ddown_ref[...] = dg(gmt_ref[...], act_ref[...], 1, 0).astype(BF).reshape(split, size, width)
    dupb_ref[...] = jnp.sum(gp_ref[...].astype(F32), axis=0, keepdims=True)


def mlp(nm, gm, weights, up_bias, size, block=256):
    rows, width = nm.shape
    split, n, deep, _ = weights.shape
    f = split * size
    squeezed = pl.Squeezed()
    const = pl.BlockSpec((rows, width), lambda i: (0, 0))
    hidden = n * f
    return pl.pallas_call(
        functools.partial(mlp_kernel, split, size, block),
        grid=(n,),
        in_specs=[
            const,
            const,
            pl.BlockSpec((split, squeezed, deep, width), lambda i: (0, i, 0, 0)),
            pl.BlockSpec((1, f), lambda i: (0, i)),
        ],
        out_specs=[
            const,
            const,
            pl.BlockSpec((split, squeezed, size, width), lambda i: (0, i, 0, 0)),
            pl.BlockSpec((split, squeezed, size, width), lambda i: (0, i, 0, 0)),
            pl.BlockSpec((1, f), lambda i: (0, i)),
        ],
        out_shape=[
            jax.ShapeDtypeStruct((rows, width), F32),
            jax.ShapeDtypeStruct((rows, width), F32),
            jax.ShapeDtypeStruct((split, n, size, width), BF),
            jax.ShapeDtypeStruct((split, n, size, width), BF),
            jax.ShapeDtypeStruct((1, hidden), F32),
        ],
        scratch_shapes=[pltpu.VMEM((width, rows), BF)] * 2 + [pltpu.VMEM((rows, f), BF)] * 2,
        compiler_params=pltpu.CompilerParams(vmem_limit_bytes=60 * 2**20),
        cost_estimate=pl.CostEstimate(
            flops=12 * rows * width * hidden, bytes_accessed=8 * width * hidden + 12 * rows * width, transcendentals=rows * hidden
        ),
        name="mlp",
    )(nm, gm, weights, up_bias)


def shards(
    block_input,
    embedding,
    history,
    cotangent,
    first_gain,
    first_shift,
    qkv_weight,
    qkv_bias,
    out_weight,
    out_bias,
    second_gain,
    second_shift,
    up_weight,
    up_bias,
    down_weight,
    down_bias,
    depth_weights,
    prefix_length,
    history_index,
):
    rows, width = block_input.shape
    local = qkv_weight.shape[2]
    heads = local // HD
    n = lax.axis_size("tensor")
    m = lax.axis_size("dp")
    z = lax.axis_index("tensor")
    dp = lax.axis_index("dp")
    length = rows * n
    hidden = up_weight.shape[1]
    cos_t, sin_t = rotary_tables(length)

    w_t = qkv_weight.reshape(width, 3, heads, HD).transpose(2, 1, 3, 0).reshape(3 * local, width)
    b_t = qkv_bias.reshape(3, heads, HD).transpose(1, 0, 2).reshape(3 * local).astype(F32)
    def mine(shard):
        size = shard.shape[0] // m
        return lax.dynamic_slice_in_dim(shard, dp * size, size, 0)

    size, out_size = width // m, local // m
    used = 2 * size + out_size
    fill = jnp.zeros((15 - used % 16, width), BF)
    early = jnp.concatenate([mine(up_weight), mine(down_weight), mine(out_weight), up_bias[None], fill], axis=0)
    normed, qkv_t, attended, of, lse, every = attend(
        prefix_length, block_input, first_gain, first_shift, w_t, b_t, cos_t, sin_t, early, n, m
    )
    out_all = every[:, :, 2 * size : used].transpose(1, 0, 2, 3).reshape(n, heads, HD, width)
    up_bias_all = every[0, :, used, :hidden].astype(F32).reshape(1, n * hidden)

    inputs_f = block_input.astype(F32)
    attn = None
    for h in range(heads):
        piece = dg(attended[h].reshape(n * HD, rows), out_all[:, h].reshape(n * HD, width), 0, 0)
        attn = piece if attn is None else attn + piece


    middle = inputs_f + (attn + out_bias.astype(F32))
    normed_mid_f, second_pull = jax.vjp(layer_norm, middle, second_gain, second_shift)
    grad_top = cotangent.astype(F32)
    grad_block = depth_weights[4] * grad_top
    grad_branch = grad_block.astype(BF)
    if size % 16 == 0:
        mlp_weights, part = every, size
    else:
        whole = every[:, :, : 2 * size].reshape(m, n, 2, size, width)
        mlp_weights, part = whole.transpose(1, 2, 0, 3, 4).reshape(1, n, 2 * hidden, width), hidden
    mlp_out, grad_normed_mid, up_grad, down_grad, up_bias_grad = mlp(
        normed_mid_f.astype(BF), grad_branch, mlp_weights, up_bias_all, part
    )
    if size % 16 != 0:
        up_grad = up_grad.reshape(n, m, size, width).transpose(1, 0, 2, 3)
        down_grad = down_grad.reshape(n, m, size, width).transpose(1, 0, 2, 3)
    block_out = middle + (mlp_out + down_bias.astype(F32))
    slot_ids = jnp.arange(3, dtype=jnp.int32)
    pick = (history_index[:, None] == slot_ids[None, :]).astype(F32)
    slot_coef = jnp.sum(depth_weights[1:4, None] * pick, axis=0)
    embed_f = embedding.astype(F32)
    mixed = depth_weights[0] * embed_f + depth_weights[4] * block_out
    for slot_id in range(3):
        mixed = mixed + slot_coef[slot_id] * history[slot_id].astype(F32)
    dwa_output = mixed.astype(BF)
    slot_sums = jnp.stack([jnp.sum(grad_top * history[slot_id].astype(F32)) for slot_id in range(3)])
    grad_depth = jnp.concatenate(
        [
            jnp.sum(grad_top * embed_f)[None],
            jnp.sum(pick * slot_sums[None, :], axis=1),
            jnp.sum(grad_top * block_out)[None],
        ]
    )
    down_bias_grad = jnp.sum(grad_branch.astype(F32), axis=0)

    grad_middle_ln, second_gain_grad, second_shift_grad = second_pull(grad_normed_mid)
    grad_middle = grad_block + grad_middle_ln
    grad_attn = grad_middle.astype(BF)
    out_bias_grad = jnp.sum(grad_attn.astype(F32), axis=0)

    grad_send = jnp.stack(
        [dg(out_all[:, h].reshape(n * HD, width), grad_attn, 1, 1).astype(BF).reshape(n, HD, rows) for h in range(heads)],
        axis=1,
    )
    out_grad = jnp.stack(
        [dg(attended[h].reshape(n * HD, rows), grad_attn, 1, 0).astype(BF).reshape(n, HD, width) for h in range(heads)], axis=1
    )
    out_grad = out_grad.reshape(n, m, out_size, width).transpose(1, 0, 2, 3)
    grad_own, back, qkv_sum, up_sum, down_sum, out_sum, w_every = attend_back(
        prefix_length, grad_send, qkv_t, of, lse, cos_t, sin_t, normed, (up_grad, down_grad, out_grad), mine(w_t)
    )
    w_all = w_every.transpose(1, 0, 2, 3).reshape(n, heads, 3 * HD, width)
    grad_normed = None
    for h in range(heads):
        piece = dg(back[h].reshape(n * 3 * HD, rows), w_all[:, h].reshape(n * 3 * HD, width), 0, 0)
        grad_normed = piece if grad_normed is None else grad_normed + piece
    qkv_bias_grad = jnp.sum(grad_own.astype(F32), axis=(1, 3)).reshape(-1)
    first_normed, first_pull = jax.vjp(layer_norm, inputs_f, first_gain, first_shift)
    grad_input_ln, first_gain_grad, first_shift_grad = first_pull(grad_normed)
    grad_input = grad_middle + grad_input_ln

    up_grad = up_sum.reshape(width, hidden).astype(F32)
    down_grad = down_sum.reshape(width, hidden).T.astype(F32)
    out_grad = out_sum.reshape(local, width).astype(F32)
    qkv_grad = qkv_sum.reshape(heads, 3, HD, width).transpose(3, 1, 0, 2).reshape(width, 3, local).astype(F32)

    spread = jnp.zeros((n, 3 * local), F32)
    spread = lax.dynamic_update_slice_in_dim(spread, qkv_bias_grad[None], z, 0)
    (
        out_bias_grad,
        second_gain_grad,
        second_shift_grad,
        down_bias_grad,
        grad_depth,
        up_bias_grad,
        qkv_bias_grad,
        first_gain_grad,
        first_shift_grad,
    ) = total_small(
        [
            out_bias_grad,
            second_gain_grad,
            second_shift_grad,
            down_bias_grad,
            grad_depth,
            up_bias_grad[0],
            spread,
            first_gain_grad,
            first_shift_grad,
        ],
        n,
        m,
    )
    up_bias_grad = lax.dynamic_slice_in_dim(up_bias_grad, z * hidden, hidden, 0)
    qkv_bias_grad = lax.dynamic_index_in_dim(qkv_bias_grad, z, 0, keepdims=False)
    qkv_bias_grad = qkv_bias_grad.reshape(heads, 3, HD).transpose(1, 0, 2).reshape(3, local)
    return (
        dwa_output,
        grad_input,
        first_gain_grad,
        first_shift_grad,
        qkv_grad,
        qkv_bias_grad,
        out_grad,
        out_bias_grad,
        second_gain_grad,
        second_shift_grad,
        up_grad,
        up_bias_grad,
        down_grad,
        down_bias_grad,
        grad_depth,
    )


def solution(mesh):
    both = ("dp", "tensor")
    return jax.shard_map(
        shards,
        mesh=mesh,
        in_specs=(
            P(both, None),
            P(both, None),
            P(None, both, None),
            P(both, None),
            P(),
            P(),
            P(None, None, "tensor"),
            P(None, "tensor"),
            P("tensor", None),
            P(),
            P(),
            P(),
            P(None, "tensor"),
            P("tensor"),
            P("tensor", None),
            P(),
            P(),
            P("dp"),
            P(),
        ),
        out_specs=(
            P(both, None),
            P(both, None),
            P(),
            P(),
            P(None, None, "tensor"),
            P(None, "tensor"),
            P("tensor", None),
            P(),
            P(),
            P(),
            P(None, "tensor"),
            P("tensor"),
            P("tensor", None),
            P(),
            P(),
        ),
        check_vma=False,
    )
```

```python
import functools

import jax
import jax.numpy as jnp
from jax import lax
from jax.experimental import pallas as pl
from jax.experimental.pallas import tpu as pltpu
from jax.sharding import PartitionSpec as P

HD = 64
NEG = -1e30
LOG2E = 1.4426950408889634
F32 = jnp.float32
BF = jnp.bfloat16


def dg(a, b, ca, cb):
    return lax.dot_general(a, b, (((ca,), (cb,)), ((), ())), preferred_element_type=F32)


def split_query(q):
    scaled = q.astype(F32) * (LOG2E * HD**-0.5)
    high = scaled.astype(BF)
    low = (scaled - high.astype(F32)).astype(BF)
    return jnp.concatenate([high, low], axis=0)


def visible(key_start, query_start, keys, queries, prefix):
    key_pos = key_start + lax.broadcasted_iota(jnp.int32, (keys, queries), 0)
    query_pos = query_start + lax.broadcasted_iota(jnp.int32, (1, queries), 1)
    return key_pos <= jnp.maximum(query_pos, prefix - 1)


def remote(src, dst, send, recv, peer):
    return pltpu.make_async_remote_copy(
        src_ref=src,
        dst_ref=dst,
        send_sem=send,
        recv_sem=recv,
        device_id=peer,
        device_id_type=pl.DeviceIdType.MESH,
    )


def greet(axis_counts):
    barrier = pltpu.get_barrier_semaphore()
    total = 0
    for axis, count in axis_counts:
        me = lax.axis_index(axis)
        for k in range(1, count):
            pl.semaphore_signal(
                barrier, inc=1, device_id={axis: lax.rem(me + k, count)}, device_id_type=pl.DeviceIdType.MESH
            )
        total += count - 1
    pl.semaphore_wait(barrier, total)


def gatherer(n, m, src, dst, line_send, line_recv, plane_send, plane_recv, own):
    z = lax.axis_index("tensor")
    dp = lax.axis_index("dp")

    def keep():
        return pltpu.make_async_copy(src, dst.at[dp, z], own.at[0])

    def line(k, t):
        return remote(src, dst.at[dp, t], line_send.at[k - 1], line_recv.at[t], {"tensor": lax.rem(z + k, n)})

    def plane(kk, k, d):
        t = lax.rem(z + kk, n)
        start = src if kk == 0 else dst.at[dp, t]
        peer = lax.rem(dp + k, m)
        return remote(start, dst.at[d, t], plane_send.at[kk, k - 1], plane_recv.at[t, d], {"dp": peer})

    def start():
        keep().start()
        for k in range(1, n):
            line(k, z).start()
        for k in range(1, m):
            plane(0, k, dp).start()

    def forward():
        for kk in range(1, n):
            line(kk, lax.rem(z + kk, n)).wait_recv()
            for k in range(1, m):
                plane(kk, k, dp).start()

    def finish():
        keep().wait()
        for k in range(1, n):
            line(k, z).wait_send()
        for kk in range(n):
            for k in range(1, m):
                copy = plane(kk, k, lax.rem(dp + k, m))
                copy.wait_send()
                copy.wait_recv()

    return start, forward, finish


def gather_sems(n, m):
    dma = pltpu.SemaphoreType.DMA
    return [dma((n - 1,)), dma((n,)), dma((n, m - 1)), dma((n, m)), dma((1,))]


def fwd_kernel(
    n, m, heads, rows, bk, sub,
    pref_ref, x_ref, gain_ref, shift_ref, w_ref, b_ref, cos_ref, sin_ref, shard_ref,
    normed_ref, qkv_ref, att_ref, of_ref, lse_ref, every_ref,
    q2_ref, k2_ref, v2_ref, m_ref, acc_ref, ob_ref, rs, rr, ls, lr, os_sem, or_sem, oo_sem, *gather,
):
    z = lax.axis_index("tensor")
    per = rows // bk
    prefix_chunks = -(-(n * rows // 2) // rows)
    greet([("tensor", n), ("dp", m)])
    gather_start, gather_forward, gather_finish = gatherer(n, m, shard_ref, every_ref, *gather)
    gather_start()
    prefix = pref_ref[0]

    def to_right(s):
        c = z - (s - 1)
        return remote(normed_ref.at[c], normed_ref.at[c], rs.at[s - 1], rr.at[s - 1], {"tensor": z + 1})

    def to_left(s):
        c = z + (s - 1)
        return remote(normed_ref.at[c], normed_ref.at[c], ls.at[s - 1], lr.at[s - 1], {"tensor": z - 1})

    def from_left(s):
        c = z - s
        return remote(normed_ref.at[c], normed_ref.at[c], rs.at[s - 1], rr.at[s - 1], {"tensor": z - 1})

    def from_right(s):
        c = z + s
        return remote(normed_ref.at[c], normed_ref.at[c], ls.at[s - 1], lr.at[s - 1], {"tensor": z + 1})

    def has_right(s):
        return (z + 1 < n) & (z - (s - 1) >= 0)

    def has_left(s):
        return (z >= 1) & (z + (s - 1) < n)

    for o in range(0, rows, bk):
        x = x_ref[o : o + bk].astype(F32)
        normed_ref[z, o : o + bk] = layer_norm(x, gain_ref[...], shift_ref[...]).astype(BF)

    @pl.when(has_right(1))
    def _():
        to_right(1).start()

    @pl.when(has_left(1))
    def _():
        to_left(1).start()

    m_ref[...] = jnp.full(m_ref.shape, NEG, F32)
    acc_ref[...] = jnp.zeros(acc_ref.shape, F32)
    first = lax.broadcasted_iota(jnp.int32, (16, bk), 0) == 0
    for h in range(heads):
        for c in range(n * per):
            v2_ref[h, c, HD : HD + 16, :] = jnp.where(first, 1.0, 0.0).astype(BF)

    def att_remote(h, i):
        return remote(ob_ref.at[h, i], att_ref.at[h, z], os_sem.at[h, i], or_sem.at[h, z], {"tensor": i})

    def att_own(h):
        return pltpu.make_async_copy(ob_ref.at[h, z], att_ref.at[h, z], oo_sem.at[h])

    def enter(c):
        for o in range(0, rows, bk):
            at = pl.ds(pl.multiple_of(c * rows + o, bk), bk)
            cos, sin = cos_ref[:, at], sin_ref[:, at]
            proj = dg(w_ref[...], normed_ref[c, o : o + bk, :], 1, 1) + b_ref[...]
            for h in range(heads):
                r0 = h * 3 * HD
                parts = []
                for part in range(2):
                    u = proj[r0 + part * HD : r0 + (part + 1) * HD]
                    f, b = u[: HD // 2], u[HD // 2 :]
                    parts.append(jnp.concatenate([f * cos - b * sin, b * cos + f * sin], axis=0))
                q = parts[0].astype(BF)
                v = proj[r0 + 2 * HD : r0 + 3 * HD].astype(BF)
                qkv_ref[h, c, 0, :, o : o + bk] = q
                qkv_ref[h, c, 1, :, o : o + bk] = parts[1].astype(BF)
                qkv_ref[h, c, 2, :, o : o + bk] = v
                q2_ref[h, c, :, o : o + bk] = split_query(q)
                kt = parts[1].T.astype(BF)
                k2_ref[h, c * per + o // bk] = jnp.concatenate([kt, kt], axis=1)
                v2_ref[h, c * per + o // bk, 0:HD, :] = v

    def pair(q, k, masked):
        for h in range(heads):
            for b in range(per):
                kj, vj = k2_ref[h, k * per + b], v2_ref[h, k * per + b]
                for s0 in range(0, rows, sub):
                    sl = slice(s0, s0 + sub)
                    s = dg(kj, q2_ref[h, q, :, sl], 1, 0)
                    if masked:
                        s = jnp.where(visible(k * rows + b * bk, q * rows + s0, bk, sub, prefix), s, NEG)
                    m = m_ref[h, q, :, sl]
                    mn = jnp.maximum(m, jnp.max(s, axis=0, keepdims=True))
                    p = jnp.exp2(s - mn).astype(BF)
                    scale = jnp.exp2(m - mn)
                    m_ref[h, q, :, sl] = mn
                    acc_ref[h, q, :, sl] = acc_ref[h, q, :, sl] * scale + dg(vj, p, 1, 0)

    def finish(q):
        for h in range(heads):
            total = acc_ref[h, q, HD : HD + 1, :]
            out = acc_ref[h, q, 0:HD, :] / total
            of_ref[h, q] = out
            lse_ref[h, q] = m_ref[h, q] + jnp.log2(total)
            ob_ref[h, q] = out.astype(BF)

            @pl.when(z != q)
            def _(h=h):
                att_remote(h, q).start()

            @pl.when(z == q)
            def _(h=h):
                att_own(h).start()

    def relay(s):
        @pl.when((s < n) & (z - s >= 0))
        def _():
            from_left(s).wait_recv()

        @pl.when((s + 1 < n) & has_right(s + 1))
        def _():
            to_right(s + 1).start()

        @pl.when((s < n) & (z + s < n))
        def _():
            from_right(s).wait_recv()

        @pl.when((s + 1 < n) & has_left(s + 1))
        def _():
            to_left(s + 1).start()

    def event(e, carry):
        s = (e + 1) // 2
        low = e % 2 == 1
        high = (e % 2 == 0) & (e > 0)

        @pl.when(e == 1)
        def _():
            relay(1)
            gather_forward()

        @pl.when(high & (z + s >= n))
        def _():
            relay(s + 1)

        c = jnp.where(low, z - s, z + s)
        bottom = jnp.maximum(z - s, 0)
        start = jnp.where(low, c + 1, jnp.where(high, bottom, c))
        stop = jnp.where(low, jnp.minimum(n, z + s), c)

        @pl.when((c >= 0) & (c < n))
        def _():
            enter(c)
            all_low = low & (c == 0)

            def full_pair(a, t):
                pair(jnp.maximum(a, c), jnp.minimum(a, c), False)

                @pl.when(all_low)
                def _():
                    finish(a)

                return t

            lax.fori_loop(start, stop, full_pair, 0)

            @pl.when(high)
            def _():
                relay(s + 1)

            def masked_pair(a, t):
                pair(jnp.minimum(a, c), jnp.maximum(a, c), True)
                return t

            inner = c < prefix_chunks
            lax.fori_loop(
                jnp.where(inner & high, start, c),
                jnp.where(inner & low, jnp.minimum(stop, prefix_chunks), c + 1),
                masked_pair,
                0,
            )
            ready = all_low | ((bottom == 0) & high & (c >= prefix_chunks - 1))
            from_q = jnp.where(c == prefix_chunks - 1, 0, c)

            def finish_one(q, t):
                finish(q)
                return t

            lax.fori_loop(from_q, jnp.where(ready, c + 1, from_q), finish_one, 0)

        return carry

    lax.fori_loop(0, 2 * n - 1, event, 0)
    gather_finish()
    for s in range(1, n):

        @pl.when(has_right(s))
        def _(s=s):
            to_right(s).wait_send()

        @pl.when(has_left(s))
        def _(s=s):
            to_left(s).wait_send()

    for h in range(heads):
        att_own(h).wait()
        for k in range(1, n):
            d = lax.rem(z + k, n)
            att_remote(h, d).wait_send()
            remote(ob_ref.at[h, d], att_ref.at[h, d], os_sem.at[h, d], or_sem.at[h, d], {"tensor": d}).wait_recv()


def attend(prefix, x, gain, shift, w, bias, cos_t, sin_t, shard, n, m, bk=1024, sub=1024):
    rows, width = x.shape
    heads = w.shape[0] // (3 * HD)
    length = n * rows
    vmem = pl.BlockSpec(memory_space=pltpu.VMEM)
    dma = pltpu.SemaphoreType.DMA
    return pl.pallas_call(
        functools.partial(fwd_kernel, n, m, heads, rows, bk, sub),
        in_specs=[pl.BlockSpec(memory_space=pltpu.SMEM)] + [vmem] * 7 + [pl.BlockSpec(memory_space=pl.ANY)],
        out_specs=[vmem] * 5 + [pl.BlockSpec(memory_space=pl.ANY)],
        out_shape=[
            jax.ShapeDtypeStruct((n, rows, width), BF),
            jax.ShapeDtypeStruct((heads, n, 3, HD, rows), BF),
            jax.ShapeDtypeStruct((heads, n, HD, rows), BF),
            jax.ShapeDtypeStruct((heads, n, HD, rows), F32),
            jax.ShapeDtypeStruct((heads, n, 1, rows), F32),
            jax.ShapeDtypeStruct((m, n) + shard.shape, BF),
        ],
        scratch_shapes=[
            pltpu.VMEM((heads, n, 2 * HD, rows), BF),
            pltpu.VMEM((heads, length // bk, bk, 2 * HD), BF),
            pltpu.VMEM((heads, length // bk, HD + 16, bk), BF),
            pltpu.VMEM((heads, n, 1, rows), F32),
            pltpu.VMEM((heads, n, HD + 16, rows), F32),
            pltpu.VMEM((heads, n, HD, rows), BF),
            dma((n - 1,)),
            dma((n - 1,)),
            dma((n - 1,)),
            dma((n - 1,)),
            dma((heads, n)),
            dma((heads, n)),
            dma((heads,)),
        ]
        + gather_sems(n, m),
        compiler_params=pltpu.CompilerParams(
            collective_id=0, has_side_effects=True, vmem_limit_bytes=60 * 2**20
        ),
        cost_estimate=pl.CostEstimate(
            flops=int(heads * 4 * 256 * length * length * 0.7),
            bytes_accessed=heads * length * HD * 20,
            transcendentals=int(heads * length * length * 0.7),
        ),
        name="attend_forward",
    )(prefix, x, gain.reshape(1, width), shift.reshape(1, width), w, bias[:, None], cos_t, sin_t, shard)


def small_kernel(n, m, x_ref, o_ref, zbuf, mid, pbuf, zs, zr, ps, pr):
    z = lax.axis_index("tensor")
    d = lax.axis_index("dp")
    greet([("tensor", n), ("dp", m)])

    def stage(axis, me, count, src, buf, send, recv):
        buf[me] = src[...]
        for k in range(1, count):
            peer = lax.rem(me + k, count)
            remote(src, buf.at[me], send.at[k - 1], recv.at[me], {axis: peer}).start()
        for k in range(1, count):
            peer = lax.rem(me + k, count)
            copy = remote(src, buf.at[peer], send.at[k - 1], recv.at[peer], {axis: peer})
            copy.wait_send()
            copy.wait_recv()
        total = buf[0]
        for k in range(1, count):
            total = total + buf[k]
        return total

    mid[...] = stage("tensor", z, n, x_ref, zbuf, zs, zr)
    o_ref[...] = stage("dp", d, m, mid, pbuf, ps, pr)


def total_small(vectors, n, m):
    sizes = [v.size for v in vectors]
    flat = jnp.concatenate([v.reshape(-1) for v in vectors])
    flat = jnp.pad(flat, (0, -flat.size % 1024)).reshape(-1, 128)
    vmem = pl.BlockSpec(memory_space=pltpu.VMEM)
    dma = pltpu.SemaphoreType.DMA
    summed = pl.pallas_call(
        functools.partial(small_kernel, n, m),
        in_specs=[vmem],
        out_specs=vmem,
        out_shape=jax.ShapeDtypeStruct(flat.shape, F32),
        scratch_shapes=[
            pltpu.VMEM((n,) + flat.shape, F32),
            pltpu.VMEM(flat.shape, F32),
            pltpu.VMEM((m,) + flat.shape, F32),
            dma((n - 1,)),
            dma((n,)),
            dma((m - 1,)),
            dma((m,)),
        ],
        compiler_params=pltpu.CompilerParams(collective_id=1, has_side_effects=True),
        name="total_small",
    )(flat).reshape(-1)
    out, at = [], 0
    for v, size in zip(vectors, sizes):
        out.append(summed[at : at + size].reshape(v.shape))
        at += size
    return out


def unrotate(front, back, c, s):
    return front * c + back * s, back * c - front * s


def bit_orders(m):
    bits = list(range(m.bit_length() - 1))
    return [bits, bits[:1] + bits[:0:-1], bits]


def bwd_kernel(n, heads, rows, bk, sub, m, *refs):
    steps = m.bit_length() - 1
    (pref_ref, send_ref, qkv_ref, of_ref, lse_ref, cos_ref, sin_ref, normed_ref), refs = refs[:8], refs[8:]
    parts, (shard_ref,), refs = refs[:3], refs[3:4], refs[4:]
    (g_ref, back_ref), refs = refs[:2], refs[2:]
    (rw_ref,), results, (every_ref,), refs = refs[:1], refs[1:4], refs[4:5], refs[5:]
    (do_ref, q2_ref, qn_ref, don_ref, dd_ref, dq_ref, dk_ref, dv_ref), refs = refs[:8], refs[8:]
    (wv_ref, ws_ref, wb_ref, wf_ref), refs = refs[:4], refs[4:]
    tracks = []
    for tag, order in enumerate(bit_orders(m)):
        held, came, (zbuf, fin) = refs[0], refs[1 : steps + 1], refs[steps + 1 : steps + 3]
        refs = refs[steps + 3 :]
        tracks.append((tag, order, parts[tag], held, came, zbuf, fin, results[tag]))
    (own_sem, s_sem, r_sem, kvs, kvr, qs, qr, kvo, qo), refs = refs[:9], refs[9:]
    (hs, hr, ho, p2s, p2r, p2o, p3s, p3r, p3o, w1s, w1r, w1o, w2s, w2r, w2o), gather = refs[:15], refs[15:]
    z = lax.axis_index("tensor")
    dp = lax.axis_index("dp")
    length = n * rows
    per = rows // bk
    prefix_chunks = -(-(length // 2) // rows)
    greet([("tensor", n), ("dp", m)])

    gather_start, gather_forward, gather_finish = gatherer(n, m, shard_ref, every_ref, *gather)
    def spread(axis, me, count, pick, dst, send, recv, own, tag):
        pltpu.make_async_copy(pick(me), dst.at[me], own.at[tag]).start()
        for k in range(1, count):
            d = lax.rem(me + k, count)
            remote(pick(d), dst.at[me], send.at[tag, k - 1], recv.at[tag, me], {axis: d}).start()

    def arrived(axis, me, count, pick, dst, recv, send, own, tag):
        pltpu.make_async_copy(pick(me), dst.at[me], own.at[tag]).wait()
        for k in range(1, count):
            d = lax.rem(me + k, count)
            copy = remote(pick(d), dst.at[d], send.at[tag, k - 1], recv.at[tag, d], {axis: d})
            copy.wait_send()
            copy.wait_recv()

    def own_bit(b):
        return (dp // 2**b) % 2

    def slice_of(order, bit, j):
        index = bit * 2 ** order[0]
        for place, b in enumerate(order[1:]):
            index = index + ((j >> place) & 1) * 2**b
        return index

    def place(order, i, last):
        at = last * 2 ** (i - 1)
        for k in range(1, i):
            at = at + own_bit(order[k]) * 2 ** (k - 1)
        return at

    def halve_copies(i):
        for tag, order, part, held, came, zbuf, fin, res in tracks:
            bit = own_bit(order[i])
            partner = dp + (1 - 2 * bit) * 2 ** order[i]
            for j in range(m >> (i + 1)):
                src = part.at[slice_of(order, 1 - bit, j)] if i == 0 else held.at[place(order, i, 1 - bit) + 2**i * j]
                yield tag, j, bit, order, remote(src, came[i].at[j], hs.at[tag, i, j], hr.at[tag, i, j], {"dp": partner})

    def kept_copies():
        for tag, order, part, held, came, zbuf, fin, res in tracks:
            for j in range(m // 2):
                src = part.at[slice_of(order, own_bit(order[0]), j)]
                yield pltpu.make_async_copy(src, held.at[j], ho.at[tag, j])

    def halve_start(i):
        for _, _, _, _, copy in halve_copies(i):
            copy.start()

    def halve_sum(i):
        if i == 0:
            for copy in kept_copies():
                copy.wait()
        for tag, j, bit, order, copy in halve_copies(i):
            copy.wait_send()
            copy.wait_recv()
            held, came = tracks[tag][3], tracks[tag][4]
            at = j if i == 0 else place(order, i, bit) + 2**i * j
            for t in range(n):
                held[at, t] = (held[at, t].astype(F32) + came[i][j, t].astype(F32)).astype(BF)

    def line_start():
        for tag, order, part, held, came, zbuf, fin, res in tracks:
            spread("tensor", z, n, lambda d, held=held, order=order: held.at[place(order, steps - 1, own_bit(order[-1])), d], zbuf, p2s, p2r, p2o, tag)

    def line_sum():
        for tag, order, part, held, came, zbuf, fin, res in tracks:
            arrived("tensor", z, n, lambda d, held=held, order=order: held.at[place(order, steps - 1, own_bit(order[-1])), d], zbuf, p2r, p2s, p2o, tag)
            total = zbuf[0].astype(F32)
            for k in range(1, n):
                total = total + zbuf[k].astype(F32)
            fin[...] = total.astype(BF)
            spread("dp", dp, m, lambda d, fin=fin: fin, res, p3s, p3r, p3o, tag)

    def after_last():
        for tag, order, part, held, came, zbuf, fin, res in tracks:
            arrived("dp", dp, m, lambda d, fin=fin: fin, res, p3r, p3s, p3o, tag)

    for copy in kept_copies():
        copy.start()
    halve_start(0)
    points = (0, 3, 4) if steps == 3 else tuple(range(steps))

    def at_point(e):
        for i, point in enumerate(points):

            @pl.when(e == point)
            def _(i=i):
                halve_sum(i)
                if i + 1 < steps:
                    halve_start(i + 1)
                else:
                    line_start()

        @pl.when(e == 1)
        def _():
            gather_start()

        @pl.when(e == n + 1)
        def _():
            gather_forward()

        @pl.when(e == 2 * n - 1)
        def _():
            line_sum()

    def weight_start(h):
        grad = dg(g_ref[h, 0], normed_ref[0], 1, 0)
        for t in range(1, n):
            grad = grad + dg(g_ref[h, t], normed_ref[t], 1, 0)
        wv_ref[...] = grad
        q = 3 * HD // m
        for i in range(m):
            ws_ref[h, i] = wv_ref[i * q : (i + 1) * q].astype(BF)
        spread("dp", dp, m, lambda d: ws_ref.at[h, d], wb_ref.at[h], w1s, w1r, w1o, h)

    def weight_sum(h):
        arrived("dp", dp, m, lambda d: ws_ref.at[h, d], wb_ref.at[h], w1r, w1s, w1o, h)
        total = wb_ref[h, 0].astype(F32)
        for k in range(1, m):
            total = total + wb_ref[h, k].astype(F32)
        wf_ref[h] = total.astype(BF)
        spread("dp", dp, m, lambda d: wf_ref.at[h], rw_ref.at[h], w2s, w2r, w2o, h)

    def weight_end(h):
        arrived("dp", dp, m, lambda d: wf_ref.at[h], rw_ref.at[h], w2r, w2s, w2o, h)

    def do_copy(h, k):
        d = lax.rem(z + k, n)
        return remote(send_ref.at[d, h], do_ref.at[h, z], s_sem.at[h, k - 1], r_sem.at[h, k - 1], {"tensor": d})

    def own_copy(h):
        return pltpu.make_async_copy(send_ref.at[z, h], do_ref.at[h, z], own_sem.at[h])

    def do_start(h):
        own_copy(h).start()
        for k in range(1, n):
            do_copy(h, k).start()

    do_start(0)
    prefix = pref_ref[0]
    kv_rows, q_rows = pl.ds(HD, 2 * HD), pl.ds(0, HD)

    def piece(h, t, part, source, send, recv):
        return remote(
            g_ref.at[h, t, part], back_ref.at[h, source, part], send.at[h, t], recv.at[h, source], {"tensor": t}
        )

    def own_piece(h, part, sem):
        return pltpu.make_async_copy(g_ref.at[h, z, part], back_ref.at[h, z, part], sem.at[h])

    def hand_out(h, t, part, send, recv, own):
        @pl.when(z != t)
        def _():
            piece(h, t, part, z, send, recv).start()

        @pl.when(z == t)
        def _():
            own_piece(h, part, own).start()

    def head(h, carry):
        own_copy(h).wait()
        for k in range(1, n):
            do_copy(h, k).wait_recv()

        @pl.when(h + 1 < heads)
        def _():
            do_start(h + 1)

        for c in range(n):
            q = qkv_ref[h, c, 0]
            q2_ref[c] = split_query(q)
            qn_ref[c] = q.astype(F32).T.astype(BF)
            dof = do_ref[h, c].astype(F32)
            don_ref[c] = dof.T.astype(BF)
            inner = jnp.sum(dof * of_ref[h, c], axis=0, keepdims=True)
            dd_ref[c] = jnp.concatenate([inner, lse_ref[h, c]], axis=0)
            dq_ref[c] = jnp.zeros((HD, rows), F32)

        def keys(turn, c1):
            t = lax.rem(z + 1 + turn, n)
            for o in range(0, rows, bk):
                kt = qkv_ref[h, t, 1, :, o : o + bk]
                kn = kt.astype(F32).T.astype(BF)
                k2 = jnp.concatenate([kn, kn], axis=1)
                vn = qkv_ref[h, t, 2, :, o : o + bk].astype(F32).T.astype(BF)
                dk_ref[...] = jnp.zeros(dk_ref.shape, F32)
                dv_ref[...] = jnp.zeros(dv_ref.shape, F32)

                def block(i, masked, o=o, kt=kt, k2=k2, vn=vn):
                    for s0 in range(0, rows, sub):
                        sl = slice(s0, s0 + sub)
                        p = jnp.exp2(dg(k2, q2_ref[i, :, sl], 1, 0) - dd_ref[i, 1:2, sl])
                        if masked:
                            p = jnp.where(visible(t * rows + o, i * rows + s0, bk, sub, prefix), p, 0.0)
                        dp = dg(vn, do_ref[h, i, :, sl], 1, 0)
                        dv_ref[...] += dg(p.astype(BF), don_ref[i, sl, :], 1, 0)
                        ds = (p * (dp - dd_ref[i, 0:1, sl])).astype(BF)
                        dk_ref[...] += dg(ds, qn_ref[i, sl, :], 1, 0)
                        dq_ref[i, :, sl] += dg(kt, ds, 1, 0)

                def masked_block(i, c2, block=block):
                    block(i, True)
                    return c2

                def full_block(i, c2, block=block):
                    block(i, False)
                    return c2

                lax.fori_loop(jnp.where(t < prefix_chunks, 0, t), t + 1, masked_block, 0)
                lax.fori_loop(t + 1, n, full_block, 0)
                dk = dk_ref[...].T * HD**-0.5
                at = pl.ds(pl.multiple_of(t * rows + o, bk), bk)
                a, b = unrotate(dk[: HD // 2], dk[HD // 2 :], cos_ref[:, at], sin_ref[:, at])
                g_ref[h, t, HD : HD + HD // 2, o : o + bk] = a.astype(BF)
                g_ref[h, t, HD + HD // 2 : 2 * HD, o : o + bk] = b.astype(BF)
                g_ref[h, t, 2 * HD : 3 * HD, o : o + bk] = dv_ref[...].T.astype(BF)
            hand_out(h, t, kv_rows, kvs, kvr, kvo)
            at_point(h * n + turn)
            return c1

        lax.fori_loop(0, n, keys, 0)
        for c in range(n):
            x = dq_ref[c] * HD**-0.5
            at = slice(c * rows, (c + 1) * rows)
            a, b = unrotate(x[: HD // 2], x[HD // 2 :], cos_ref[:, at], sin_ref[:, at])
            g_ref[h, c, : HD // 2, :] = a.astype(BF)
            g_ref[h, c, HD // 2 : HD, :] = b.astype(BF)
            hand_out(h, c, q_rows, qs, qr, qo)
        weight_start(h)

        @pl.when(h > 0)
        def _():
            weight_sum(h - 1)

        return carry

    lax.fori_loop(0, heads, head, 0)
    weight_sum(heads - 1)
    gather_finish()
    after_last()
    for h in range(heads):
        weight_end(h)
    for h in range(heads):
        own_piece(h, kv_rows, kvo).wait()
        own_piece(h, q_rows, qo).wait()
        for k in range(1, n):
            do_copy(h, k).wait_send()
            d = lax.rem(z + k, n)
            for part, send, recv in ((kv_rows, kvs, kvr), (q_rows, qs, qr)):
                copy = piece(h, d, part, d, send, recv)
                copy.wait_send()
                copy.wait_recv()


def attend_back(prefix, send, qkv, of, lse, cos_t, sin_t, normed, parts, shard, bk=512, sub=256):
    n, heads, _, rows = send.shape
    m, width = parts[0].shape[0], parts[0].shape[-1]
    steps = m.bit_length() - 1
    size_w = 3 * HD // m
    length = n * rows
    vmem = pl.BlockSpec(memory_space=pltpu.VMEM)
    dma = pltpu.SemaphoreType.DMA
    buffers = []
    for part in parts:
        size = part.shape[2]
        for count in [m // 2] + [m >> (i + 1) for i in range(steps)]:
            buffers.append(pltpu.VMEM((count, n, size, width), BF))
        buffers += [pltpu.VMEM((n, size, width), BF), pltpu.VMEM((size, width), BF)]
    return pl.pallas_call(
        functools.partial(bwd_kernel, n, heads, rows, bk, sub, m),
        in_specs=[pl.BlockSpec(memory_space=pltpu.SMEM)] + [vmem] * 7 + [pl.BlockSpec(memory_space=pl.ANY)] * 4,
        out_specs=[vmem] * 6 + [pl.BlockSpec(memory_space=pl.ANY)],
        out_shape=[
            jax.ShapeDtypeStruct((heads, n, 3 * HD, rows), BF),
            jax.ShapeDtypeStruct((heads, n, 3 * HD, rows), BF),
            jax.ShapeDtypeStruct((heads, m, size_w, width), BF),
        ]
        + [jax.ShapeDtypeStruct((m, part.shape[2], width), BF) for part in parts]
        + [jax.ShapeDtypeStruct((m, n) + shard.shape, BF)],
        scratch_shapes=[
            pltpu.VMEM((heads, n, HD, rows), BF),
            pltpu.VMEM((n, 2 * HD, rows), BF),
            pltpu.VMEM((n, rows, HD), BF),
            pltpu.VMEM((n, rows, HD), BF),
            pltpu.VMEM((n, 2, rows), F32),
            pltpu.VMEM((n, HD, rows), F32),
            pltpu.VMEM((bk, HD), F32),
            pltpu.VMEM((bk, HD), F32),
            pltpu.VMEM((3 * HD, width), F32),
            pltpu.VMEM((heads, m, size_w, width), BF),
            pltpu.VMEM((heads, m, size_w, width), BF),
            pltpu.VMEM((heads, size_w, width), BF),
        ]
        + buffers
        + [
            dma((heads,)),
            dma((heads, n - 1)),
            dma((heads, n - 1)),
            dma((heads, n)),
            dma((heads, n)),
            dma((heads, n)),
            dma((heads, n)),
            dma((heads,)),
            dma((heads,)),
            dma((3, steps, m // 2)),
            dma((3, steps, m // 2)),
            dma((3, m // 2)),
            dma((3, n - 1)),
            dma((3, n)),
            dma((3,)),
            dma((3, m - 1)),
            dma((3, m)),
            dma((3,)),
            dma((heads, m - 1)),
            dma((heads, m)),
            dma((heads,)),
            dma((heads, m - 1)),
            dma((heads, m)),
            dma((heads,)),
        ]
        + gather_sems(n, m),
        compiler_params=pltpu.CompilerParams(
            collective_id=2, has_side_effects=True, vmem_limit_bytes=63 * 2**20
        ),
        cost_estimate=pl.CostEstimate(
            flops=int(heads * 10 * 256 * length * length * 0.7),
            bytes_accessed=heads * length * HD * 20,
            transcendentals=int(heads * length * length * 0.7),
        ),
        name="attend_backward",
    )(prefix, send, qkv, of, lse, cos_t, sin_t, normed, *parts, shard)


EPS = 1e-05
ROPE_BASE = 10000.0
GELU_C = 0.7978845608028654


def layer_norm(values, norm_gain, norm_shift):
    center = values - jnp.mean(values, axis=-1, keepdims=True)
    spread = jnp.mean(center * center, axis=-1, keepdims=True)
    return center * lax.rsqrt(spread + EPS) * norm_gain + norm_shift


def rotary_tables(length):
    half_dim = HD // 2
    frequency = ROPE_BASE ** (-jnp.arange(half_dim, dtype=jnp.float32) / half_dim)
    angles = frequency[:, None] * jnp.arange(length, dtype=jnp.float32)[None, :]
    return (jnp.cos(angles), jnp.sin(angles))


def mlp_kernel(
    split, size, block, nm_ref, gm_ref, w_ref, upb_ref, out_ref, dnm_ref, dup_ref, ddown_ref, dupb_ref, nmt_ref, gmt_ref, act_ref, gp_ref
):
    step = pl.program_id(0)

    @pl.when(step == 0)
    def _():
        nmt_ref[...] = nm_ref[...].T
        gmt_ref[...] = gm_ref[...].T
        out_ref[...] = jnp.zeros(out_ref.shape, F32)
        dnm_ref[...] = jnp.zeros(dnm_ref.shape, F32)

    width = w_ref.shape[-1]
    up = w_ref[:, :size].reshape(split * size, width)
    down = w_ref[:, size : 2 * size].reshape(split * size, width)
    for r in range(0, nm_ref.shape[0], block):
        at = slice(r, r + block)
        pre = dg(nm_ref[at], up, 1, 0) + upb_ref[...]
        sq = pre * pre
        th = jnp.tanh(GELU_C * (pre + 0.044715 * sq * pre))
        half = 0.5 * (1.0 + th)
        act = (pre * half).astype(BF)
        slope = half + 0.5 * pre * (1.0 - th * th) * (GELU_C + (3.0 * 0.044715 * GELU_C) * sq)
        gp = (dg(gm_ref[at], down, 1, 1) * slope).astype(BF)
        act_ref[at] = act
        gp_ref[at] = gp
        out_ref[at] += dg(act, down, 1, 0)
        dnm_ref[at] += dg(gp, up, 1, 1)
    dup_ref[...] = dg(nmt_ref[...], gp_ref[...], 1, 0).astype(BF).reshape(split, size, width)
    ddown_ref[...] = dg(gmt_ref[...], act_ref[...], 1, 0).astype(BF).reshape(split, size, width)
    dupb_ref[...] = jnp.sum(gp_ref[...].astype(F32), axis=0, keepdims=True)


def mlp(nm, gm, weights, up_bias, size, block=256):
    rows, width = nm.shape
    split, n, deep, _ = weights.shape
    f = split * size
    squeezed = pl.Squeezed()
    const = pl.BlockSpec((rows, width), lambda i: (0, 0))
    hidden = n * f
    return pl.pallas_call(
        functools.partial(mlp_kernel, split, size, block),
        grid=(n,),
        in_specs=[
            const,
            const,
            pl.BlockSpec((split, squeezed, deep, width), lambda i: (0, i, 0, 0)),
            pl.BlockSpec((1, f), lambda i: (0, i)),
        ],
        out_specs=[
            const,
            const,
            pl.BlockSpec((split, squeezed, size, width), lambda i: (0, i, 0, 0)),
            pl.BlockSpec((split, squeezed, size, width), lambda i: (0, i, 0, 0)),
            pl.BlockSpec((1, f), lambda i: (0, i)),
        ],
        out_shape=[
            jax.ShapeDtypeStruct((rows, width), F32),
            jax.ShapeDtypeStruct((rows, width), F32),
            jax.ShapeDtypeStruct((split, n, size, width), BF),
            jax.ShapeDtypeStruct((split, n, size, width), BF),
            jax.ShapeDtypeStruct((1, hidden), F32),
        ],
        scratch_shapes=[pltpu.VMEM((width, rows), BF)] * 2 + [pltpu.VMEM((rows, f), BF)] * 2,
        compiler_params=pltpu.CompilerParams(vmem_limit_bytes=60 * 2**20),
        cost_estimate=pl.CostEstimate(
            flops=12 * rows * width * hidden, bytes_accessed=8 * width * hidden + 12 * rows * width, transcendentals=rows * hidden
        ),
        name="mlp",
    )(nm, gm, weights, up_bias)


def shards(
    block_input,
    embedding,
    history,
    cotangent,
    first_gain,
    first_shift,
    qkv_weight,
    qkv_bias,
    out_weight,
    out_bias,
    second_gain,
    second_shift,
    up_weight,
    up_bias,
    down_weight,
    down_bias,
    depth_weights,
    prefix_length,
    history_index,
):
    rows, width = block_input.shape
    local = qkv_weight.shape[2]
    heads = local // HD
    n = lax.axis_size("tensor")
    m = lax.axis_size("dp")
    z = lax.axis_index("tensor")
    dp = lax.axis_index("dp")
    length = rows * n
    hidden = up_weight.shape[1]
    cos_t, sin_t = rotary_tables(length)

    w_t = qkv_weight.reshape(width, 3, heads, HD).transpose(2, 1, 3, 0).reshape(3 * local, width)
    b_t = qkv_bias.reshape(3, heads, HD).transpose(1, 0, 2).reshape(3 * local).astype(F32)
    def mine(shard):
        size = shard.shape[0] // m
        return lax.dynamic_slice_in_dim(shard, dp * size, size, 0)

    size, out_size = width // m, local // m
    used = 2 * size + out_size
    fill = jnp.zeros((15 - used % 16, width), BF)
    early = jnp.concatenate([mine(up_weight), mine(down_weight), mine(out_weight), up_bias[None], fill], axis=0)
    normed, qkv_t, attended, of, lse, every = attend(
        prefix_length, block_input, first_gain, first_shift, w_t, b_t, cos_t, sin_t, early, n, m
    )
    out_all = every[:, :, 2 * size : used].transpose(1, 0, 2, 3).reshape(n, heads, HD, width)
    up_bias_all = every[0, :, used, :hidden].astype(F32).reshape(1, n * hidden)

    inputs_f = block_input.astype(F32)
    attn = None
    for h in range(heads):
        piece = dg(attended[h].reshape(n * HD, rows), out_all[:, h].reshape(n * HD, width), 0, 0)
        attn = piece if attn is None else attn + piece


    middle = inputs_f + (attn + out_bias.astype(F32))
    normed_mid_f, second_pull = jax.vjp(layer_norm, middle, second_gain, second_shift)
    grad_top = cotangent.astype(F32)
    grad_block = depth_weights[4] * grad_top
    grad_branch = grad_block.astype(BF)
    if size % 16 == 0:
        mlp_weights, part = every, size
    else:
        whole = every[:, :, : 2 * size].reshape(m, n, 2, size, width)
        mlp_weights, part = whole.transpose(1, 2, 0, 3, 4).reshape(1, n, 2 * hidden, width), hidden
    mlp_out, grad_normed_mid, up_grad, down_grad, up_bias_grad = mlp(
        normed_mid_f.astype(BF), grad_branch, mlp_weights, up_bias_all, part
    )
    if size % 16 != 0:
        up_grad = up_grad.reshape(n, m, size, width).transpose(1, 0, 2, 3)
        down_grad = down_grad.reshape(n, m, size, width).transpose(1, 0, 2, 3)
    block_out = middle + (mlp_out + down_bias.astype(F32))
    slot_ids = jnp.arange(3, dtype=jnp.int32)
    pick = (history_index[:, None] == slot_ids[None, :]).astype(F32)
    slot_coef = jnp.sum(depth_weights[1:4, None] * pick, axis=0)
    embed_f = embedding.astype(F32)
    mixed = depth_weights[0] * embed_f + depth_weights[4] * block_out
    for slot_id in range(3):
        mixed = mixed + slot_coef[slot_id] * history[slot_id].astype(F32)
    dwa_output = mixed.astype(BF)
    slot_sums = jnp.stack([jnp.sum(grad_top * history[slot_id].astype(F32)) for slot_id in range(3)])
    grad_depth = jnp.concatenate(
        [
            jnp.sum(grad_top * embed_f)[None],
            jnp.sum(pick * slot_sums[None, :], axis=1),
            jnp.sum(grad_top * block_out)[None],
        ]
    )
    down_bias_grad = jnp.sum(grad_branch.astype(F32), axis=0)

    grad_middle_ln, second_gain_grad, second_shift_grad = second_pull(grad_normed_mid)
    grad_middle = grad_block + grad_middle_ln
    grad_attn = grad_middle.astype(BF)
    out_bias_grad = jnp.sum(grad_attn.astype(F32), axis=0)

    grad_send = jnp.stack(
        [dg(out_all[:, h].reshape(n * HD, width), grad_attn, 1, 1).astype(BF).reshape(n, HD, rows) for h in range(heads)],
        axis=1,
    )
    out_grad = jnp.stack(
        [dg(attended[h].reshape(n * HD, rows), grad_attn, 1, 0).astype(BF).reshape(n, HD, width) for h in range(heads)], axis=1
    )
    out_grad = out_grad.reshape(n, m, out_size, width).transpose(1, 0, 2, 3)
    grad_own, back, qkv_sum, up_sum, down_sum, out_sum, w_every = attend_back(
        prefix_length, grad_send, qkv_t, of, lse, cos_t, sin_t, normed, (up_grad, down_grad, out_grad), mine(w_t)
    )
    w_all = w_every.transpose(1, 0, 2, 3).reshape(n, heads, 3 * HD, width)
    grad_normed = None
    for h in range(heads):
        piece = dg(back[h].reshape(n * 3 * HD, rows), w_all[:, h].reshape(n * 3 * HD, width), 0, 0)
        grad_normed = piece if grad_normed is None else grad_normed + piece
    qkv_bias_grad = jnp.sum(grad_own.astype(F32), axis=(1, 3)).reshape(-1)
    first_normed, first_pull = jax.vjp(layer_norm, inputs_f, first_gain, first_shift)
    grad_input_ln, first_gain_grad, first_shift_grad = first_pull(grad_normed)
    grad_input = grad_middle + grad_input_ln

    up_grad = up_sum.reshape(width, hidden).astype(F32)
    down_grad = down_sum.reshape(width, hidden).T.astype(F32)
    out_grad = out_sum.reshape(local, width).astype(F32)
    qkv_grad = qkv_sum.reshape(heads, 3, HD, width).transpose(3, 1, 0, 2).reshape(width, 3, local).astype(F32)

    spread = jnp.zeros((n, 3 * local), F32)
    spread = lax.dynamic_update_slice_in_dim(spread, qkv_bias_grad[None], z, 0)
    (
        out_bias_grad,
        second_gain_grad,
        second_shift_grad,
        down_bias_grad,
        grad_depth,
        up_bias_grad,
        qkv_bias_grad,
        first_gain_grad,
        first_shift_grad,
    ) = total_small(
        [
            out_bias_grad,
            second_gain_grad,
            second_shift_grad,
            down_bias_grad,
            grad_depth,
            up_bias_grad[0],
            spread,
            first_gain_grad,
            first_shift_grad,
        ],
        n,
        m,
    )
    up_bias_grad = lax.dynamic_slice_in_dim(up_bias_grad, z * hidden, hidden, 0)
    qkv_bias_grad = lax.dynamic_index_in_dim(qkv_bias_grad, z, 0, keepdims=False)
    qkv_bias_grad = qkv_bias_grad.reshape(heads, 3, HD).transpose(1, 0, 2).reshape(3, local)
    return (
        dwa_output,
        grad_input,
        first_gain_grad,
        first_shift_grad,
        qkv_grad,
        qkv_bias_grad,
        out_grad,
        out_bias_grad,
        second_gain_grad,
        second_shift_grad,
        up_grad,
        up_bias_grad,
        down_grad,
        down_bias_grad,
        grad_depth,
    )


def solution(mesh):
    both = ("dp", "tensor")
    return jax.shard_map(
        shards,
        mesh=mesh,
        in_specs=(
            P(both, None),
            P(both, None),
            P(None, both, None),
            P(both, None),
            P(),
            P(),
            P(None, None, "tensor"),
            P(None, "tensor"),
            P("tensor", None),
            P(),
            P(),
            P(),
            P(None, "tensor"),
            P("tensor"),
            P("tensor", None),
            P(),
            P(),
            P("dp"),
            P(),
        ),
        out_specs=(
            P(both, None),
            P(both, None),
            P(),
            P(),
            P(None, None, "tensor"),
            P(None, "tensor"),
            P("tensor", None),
            P(),
            P(),
            P(),
            P(None, "tensor"),
            P("tensor"),
            P("tensor", None),
            P(),
            P(),
        ),
        check_vma=False,
    )
```

```python
import functools

import jax
import jax.numpy as jnp
from jax import lax
from jax.experimental import pallas as pl
from jax.experimental.pallas import tpu as pltpu
from jax.sharding import PartitionSpec as P

HD = 64
NEG = -1e30
LOG2E = 1.4426950408889634
F32 = jnp.float32
BF = jnp.bfloat16


def dg(a, b, ca, cb):
    return lax.dot_general(a, b, (((ca,), (cb,)), ((), ())), preferred_element_type=F32)


def split_query(q):
    scaled = q.astype(F32) * (LOG2E * HD**-0.5)
    high = scaled.astype(BF)
    low = (scaled - high.astype(F32)).astype(BF)
    return jnp.concatenate([high, low], axis=0)


def visible(key_start, query_start, keys, queries, prefix):
    key_pos = key_start + lax.broadcasted_iota(jnp.int32, (keys, queries), 0)
    query_pos = query_start + lax.broadcasted_iota(jnp.int32, (1, queries), 1)
    return key_pos <= jnp.maximum(query_pos, prefix - 1)


def remote(src, dst, send, recv, peer):
    return pltpu.make_async_remote_copy(
        src_ref=src,
        dst_ref=dst,
        send_sem=send,
        recv_sem=recv,
        device_id=peer,
        device_id_type=pl.DeviceIdType.MESH,
    )


def greet(axis_counts):
    barrier = pltpu.get_barrier_semaphore()
    total = 0
    for axis, count in axis_counts:
        me = lax.axis_index(axis)
        for k in range(1, count):
            pl.semaphore_signal(
                barrier, inc=1, device_id={axis: lax.rem(me + k, count)}, device_id_type=pl.DeviceIdType.MESH
            )
        total += count - 1
    pl.semaphore_wait(barrier, total)


def gatherer(n, m, src, dst, line_send, line_recv, plane_send, plane_recv, own):
    z = lax.axis_index("tensor")
    dp = lax.axis_index("dp")

    def keep():
        return pltpu.make_async_copy(src, dst.at[dp, z], own.at[0])

    def line(k, t):
        return remote(src, dst.at[dp, t], line_send.at[k - 1], line_recv.at[t], {"tensor": lax.rem(z + k, n)})

    def plane(kk, k, d):
        t = lax.rem(z + kk, n)
        start = src if kk == 0 else dst.at[dp, t]
        peer = lax.rem(dp + k, m)
        return remote(start, dst.at[d, t], plane_send.at[kk, k - 1], plane_recv.at[t, d], {"dp": peer})

    def start():
        keep().start()
        for k in range(1, n):
            line(k, z).start()
        for k in range(1, m):
            plane(0, k, dp).start()

    def forward():
        for kk in range(1, n):
            line(kk, lax.rem(z + kk, n)).wait_recv()
            for k in range(1, m):
                plane(kk, k, dp).start()

    def finish():
        keep().wait()
        for k in range(1, n):
            line(k, z).wait_send()
        for kk in range(n):
            for k in range(1, m):
                copy = plane(kk, k, lax.rem(dp + k, m))
                copy.wait_send()
                copy.wait_recv()

    return start, forward, finish


def gather_sems(n, m):
    dma = pltpu.SemaphoreType.DMA
    return [dma((n - 1,)), dma((n,)), dma((n, m - 1)), dma((n, m)), dma((1,))]


def fwd_kernel(
    n, m, heads, rows, bk, sub,
    pref_ref, x_ref, gain_ref, shift_ref, w_ref, b_ref, cos_ref, sin_ref, shard_ref,
    normed_ref, qkv_ref, att_ref, of_ref, lse_ref, every_ref,
    q2_ref, k2_ref, v2_ref, m_ref, acc_ref, ob_ref, rs, rr, ls, lr, os_sem, or_sem, oo_sem, *gather,
):
    z = lax.axis_index("tensor")
    per = rows // bk
    prefix_chunks = -(-(n * rows // 2) // rows)
    greet([("tensor", n), ("dp", m)])
    gather_start, gather_forward, gather_finish = gatherer(n, m, shard_ref, every_ref, *gather)
    gather_start()
    prefix = pref_ref[0]

    def to_right(s):
        c = z - (s - 1)
        return remote(normed_ref.at[c], normed_ref.at[c], rs.at[s - 1], rr.at[s - 1], {"tensor": z + 1})

    def to_left(s):
        c = z + (s - 1)
        return remote(normed_ref.at[c], normed_ref.at[c], ls.at[s - 1], lr.at[s - 1], {"tensor": z - 1})

    def from_left(s):
        c = z - s
        return remote(normed_ref.at[c], normed_ref.at[c], rs.at[s - 1], rr.at[s - 1], {"tensor": z - 1})

    def from_right(s):
        c = z + s
        return remote(normed_ref.at[c], normed_ref.at[c], ls.at[s - 1], lr.at[s - 1], {"tensor": z + 1})

    def has_right(s):
        return (z + 1 < n) & (z - (s - 1) >= 0)

    def has_left(s):
        return (z >= 1) & (z + (s - 1) < n)

    for o in range(0, rows, bk):
        x = x_ref[o : o + bk].astype(F32)
        normed_ref[z, o : o + bk] = layer_norm(x, gain_ref[...], shift_ref[...]).astype(BF)

    @pl.when(has_right(1))
    def _():
        to_right(1).start()

    @pl.when(has_left(1))
    def _():
        to_left(1).start()

    m_ref[...] = jnp.full(m_ref.shape, NEG, F32)
    acc_ref[...] = jnp.zeros(acc_ref.shape, F32)
    first = lax.broadcasted_iota(jnp.int32, (16, bk), 0) == 0
    for h in range(heads):
        for c in range(n * per):
            v2_ref[h, c, HD : HD + 16, :] = jnp.where(first, 1.0, 0.0).astype(BF)

    def att_remote(h, i):
        return remote(ob_ref.at[h, i], att_ref.at[h, z], os_sem.at[h, i], or_sem.at[h, z], {"tensor": i})

    def att_own(h):
        return pltpu.make_async_copy(ob_ref.at[h, z], att_ref.at[h, z], oo_sem.at[h])

    def enter(c):
        for o in range(0, rows, bk):
            at = pl.ds(pl.multiple_of(c * rows + o, bk), bk)
            cos, sin = cos_ref[:, at], sin_ref[:, at]
            proj = dg(w_ref[...], normed_ref[c, o : o + bk, :], 1, 1) + b_ref[...]
            for h in range(heads):
                r0 = h * 3 * HD
                parts = []
                for part in range(2):
                    u = proj[r0 + part * HD : r0 + (part + 1) * HD]
                    f, b = u[: HD // 2], u[HD // 2 :]
                    parts.append(jnp.concatenate([f * cos - b * sin, b * cos + f * sin], axis=0))
                q = parts[0].astype(BF)
                v = proj[r0 + 2 * HD : r0 + 3 * HD].astype(BF)
                qkv_ref[h, c, 0, :, o : o + bk] = q
                qkv_ref[h, c, 1, :, o : o + bk] = parts[1].astype(BF)
                qkv_ref[h, c, 2, :, o : o + bk] = v
                q2_ref[h, c, :, o : o + bk] = split_query(q)
                kt = parts[1].T.astype(BF)
                k2_ref[h, c * per + o // bk] = jnp.concatenate([kt, kt], axis=1)
                v2_ref[h, c * per + o // bk, 0:HD, :] = v

    def pair(q, k, masked):
        for h in range(heads):
            for b in range(per):
                kj, vj = k2_ref[h, k * per + b], v2_ref[h, k * per + b]
                for s0 in range(0, rows, sub):
                    sl = slice(s0, s0 + sub)
                    s = dg(kj, q2_ref[h, q, :, sl], 1, 0)
                    if masked:
                        s = jnp.where(visible(k * rows + b * bk, q * rows + s0, bk, sub, prefix), s, NEG)
                    m = m_ref[h, q, :, sl]
                    mn = jnp.maximum(m, jnp.max(s, axis=0, keepdims=True))
                    p = jnp.exp2(s - mn).astype(BF)
                    scale = jnp.exp2(m - mn)
                    m_ref[h, q, :, sl] = mn
                    acc_ref[h, q, :, sl] = acc_ref[h, q, :, sl] * scale + dg(vj, p, 1, 0)

    def finish(q):
        for h in range(heads):
            total = acc_ref[h, q, HD : HD + 1, :]
            out = acc_ref[h, q, 0:HD, :] / total
            of_ref[h, q] = out
            lse_ref[h, q] = m_ref[h, q] + jnp.log2(total)
            ob_ref[h, q] = out.astype(BF)

            @pl.when(z != q)
            def _(h=h):
                att_remote(h, q).start()

            @pl.when(z == q)
            def _(h=h):
                att_own(h).start()

    def relay(s):
        @pl.when((s < n) & (z - s >= 0))
        def _():
            from_left(s).wait_recv()

        @pl.when((s + 1 < n) & has_right(s + 1))
        def _():
            to_right(s + 1).start()

        @pl.when((s < n) & (z + s < n))
        def _():
            from_right(s).wait_recv()

        @pl.when((s + 1 < n) & has_left(s + 1))
        def _():
            to_left(s + 1).start()

    def event(e, carry):
        s = (e + 1) // 2
        low = e % 2 == 1
        high = (e % 2 == 0) & (e > 0)

        @pl.when(e == 1)
        def _():
            relay(1)
            gather_forward()

        @pl.when(high & (z + s >= n))
        def _():
            relay(s + 1)

        c = jnp.where(low, z - s, z + s)
        bottom = jnp.maximum(z - s, 0)
        start = jnp.where(low, c + 1, jnp.where(high, bottom, c))
        stop = jnp.where(low, jnp.minimum(n, z + s), c)

        @pl.when((c >= 0) & (c < n))
        def _():
            enter(c)
            all_low = low & (c == 0)

            def full_pair(a, t):
                pair(jnp.maximum(a, c), jnp.minimum(a, c), False)

                @pl.when(all_low)
                def _():
                    finish(a)

                return t

            lax.fori_loop(start, stop, full_pair, 0)

            @pl.when(high)
            def _():
                relay(s + 1)

            def masked_pair(a, t):
                pair(jnp.minimum(a, c), jnp.maximum(a, c), True)
                return t

            inner = c < prefix_chunks
            lax.fori_loop(
                jnp.where(inner & high, start, c),
                jnp.where(inner & low, jnp.minimum(stop, prefix_chunks), c + 1),
                masked_pair,
                0,
            )
            ready = all_low | ((bottom == 0) & high & (c >= prefix_chunks - 1))
            from_q = jnp.where(c == prefix_chunks - 1, 0, c)

            def finish_one(q, t):
                finish(q)
                return t

            lax.fori_loop(from_q, jnp.where(ready, c + 1, from_q), finish_one, 0)

        return carry

    lax.fori_loop(0, 2 * n - 1, event, 0)
    gather_finish()
    for s in range(1, n):

        @pl.when(has_right(s))
        def _(s=s):
            to_right(s).wait_send()

        @pl.when(has_left(s))
        def _(s=s):
            to_left(s).wait_send()

    for h in range(heads):
        att_own(h).wait()
        for k in range(1, n):
            d = lax.rem(z + k, n)
            att_remote(h, d).wait_send()
            remote(ob_ref.at[h, d], att_ref.at[h, d], os_sem.at[h, d], or_sem.at[h, d], {"tensor": d}).wait_recv()


def attend(prefix, x, gain, shift, w, bias, cos_t, sin_t, shard, n, m, bk=1024, sub=1024):
    rows, width = x.shape
    heads = w.shape[0] // (3 * HD)
    length = n * rows
    vmem = pl.BlockSpec(memory_space=pltpu.VMEM)
    dma = pltpu.SemaphoreType.DMA
    return pl.pallas_call(
        functools.partial(fwd_kernel, n, m, heads, rows, bk, sub),
        in_specs=[pl.BlockSpec(memory_space=pltpu.SMEM)] + [vmem] * 7 + [pl.BlockSpec(memory_space=pl.ANY)],
        out_specs=[vmem] * 5 + [pl.BlockSpec(memory_space=pl.ANY)],
        out_shape=[
            jax.ShapeDtypeStruct((n, rows, width), BF),
            jax.ShapeDtypeStruct((heads, n, 3, HD, rows), BF),
            jax.ShapeDtypeStruct((heads, n, HD, rows), BF),
            jax.ShapeDtypeStruct((heads, n, HD, rows), F32),
            jax.ShapeDtypeStruct((heads, n, 1, rows), F32),
            jax.ShapeDtypeStruct((m, n) + shard.shape, BF),
        ],
        scratch_shapes=[
            pltpu.VMEM((heads, n, 2 * HD, rows), BF),
            pltpu.VMEM((heads, length // bk, bk, 2 * HD), BF),
            pltpu.VMEM((heads, length // bk, HD + 16, bk), BF),
            pltpu.VMEM((heads, n, 1, rows), F32),
            pltpu.VMEM((heads, n, HD + 16, rows), F32),
            pltpu.VMEM((heads, n, HD, rows), BF),
            dma((n - 1,)),
            dma((n - 1,)),
            dma((n - 1,)),
            dma((n - 1,)),
            dma((heads, n)),
            dma((heads, n)),
            dma((heads,)),
        ]
        + gather_sems(n, m),
        compiler_params=pltpu.CompilerParams(
            collective_id=0, has_side_effects=True, vmem_limit_bytes=60 * 2**20
        ),
        cost_estimate=pl.CostEstimate(
            flops=int(heads * 4 * 256 * length * length * 0.7),
            bytes_accessed=heads * length * HD * 20,
            transcendentals=int(heads * length * length * 0.7),
        ),
        name="attend_forward",
    )(prefix, x, gain.reshape(1, width), shift.reshape(1, width), w, bias[:, None], cos_t, sin_t, shard)


def small_kernel(n, m, x_ref, o_ref, zbuf, mid, pbuf, zs, zr, ps, pr):
    z = lax.axis_index("tensor")
    d = lax.axis_index("dp")
    greet([("tensor", n), ("dp", m)])

    def stage(axis, me, count, src, buf, send, recv):
        buf[me] = src[...]
        for k in range(1, count):
            peer = lax.rem(me + k, count)
            remote(src, buf.at[me], send.at[k - 1], recv.at[me], {axis: peer}).start()
        for k in range(1, count):
            peer = lax.rem(me + k, count)
            copy = remote(src, buf.at[peer], send.at[k - 1], recv.at[peer], {axis: peer})
            copy.wait_send()
            copy.wait_recv()
        total = buf[0]
        for k in range(1, count):
            total = total + buf[k]
        return total

    mid[...] = stage("tensor", z, n, x_ref, zbuf, zs, zr)
    o_ref[...] = stage("dp", d, m, mid, pbuf, ps, pr)


def total_small(vectors, n, m):
    sizes = [v.size for v in vectors]
    flat = jnp.concatenate([v.reshape(-1) for v in vectors])
    flat = jnp.pad(flat, (0, -flat.size % 1024)).reshape(-1, 128)
    vmem = pl.BlockSpec(memory_space=pltpu.VMEM)
    dma = pltpu.SemaphoreType.DMA
    summed = pl.pallas_call(
        functools.partial(small_kernel, n, m),
        in_specs=[vmem],
        out_specs=vmem,
        out_shape=jax.ShapeDtypeStruct(flat.shape, F32),
        scratch_shapes=[
            pltpu.VMEM((n,) + flat.shape, F32),
            pltpu.VMEM(flat.shape, F32),
            pltpu.VMEM((m,) + flat.shape, F32),
            dma((n - 1,)),
            dma((n,)),
            dma((m - 1,)),
            dma((m,)),
        ],
        compiler_params=pltpu.CompilerParams(collective_id=1, has_side_effects=True),
        name="total_small",
    )(flat).reshape(-1)
    out, at = [], 0
    for v, size in zip(vectors, sizes):
        out.append(summed[at : at + size].reshape(v.shape))
        at += size
    return out


def unrotate(front, back, c, s):
    return front * c + back * s, back * c - front * s


def bit_orders(m):
    bits = list(range(m.bit_length() - 1))
    return [bits, bits[:1] + bits[:0:-1], bits]


def bwd_kernel(n, heads, rows, bk, sub, m, *refs):
    steps = m.bit_length() - 1
    (pref_ref, send_ref, qkv_ref, of_ref, lse_ref, cos_ref, sin_ref, normed_ref), refs = refs[:8], refs[8:]
    parts, (shard_ref,), refs = refs[:3], refs[3:4], refs[4:]
    (g_ref, back_ref), refs = refs[:2], refs[2:]
    (rw_ref,), results, (every_ref,), refs = refs[:1], refs[1:4], refs[4:5], refs[5:]
    (do_ref, q2_ref, qn_ref, don_ref, dd_ref, dq_ref, dk_ref, dv_ref), refs = refs[:8], refs[8:]
    (wv_ref, ws_ref, wb_ref, wf_ref), refs = refs[:4], refs[4:]
    tracks = []
    for tag, order in enumerate(bit_orders(m)):
        held, came, (zbuf, fin) = refs[0], refs[1 : steps + 1], refs[steps + 1 : steps + 3]
        refs = refs[steps + 3 :]
        tracks.append((tag, order, parts[tag], held, came, zbuf, fin, results[tag]))
    (own_sem, s_sem, r_sem, kvs, kvr, qs, qr, kvo, qo), refs = refs[:9], refs[9:]
    (hs, hr, ho, p2s, p2r, p2o, p3s, p3r, p3o, w1s, w1r, w1o, w2s, w2r, w2o), gather = refs[:15], refs[15:]
    z = lax.axis_index("tensor")
    dp = lax.axis_index("dp")
    length = n * rows
    per = rows // bk
    prefix_chunks = -(-(length // 2) // rows)
    greet([("tensor", n), ("dp", m)])

    gather_start, gather_forward, gather_finish = gatherer(n, m, shard_ref, every_ref, *gather)
    def spread(axis, me, count, pick, dst, send, recv, own, tag):
        pltpu.make_async_copy(pick(me), dst.at[me], own.at[tag]).start()
        for k in range(1, count):
            d = lax.rem(me + k, count)
            remote(pick(d), dst.at[me], send.at[tag, k - 1], recv.at[tag, me], {axis: d}).start()

    def arrived(axis, me, count, pick, dst, recv, send, own, tag):
        pltpu.make_async_copy(pick(me), dst.at[me], own.at[tag]).wait()
        for k in range(1, count):
            d = lax.rem(me + k, count)
            copy = remote(pick(d), dst.at[d], send.at[tag, k - 1], recv.at[tag, d], {axis: d})
            copy.wait_send()
            copy.wait_recv()

    def own_bit(b):
        return (dp // 2**b) % 2

    def slice_of(order, bit, j):
        index = bit * 2 ** order[0]
        for place, b in enumerate(order[1:]):
            index = index + ((j >> place) & 1) * 2**b
        return index

    def place(order, i, last):
        at = last * 2 ** (i - 1)
        for k in range(1, i):
            at = at + own_bit(order[k]) * 2 ** (k - 1)
        return at

    def halve_copies(i):
        for tag, order, part, held, came, zbuf, fin, res in tracks:
            bit = own_bit(order[i])
            partner = dp + (1 - 2 * bit) * 2 ** order[i]
            for j in range(m >> (i + 1)):
                src = part.at[slice_of(order, 1 - bit, j)] if i == 0 else held.at[place(order, i, 1 - bit) + 2**i * j]
                yield tag, j, bit, order, remote(src, came[i].at[j], hs.at[tag, i, j], hr.at[tag, i, j], {"dp": partner})

    def kept_copies():
        for tag, order, part, held, came, zbuf, fin, res in tracks:
            for j in range(m // 2):
                src = part.at[slice_of(order, own_bit(order[0]), j)]
                yield pltpu.make_async_copy(src, held.at[j], ho.at[tag, j])

    def halve_start(i):
        for _, _, _, _, copy in halve_copies(i):
            copy.start()

    def halve_sum(i):
        if i == 0:
            for copy in kept_copies():
                copy.wait()
        for tag, j, bit, order, copy in halve_copies(i):
            copy.wait_send()
            copy.wait_recv()
            held, came = tracks[tag][3], tracks[tag][4]
            at = j if i == 0 else place(order, i, bit) + 2**i * j
            for t in range(n):
                held[at, t] = (held[at, t].astype(F32) + came[i][j, t].astype(F32)).astype(BF)

    def line_start():
        for tag, order, part, held, came, zbuf, fin, res in tracks:
            spread("tensor", z, n, lambda d, held=held, order=order: held.at[place(order, steps - 1, own_bit(order[-1])), d], zbuf, p2s, p2r, p2o, tag)

    def line_sum():
        for tag, order, part, held, came, zbuf, fin, res in tracks:
            arrived("tensor", z, n, lambda d, held=held, order=order: held.at[place(order, steps - 1, own_bit(order[-1])), d], zbuf, p2r, p2s, p2o, tag)
            total = zbuf[0].astype(F32)
            for k in range(1, n):
                total = total + zbuf[k].astype(F32)
            fin[...] = total.astype(BF)
            spread("dp", dp, m, lambda d, fin=fin: fin, res, p3s, p3r, p3o, tag)

    def after_last():
        for tag, order, part, held, came, zbuf, fin, res in tracks:
            arrived("dp", dp, m, lambda d, fin=fin: fin, res, p3r, p3s, p3o, tag)

    for copy in kept_copies():
        copy.start()
    halve_start(0)
    points = (0, 3, 4) if steps == 3 else tuple(range(steps))

    def at_point(e):
        for i, point in enumerate(points):

            @pl.when(e == point)
            def _(i=i):
                halve_sum(i)
                if i + 1 < steps:
                    halve_start(i + 1)
                else:
                    line_start()

        @pl.when(e == 1)
        def _():
            gather_start()

        @pl.when(e == n + 1)
        def _():
            gather_forward()

        @pl.when(e == 2 * n - 1)
        def _():
            line_sum()

    def weight_start(h):
        grad = dg(g_ref[h, 0], normed_ref[0], 1, 0)
        for t in range(1, n):
            grad = grad + dg(g_ref[h, t], normed_ref[t], 1, 0)
        wv_ref[...] = grad
        q = 3 * HD // m
        for i in range(m):
            ws_ref[h, i] = wv_ref[i * q : (i + 1) * q].astype(BF)
        spread("dp", dp, m, lambda d: ws_ref.at[h, d], wb_ref.at[h], w1s, w1r, w1o, h)

    def weight_sum(h):
        arrived("dp", dp, m, lambda d: ws_ref.at[h, d], wb_ref.at[h], w1r, w1s, w1o, h)
        total = wb_ref[h, 0].astype(F32)
        for k in range(1, m):
            total = total + wb_ref[h, k].astype(F32)
        wf_ref[h] = total.astype(BF)
        spread("dp", dp, m, lambda d: wf_ref.at[h], rw_ref.at[h], w2s, w2r, w2o, h)

    def weight_end(h):
        arrived("dp", dp, m, lambda d: wf_ref.at[h], rw_ref.at[h], w2r, w2s, w2o, h)

    def do_copy(h, k):
        d = lax.rem(z + k, n)
        return remote(send_ref.at[d, h], do_ref.at[h, z], s_sem.at[h, k - 1], r_sem.at[h, k - 1], {"tensor": d})

    def own_copy(h):
        return pltpu.make_async_copy(send_ref.at[z, h], do_ref.at[h, z], own_sem.at[h])

    def do_start(h):
        own_copy(h).start()
        for k in range(1, n):
            do_copy(h, k).start()

    do_start(0)
    prefix = pref_ref[0]
    kv_rows, q_rows = pl.ds(HD, 2 * HD), pl.ds(0, HD)

    def piece(h, t, part, source, send, recv):
        return remote(
            g_ref.at[h, t, part], back_ref.at[source, h, part], send.at[h, t], recv.at[h, source], {"tensor": t}
        )

    def own_piece(h, part, sem):
        return pltpu.make_async_copy(g_ref.at[h, z, part], back_ref.at[z, h, part], sem.at[h])

    def hand_out(h, t, part, send, recv, own):
        @pl.when(z != t)
        def _():
            piece(h, t, part, z, send, recv).start()

        @pl.when(z == t)
        def _():
            own_piece(h, part, own).start()

    def head(h, carry):
        own_copy(h).wait()
        for k in range(1, n):
            do_copy(h, k).wait_recv()

        @pl.when(h + 1 < heads)
        def _():
            do_start(h + 1)

        for c in range(n):
            q = qkv_ref[h, c, 0]
            q2_ref[c] = split_query(q)
            qn_ref[c] = q.astype(F32).T.astype(BF)
            dof = do_ref[h, c].astype(F32)
            don_ref[c] = dof.T.astype(BF)
            inner = jnp.sum(dof * of_ref[h, c], axis=0, keepdims=True)
            dd_ref[c] = jnp.concatenate([inner, lse_ref[h, c]], axis=0)
            dq_ref[c] = jnp.zeros((HD, rows), F32)

        def keys(turn, c1):
            t = lax.rem(z + 1 + turn, n)
            for o in range(0, rows, bk):
                kt = qkv_ref[h, t, 1, :, o : o + bk]
                kn = kt.astype(F32).T.astype(BF)
                k2 = jnp.concatenate([kn, kn], axis=1)
                vn = qkv_ref[h, t, 2, :, o : o + bk].astype(F32).T.astype(BF)
                dk_ref[...] = jnp.zeros(dk_ref.shape, F32)
                dv_ref[...] = jnp.zeros(dv_ref.shape, F32)

                def block(i, masked, o=o, kt=kt, k2=k2, vn=vn):
                    for s0 in range(0, rows, sub):
                        sl = slice(s0, s0 + sub)
                        p = jnp.exp2(dg(k2, q2_ref[i, :, sl], 1, 0) - dd_ref[i, 1:2, sl])
                        if masked:
                            p = jnp.where(visible(t * rows + o, i * rows + s0, bk, sub, prefix), p, 0.0)
                        dp = dg(vn, do_ref[h, i, :, sl], 1, 0)
                        dv_ref[...] += dg(p.astype(BF), don_ref[i, sl, :], 1, 0)
                        ds = (p * (dp - dd_ref[i, 0:1, sl])).astype(BF)
                        dk_ref[...] += dg(ds, qn_ref[i, sl, :], 1, 0)
                        dq_ref[i, :, sl] += dg(kt, ds, 1, 0)

                def masked_block(i, c2, block=block):
                    block(i, True)
                    return c2

                def full_block(i, c2, block=block):
                    block(i, False)
                    return c2

                lax.fori_loop(jnp.where(t < prefix_chunks, 0, t), t + 1, masked_block, 0)
                lax.fori_loop(t + 1, n, full_block, 0)
                dk = dk_ref[...].T * HD**-0.5
                at = pl.ds(pl.multiple_of(t * rows + o, bk), bk)
                a, b = unrotate(dk[: HD // 2], dk[HD // 2 :], cos_ref[:, at], sin_ref[:, at])
                g_ref[h, t, HD : HD + HD // 2, o : o + bk] = a.astype(BF)
                g_ref[h, t, HD + HD // 2 : 2 * HD, o : o + bk] = b.astype(BF)
                g_ref[h, t, 2 * HD : 3 * HD, o : o + bk] = dv_ref[...].T.astype(BF)
            hand_out(h, t, kv_rows, kvs, kvr, kvo)
            at_point(h * n + turn)
            return c1

        lax.fori_loop(0, n, keys, 0)
        for c in range(n):
            x = dq_ref[c] * HD**-0.5
            at = slice(c * rows, (c + 1) * rows)
            a, b = unrotate(x[: HD // 2], x[HD // 2 :], cos_ref[:, at], sin_ref[:, at])
            g_ref[h, c, : HD // 2, :] = a.astype(BF)
            g_ref[h, c, HD // 2 : HD, :] = b.astype(BF)
            hand_out(h, c, q_rows, qs, qr, qo)
        weight_start(h)

        @pl.when(h > 0)
        def _():
            weight_sum(h - 1)

        return carry

    lax.fori_loop(0, heads, head, 0)
    weight_sum(heads - 1)
    gather_finish()
    after_last()
    for h in range(heads):
        weight_end(h)
    for h in range(heads):
        own_piece(h, kv_rows, kvo).wait()
        own_piece(h, q_rows, qo).wait()
        for k in range(1, n):
            do_copy(h, k).wait_send()
            d = lax.rem(z + k, n)
            for part, send, recv in ((kv_rows, kvs, kvr), (q_rows, qs, qr)):
                copy = piece(h, d, part, d, send, recv)
                copy.wait_send()
                copy.wait_recv()


def attend_back(prefix, send, qkv, of, lse, cos_t, sin_t, normed, parts, shard, bk=512, sub=256):
    n, heads, _, rows = send.shape
    m, width = parts[0].shape[0], parts[0].shape[-1]
    steps = m.bit_length() - 1
    size_w = 3 * HD // m
    length = n * rows
    vmem = pl.BlockSpec(memory_space=pltpu.VMEM)
    dma = pltpu.SemaphoreType.DMA
    buffers = []
    for part in parts:
        size = part.shape[2]
        for count in [m // 2] + [m >> (i + 1) for i in range(steps)]:
            buffers.append(pltpu.VMEM((count, n, size, width), BF))
        buffers += [pltpu.VMEM((n, size, width), BF), pltpu.VMEM((size, width), BF)]
    return pl.pallas_call(
        functools.partial(bwd_kernel, n, heads, rows, bk, sub, m),
        in_specs=[pl.BlockSpec(memory_space=pltpu.SMEM)] + [vmem] * 7 + [pl.BlockSpec(memory_space=pl.ANY)] * 4,
        out_specs=[vmem] * 6 + [pl.BlockSpec(memory_space=pl.ANY)],
        out_shape=[
            jax.ShapeDtypeStruct((heads, n, 3 * HD, rows), BF),
            jax.ShapeDtypeStruct((n, heads, 3 * HD, rows), BF),
            jax.ShapeDtypeStruct((heads, m, size_w, width), BF),
        ]
        + [jax.ShapeDtypeStruct((m, part.shape[2], width), BF) for part in parts]
        + [jax.ShapeDtypeStruct((m, n) + shard.shape, BF)],
        scratch_shapes=[
            pltpu.VMEM((heads, n, HD, rows), BF),
            pltpu.VMEM((n, 2 * HD, rows), BF),
            pltpu.VMEM((n, rows, HD), BF),
            pltpu.VMEM((n, rows, HD), BF),
            pltpu.VMEM((n, 2, rows), F32),
            pltpu.VMEM((n, HD, rows), F32),
            pltpu.VMEM((bk, HD), F32),
            pltpu.VMEM((bk, HD), F32),
            pltpu.VMEM((3 * HD, width), F32),
            pltpu.VMEM((heads, m, size_w, width), BF),
            pltpu.VMEM((heads, m, size_w, width), BF),
            pltpu.VMEM((heads, size_w, width), BF),
        ]
        + buffers
        + [
            dma((heads,)),
            dma((heads, n - 1)),
            dma((heads, n - 1)),
            dma((heads, n)),
            dma((heads, n)),
            dma((heads, n)),
            dma((heads, n)),
            dma((heads,)),
            dma((heads,)),
            dma((3, steps, m // 2)),
            dma((3, steps, m // 2)),
            dma((3, m // 2)),
            dma((3, n - 1)),
            dma((3, n)),
            dma((3,)),
            dma((3, m - 1)),
            dma((3, m)),
            dma((3,)),
            dma((heads, m - 1)),
            dma((heads, m)),
            dma((heads,)),
            dma((heads, m - 1)),
            dma((heads, m)),
            dma((heads,)),
        ]
        + gather_sems(n, m),
        compiler_params=pltpu.CompilerParams(
            collective_id=2, has_side_effects=True, vmem_limit_bytes=63 * 2**20
        ),
        cost_estimate=pl.CostEstimate(
            flops=int(heads * 10 * 256 * length * length * 0.7),
            bytes_accessed=heads * length * HD * 20,
            transcendentals=int(heads * length * length * 0.7),
        ),
        name="attend_backward",
    )(prefix, send, qkv, of, lse, cos_t, sin_t, normed, *parts, shard)


EPS = 1e-05
ROPE_BASE = 10000.0
GELU_C = 0.7978845608028654


def layer_norm(values, norm_gain, norm_shift):
    center = values - jnp.mean(values, axis=-1, keepdims=True)
    spread = jnp.mean(center * center, axis=-1, keepdims=True)
    return center * lax.rsqrt(spread + EPS) * norm_gain + norm_shift


def rotary_tables(length):
    half_dim = HD // 2
    frequency = ROPE_BASE ** (-jnp.arange(half_dim, dtype=jnp.float32) / half_dim)
    angles = frequency[:, None] * jnp.arange(length, dtype=jnp.float32)[None, :]
    return (jnp.cos(angles), jnp.sin(angles))


def mlp_kernel(
    split, size, block, nm_ref, gm_ref, w_ref, upb_ref, out_ref, dnm_ref, dup_ref, ddown_ref, dupb_ref, nmt_ref, gmt_ref, act_ref, gp_ref
):
    step = pl.program_id(0)

    @pl.when(step == 0)
    def _():
        nmt_ref[...] = nm_ref[...].T
        gmt_ref[...] = gm_ref[...].T
        out_ref[...] = jnp.zeros(out_ref.shape, F32)
        dnm_ref[...] = jnp.zeros(dnm_ref.shape, F32)

    width = w_ref.shape[-1]
    up = w_ref[:, :size].reshape(split * size, width)
    down = w_ref[:, size : 2 * size].reshape(split * size, width)
    for r in range(0, nm_ref.shape[0], block):
        at = slice(r, r + block)
        pre = dg(nm_ref[at], up, 1, 0) + upb_ref[...]
        sq = pre * pre
        th = jnp.tanh(GELU_C * (pre + 0.044715 * sq * pre))
        half = 0.5 * (1.0 + th)
        act = (pre * half).astype(BF)
        slope = half + 0.5 * pre * (1.0 - th * th) * (GELU_C + (3.0 * 0.044715 * GELU_C) * sq)
        gp = (dg(gm_ref[at], down, 1, 1) * slope).astype(BF)
        act_ref[at] = act
        gp_ref[at] = gp
        out_ref[at] += dg(act, down, 1, 0)
        dnm_ref[at] += dg(gp, up, 1, 1)
    dup_ref[...] = dg(nmt_ref[...], gp_ref[...], 1, 0).astype(BF).reshape(split, size, width)
    ddown_ref[...] = dg(gmt_ref[...], act_ref[...], 1, 0).astype(BF).reshape(split, size, width)
    dupb_ref[...] = jnp.sum(gp_ref[...].astype(F32), axis=0, keepdims=True)


def mlp(nm, gm, weights, up_bias, size, block=256):
    rows, width = nm.shape
    split, n, deep, _ = weights.shape
    f = split * size
    squeezed = pl.Squeezed()
    const = pl.BlockSpec((rows, width), lambda i: (0, 0))
    hidden = n * f
    return pl.pallas_call(
        functools.partial(mlp_kernel, split, size, block),
        grid=(n,),
        in_specs=[
            const,
            const,
            pl.BlockSpec((split, squeezed, deep, width), lambda i: (0, i, 0, 0)),
            pl.BlockSpec((1, f), lambda i: (0, i)),
        ],
        out_specs=[
            const,
            const,
            pl.BlockSpec((split, squeezed, size, width), lambda i: (0, i, 0, 0)),
            pl.BlockSpec((split, squeezed, size, width), lambda i: (0, i, 0, 0)),
            pl.BlockSpec((1, f), lambda i: (0, i)),
        ],
        out_shape=[
            jax.ShapeDtypeStruct((rows, width), F32),
            jax.ShapeDtypeStruct((rows, width), F32),
            jax.ShapeDtypeStruct((split, n, size, width), BF),
            jax.ShapeDtypeStruct((split, n, size, width), BF),
            jax.ShapeDtypeStruct((1, hidden), F32),
        ],
        scratch_shapes=[pltpu.VMEM((width, rows), BF)] * 2 + [pltpu.VMEM((rows, f), BF)] * 2,
        compiler_params=pltpu.CompilerParams(vmem_limit_bytes=60 * 2**20),
        cost_estimate=pl.CostEstimate(
            flops=12 * rows * width * hidden, bytes_accessed=8 * width * hidden + 12 * rows * width, transcendentals=rows * hidden
        ),
        name="mlp",
    )(nm, gm, weights, up_bias)


def norm_backward(values, gain, grad):
    center = values - jnp.mean(values, axis=-1, keepdims=True)
    rstd = lax.rsqrt(jnp.mean(center * center, axis=-1, keepdims=True) + EPS)
    hat = center * rstd
    scaled = grad * gain
    result = rstd * (
        scaled - jnp.mean(scaled, axis=-1, keepdims=True) - hat * jnp.mean(scaled * hat, axis=-1, keepdims=True)
    )
    return result, grad * hat


def column_sum(value):
    return jnp.sum(value, axis=0, keepdims=True)


def middle_kernel(
    n, heads, block, weight_ref, grad_ref, middle_ref, top_ref, gain_ref, out_w_ref, att_ref,
    gm_ref, send_ref, out_grad_ref, vec_ref, ga_ref,
):
    vec_ref[...] = jnp.zeros(vec_ref.shape, F32)
    for r in range(0, grad_ref.shape[0], block):
        at = slice(r, r + block)
        dy = grad_ref[at]
        back, scaled = norm_backward(middle_ref[at], gain_ref[...], dy)
        gm = weight_ref[4] * top_ref[at].astype(F32) + back
        gm_ref[at] = gm
        ga = gm.astype(BF)
        ga_ref[at] = ga
        vec_ref[0:1] += column_sum(scaled)
        vec_ref[1:2] += column_sum(dy)
        vec_ref[2:3] += column_sum(ga.astype(F32))
    for d in range(n):
        got = dg(out_w_ref[d], ga_ref[...], 1, 1).astype(BF)
        for h in range(heads):
            send_ref[d, h] = got[h * HD : (h + 1) * HD]
    for h in range(heads):
        got = dg(att_ref[h], ga_ref[...], 1, 0).astype(BF)
        for d in range(n):
            out_grad_ref[d, h * HD : (h + 1) * HD] = got[d * HD : (d + 1) * HD]


def middle_back(depth_weights, grad, middle, top, gain, out_w, attended, block=256):
    rows, width = grad.shape
    n, local, _ = out_w.shape
    heads = local // HD
    vmem = pl.BlockSpec(memory_space=pltpu.VMEM)
    return pl.pallas_call(
        functools.partial(middle_kernel, n, heads, block),
        in_specs=[pl.BlockSpec(memory_space=pltpu.SMEM)] + [vmem] * 6,
        out_specs=[vmem] * 4,
        out_shape=[
            jax.ShapeDtypeStruct((rows, width), F32),
            jax.ShapeDtypeStruct((n, heads, HD, rows), BF),
            jax.ShapeDtypeStruct((n, local, width), BF),
            jax.ShapeDtypeStruct((8, width), F32),
        ],
        scratch_shapes=[pltpu.VMEM((rows, width), BF)],
        compiler_params=pltpu.CompilerParams(vmem_limit_bytes=48 * 2**20),
        cost_estimate=pl.CostEstimate(
            flops=4 * rows * width * width, bytes_accessed=20 * rows * width, transcendentals=rows
        ),
        name="middle_back",
    )(depth_weights, grad, middle, top, gain.reshape(1, width), out_w, attended.reshape(heads, n * HD, rows))


def input_kernel(n, split, back_ref, w_ref, x_ref, gm_ref, gain_ref, out_ref, vec_ref):
    step = pl.program_id(0)

    @pl.when(step == 0)
    def _():
        vec_ref[...] = jnp.zeros(vec_ref.shape, F32)

    cols, width = w_ref.shape[-1], x_ref.shape[-1]
    total = None
    for d in range(n):
        w = w_ref[:, d].reshape(width, cols)
        term = dg(w, back_ref[d], 1, 0)
        total = term if total is None else total + term
    dy = total.T
    back, scaled = norm_backward(x_ref[...].astype(F32), gain_ref[...], dy)
    out_ref[...] = gm_ref[...] + back
    vec_ref[0:1] += column_sum(scaled)
    vec_ref[1:2] += column_sum(dy)


def input_back(back, w_every, x, grad_middle, gain, block=256):
    rows, width = x.shape
    n, cols, _ = back.shape
    split = w_every.shape[0]
    row_block = pl.BlockSpec((block, width), lambda i: (i, 0))
    return pl.pallas_call(
        functools.partial(input_kernel, n, split),
        grid=(rows // block,),
        in_specs=[
            pl.BlockSpec((n, cols, block), lambda i: (0, 0, i)),
            pl.BlockSpec(w_every.shape, lambda i: (0, 0, 0, 0)),
            row_block,
            row_block,
            pl.BlockSpec((1, width), lambda i: (0, 0)),
        ],
        out_specs=[row_block, pl.BlockSpec((8, width), lambda i: (0, 0))],
        out_shape=[jax.ShapeDtypeStruct((rows, width), F32), jax.ShapeDtypeStruct((8, width), F32)],
        compiler_params=pltpu.CompilerParams(vmem_limit_bytes=48 * 2**20),
        cost_estimate=pl.CostEstimate(
            flops=2 * rows * width * n * cols, bytes_accessed=12 * rows * width + 2 * n * cols * (rows + width), transcendentals=rows
        ),
        name="input_back",
    )(back, w_every, x, grad_middle, gain.reshape(1, width))


def shards(
    block_input,
    embedding,
    history,
    cotangent,
    first_gain,
    first_shift,
    qkv_weight,
    qkv_bias,
    out_weight,
    out_bias,
    second_gain,
    second_shift,
    up_weight,
    up_bias,
    down_weight,
    down_bias,
    depth_weights,
    prefix_length,
    history_index,
):
    rows, width = block_input.shape
    local = qkv_weight.shape[2]
    heads = local // HD
    n = lax.axis_size("tensor")
    m = lax.axis_size("dp")
    z = lax.axis_index("tensor")
    dp = lax.axis_index("dp")
    length = rows * n
    hidden = up_weight.shape[1]
    cos_t, sin_t = rotary_tables(length)

    w_t = qkv_weight.reshape(width, 3, heads, HD).transpose(2, 1, 3, 0).reshape(3 * local, width)
    w_f = qkv_weight.reshape(width, 3, heads, HD).transpose(0, 2, 1, 3).reshape(width, 3 * local)
    b_t = qkv_bias.reshape(3, heads, HD).transpose(1, 0, 2).reshape(3 * local).astype(F32)
    def mine(shard):
        size = shard.shape[0] // m
        return lax.dynamic_slice_in_dim(shard, dp * size, size, 0)

    size, out_size = width // m, local // m
    used = 2 * size + out_size
    fill = jnp.zeros((15 - used % 16, width), BF)
    early = jnp.concatenate([mine(up_weight), mine(down_weight), mine(out_weight), up_bias[None], fill], axis=0)
    normed, qkv_t, attended, of, lse, every = attend(
        prefix_length, block_input, first_gain, first_shift, w_t, b_t, cos_t, sin_t, early, n, m
    )
    out_all = every[:, :, 2 * size : used].transpose(1, 0, 2, 3).reshape(n, heads, HD, width)
    up_bias_all = every[0, :, used, :hidden].astype(F32).reshape(1, n * hidden)

    inputs_f = block_input.astype(F32)
    attn = None
    for h in range(heads):
        piece = dg(attended[h].reshape(n * HD, rows), out_all[:, h].reshape(n * HD, width), 0, 0)
        attn = piece if attn is None else attn + piece


    middle = inputs_f + (attn + out_bias.astype(F32))
    normed_mid_f = layer_norm(middle, second_gain, second_shift)
    grad_top = cotangent.astype(F32)
    grad_block = depth_weights[4] * grad_top
    grad_branch = grad_block.astype(BF)
    if size % 16 == 0:
        mlp_weights, part = every, size
    else:
        whole = every[:, :, : 2 * size].reshape(m, n, 2, size, width)
        mlp_weights, part = whole.transpose(1, 2, 0, 3, 4).reshape(1, n, 2 * hidden, width), hidden
    mlp_out, grad_normed_mid, up_grad, down_grad, up_bias_grad = mlp(
        normed_mid_f.astype(BF), grad_branch, mlp_weights, up_bias_all, part
    )
    if size % 16 != 0:
        up_grad = up_grad.reshape(n, m, size, width).transpose(1, 0, 2, 3)
        down_grad = down_grad.reshape(n, m, size, width).transpose(1, 0, 2, 3)
    block_out = middle + (mlp_out + down_bias.astype(F32))
    slot_ids = jnp.arange(3, dtype=jnp.int32)
    pick = (history_index[:, None] == slot_ids[None, :]).astype(F32)
    slot_coef = jnp.sum(depth_weights[1:4, None] * pick, axis=0)
    embed_f = embedding.astype(F32)
    mixed = depth_weights[0] * embed_f + depth_weights[4] * block_out
    for slot_id in range(3):
        mixed = mixed + slot_coef[slot_id] * history[slot_id].astype(F32)
    dwa_output = mixed.astype(BF)
    slot_sums = jnp.stack([jnp.sum(grad_top * history[slot_id].astype(F32)) for slot_id in range(3)])
    grad_depth = jnp.concatenate(
        [
            jnp.sum(grad_top * embed_f)[None],
            jnp.sum(pick * slot_sums[None, :], axis=1),
            jnp.sum(grad_top * block_out)[None],
        ]
    )
    down_bias_grad = jnp.sum(grad_branch.astype(F32), axis=0)

    grad_middle, grad_send, out_grad, middle_sums = middle_back(
        depth_weights, grad_normed_mid, middle, cotangent, second_gain, out_all.reshape(n, local, width), attended
    )
    second_gain_grad, second_shift_grad, out_bias_grad = middle_sums[0], middle_sums[1], middle_sums[2]
    out_grad = out_grad.reshape(n, m, out_size, width).transpose(1, 0, 2, 3)
    grad_own, back, qkv_sum, up_sum, down_sum, out_sum, w_every = attend_back(
        prefix_length, grad_send, qkv_t, of, lse, cos_t, sin_t, normed, (up_grad, down_grad, out_grad), mine(w_f)
    )
    if size % 16 != 0:
        w_every = w_every.transpose(1, 0, 2, 3).reshape(1, n, width, 3 * local)
    qkv_bias_grad = jnp.sum(grad_own.astype(F32), axis=(1, 3)).reshape(-1)
    grad_input, input_sums = input_back(
        back.reshape(n, 3 * local, rows), w_every, block_input, grad_middle, first_gain
    )
    first_gain_grad, first_shift_grad = input_sums[0], input_sums[1]

    up_grad = up_sum.reshape(width, hidden).astype(F32)
    down_grad = down_sum.reshape(width, hidden).T.astype(F32)
    out_grad = out_sum.reshape(local, width).astype(F32)
    qkv_grad = qkv_sum.reshape(heads, 3, HD, width).transpose(3, 1, 0, 2).reshape(width, 3, local).astype(F32)

    spread = jnp.zeros((n, 3 * local), F32)
    spread = lax.dynamic_update_slice_in_dim(spread, qkv_bias_grad[None], z, 0)
    (
        out_bias_grad,
        second_gain_grad,
        second_shift_grad,
        down_bias_grad,
        grad_depth,
        up_bias_grad,
        qkv_bias_grad,
        first_gain_grad,
        first_shift_grad,
    ) = total_small(
        [
            out_bias_grad,
            second_gain_grad,
            second_shift_grad,
            down_bias_grad,
            grad_depth,
            up_bias_grad[0],
            spread,
            first_gain_grad,
            first_shift_grad,
        ],
        n,
        m,
    )
    up_bias_grad = lax.dynamic_slice_in_dim(up_bias_grad, z * hidden, hidden, 0)
    qkv_bias_grad = lax.dynamic_index_in_dim(qkv_bias_grad, z, 0, keepdims=False)
    qkv_bias_grad = qkv_bias_grad.reshape(heads, 3, HD).transpose(1, 0, 2).reshape(3, local)
    return (
        dwa_output,
        grad_input,
        first_gain_grad,
        first_shift_grad,
        qkv_grad,
        qkv_bias_grad,
        out_grad,
        out_bias_grad,
        second_gain_grad,
        second_shift_grad,
        up_grad,
        up_bias_grad,
        down_grad,
        down_bias_grad,
        grad_depth,
    )


def solution(mesh):
    both = ("dp", "tensor")
    return jax.shard_map(
        shards,
        mesh=mesh,
        in_specs=(
            P(both, None),
            P(both, None),
            P(None, both, None),
            P(both, None),
            P(),
            P(),
            P(None, None, "tensor"),
            P(None, "tensor"),
            P("tensor", None),
            P(),
            P(),
            P(),
            P(None, "tensor"),
            P("tensor"),
            P("tensor", None),
            P(),
            P(),
            P("dp"),
            P(),
        ),
        out_specs=(
            P(both, None),
            P(both, None),
            P(),
            P(),
            P(None, None, "tensor"),
            P(None, "tensor"),
            P("tensor", None),
            P(),
            P(),
            P(),
            P(None, "tensor"),
            P("tensor"),
            P("tensor", None),
            P(),
            P(),
        ),
        check_vma=False,
    )
```

```python
import functools

import jax
import jax.numpy as jnp
from jax import lax
from jax.experimental import pallas as pl
from jax.experimental.pallas import tpu as pltpu
from jax.sharding import PartitionSpec as P

HD = 64
NEG = -1e30
LOG2E = 1.4426950408889634
F32 = jnp.float32
BF = jnp.bfloat16


def dg(a, b, ca, cb):
    return lax.dot_general(a, b, (((ca,), (cb,)), ((), ())), preferred_element_type=F32)


def split_query(q):
    scaled = q.astype(F32) * (LOG2E * HD**-0.5)
    high = scaled.astype(BF)
    low = (scaled - high.astype(F32)).astype(BF)
    return jnp.concatenate([high, low], axis=0)


def visible(key_start, query_start, keys, queries, prefix):
    key_pos = key_start + lax.broadcasted_iota(jnp.int32, (keys, queries), 0)
    query_pos = query_start + lax.broadcasted_iota(jnp.int32, (1, queries), 1)
    return key_pos <= jnp.maximum(query_pos, prefix - 1)


def remote(src, dst, send, recv, peer):
    return pltpu.make_async_remote_copy(
        src_ref=src,
        dst_ref=dst,
        send_sem=send,
        recv_sem=recv,
        device_id=peer,
        device_id_type=pl.DeviceIdType.MESH,
    )


def greet(axis_counts):
    barrier = pltpu.get_barrier_semaphore()
    total = 0
    for axis, count in axis_counts:
        me = lax.axis_index(axis)
        for k in range(1, count):
            pl.semaphore_signal(
                barrier, inc=1, device_id={axis: lax.rem(me + k, count)}, device_id_type=pl.DeviceIdType.MESH
            )
        total += count - 1
    pl.semaphore_wait(barrier, total)


def gatherer(n, m, src, dst, line_send, line_recv, plane_send, plane_recv, own):
    z = lax.axis_index("tensor")
    dp = lax.axis_index("dp")

    def keep():
        return pltpu.make_async_copy(src, dst.at[dp, z], own.at[0])

    def line(k, t):
        return remote(src, dst.at[dp, t], line_send.at[k - 1], line_recv.at[t], {"tensor": lax.rem(z + k, n)})

    def plane(kk, k, d):
        t = lax.rem(z + kk, n)
        start = src if kk == 0 else dst.at[dp, t]
        peer = lax.rem(dp + k, m)
        return remote(start, dst.at[d, t], plane_send.at[kk, k - 1], plane_recv.at[t, d], {"dp": peer})

    def start():
        keep().start()
        for k in range(1, n):
            line(k, z).start()
        for k in range(1, m):
            plane(0, k, dp).start()

    def forward():
        for kk in range(1, n):
            line(kk, lax.rem(z + kk, n)).wait_recv()
            for k in range(1, m):
                plane(kk, k, dp).start()

    def finish():
        keep().wait()
        for k in range(1, n):
            line(k, z).wait_send()
        for kk in range(n):
            for k in range(1, m):
                copy = plane(kk, k, lax.rem(dp + k, m))
                copy.wait_send()
                copy.wait_recv()

    return start, forward, finish


def gather_sems(n, m):
    dma = pltpu.SemaphoreType.DMA
    return [dma((n - 1,)), dma((n,)), dma((n, m - 1)), dma((n, m)), dma((1,))]


def fwd_kernel(
    n, m, heads, rows, bk, sub,
    pref_ref, x_ref, gain_ref, shift_ref, w_ref, b_ref, cos_ref, sin_ref, shard_ref,
    normed_ref, qkv_ref, att_ref, of_ref, lse_ref, every_ref,
    q2_ref, k2_ref, v2_ref, m_ref, acc_ref, ob_ref, rs, rr, ls, lr, os_sem, or_sem, oo_sem, *gather,
):
    z = lax.axis_index("tensor")
    per = rows // bk
    prefix_chunks = -(-(n * rows // 2) // rows)
    greet([("tensor", n), ("dp", m)])
    gather_start, gather_forward, gather_finish = gatherer(n, m, shard_ref, every_ref, *gather)
    gather_start()
    prefix = pref_ref[0]

    def to_right(s):
        c = z - (s - 1)
        return remote(normed_ref.at[c], normed_ref.at[c], rs.at[s - 1], rr.at[s - 1], {"tensor": z + 1})

    def to_left(s):
        c = z + (s - 1)
        return remote(normed_ref.at[c], normed_ref.at[c], ls.at[s - 1], lr.at[s - 1], {"tensor": z - 1})

    def from_left(s):
        c = z - s
        return remote(normed_ref.at[c], normed_ref.at[c], rs.at[s - 1], rr.at[s - 1], {"tensor": z - 1})

    def from_right(s):
        c = z + s
        return remote(normed_ref.at[c], normed_ref.at[c], ls.at[s - 1], lr.at[s - 1], {"tensor": z + 1})

    def has_right(s):
        return (z + 1 < n) & (z - (s - 1) >= 0)

    def has_left(s):
        return (z >= 1) & (z + (s - 1) < n)

    for o in range(0, rows, bk):
        x = x_ref[o : o + bk].astype(F32)
        normed_ref[z, o : o + bk] = layer_norm(x, gain_ref[...], shift_ref[...]).astype(BF)

    @pl.when(has_right(1))
    def _():
        to_right(1).start()

    @pl.when(has_left(1))
    def _():
        to_left(1).start()

    m_ref[...] = jnp.full(m_ref.shape, NEG, F32)
    acc_ref[...] = jnp.zeros(acc_ref.shape, F32)
    first = lax.broadcasted_iota(jnp.int32, (16, bk), 0) == 0
    for h in range(heads):
        for c in range(n * per):
            v2_ref[h, c, HD : HD + 16, :] = jnp.where(first, 1.0, 0.0).astype(BF)

    def att_remote(h, i):
        return remote(ob_ref.at[h, i], att_ref.at[h, z], os_sem.at[h, i], or_sem.at[h, z], {"tensor": i})

    def att_own(h):
        return pltpu.make_async_copy(ob_ref.at[h, z], att_ref.at[h, z], oo_sem.at[h])

    def enter(c):
        for o in range(0, rows, bk):
            at = pl.ds(pl.multiple_of(c * rows + o, bk), bk)
            cos, sin = cos_ref[:, at], sin_ref[:, at]
            proj = dg(w_ref[...], normed_ref[c, o : o + bk, :], 1, 1) + b_ref[...]
            for h in range(heads):
                r0 = h * 3 * HD
                parts = []
                for part in range(2):
                    u = proj[r0 + part * HD : r0 + (part + 1) * HD]
                    f, b = u[: HD // 2], u[HD // 2 :]
                    parts.append(jnp.concatenate([f * cos - b * sin, b * cos + f * sin], axis=0))
                q = parts[0].astype(BF)
                v = proj[r0 + 2 * HD : r0 + 3 * HD].astype(BF)
                qkv_ref[h, c, 0, :, o : o + bk] = q
                qkv_ref[h, c, 1, :, o : o + bk] = parts[1].astype(BF)
                qkv_ref[h, c, 2, :, o : o + bk] = v
                q2_ref[h, c, :, o : o + bk] = split_query(q)
                kt = parts[1].T.astype(BF)
                k2_ref[h, c * per + o // bk] = jnp.concatenate([kt, kt], axis=1)
                v2_ref[h, c * per + o // bk, 0:HD, :] = v

    def pair(q, k, masked):
        for h in range(heads):
            for b in range(per):
                kj, vj = k2_ref[h, k * per + b], v2_ref[h, k * per + b]
                for s0 in range(0, rows, sub):
                    sl = slice(s0, s0 + sub)
                    s = dg(kj, q2_ref[h, q, :, sl], 1, 0)
                    if masked:
                        s = jnp.where(visible(k * rows + b * bk, q * rows + s0, bk, sub, prefix), s, NEG)
                    m = m_ref[h, q, :, sl]
                    mn = jnp.maximum(m, jnp.max(s, axis=0, keepdims=True))
                    p = jnp.exp2(s - mn).astype(BF)
                    scale = jnp.exp2(m - mn)
                    m_ref[h, q, :, sl] = mn
                    acc_ref[h, q, :, sl] = acc_ref[h, q, :, sl] * scale + dg(vj, p, 1, 0)

    def finish(q):
        for h in range(heads):
            total = acc_ref[h, q, HD : HD + 1, :]
            out = acc_ref[h, q, 0:HD, :] / total
            of_ref[h, q] = out
            lse_ref[h, q] = m_ref[h, q] + jnp.log2(total)
            ob_ref[h, q] = out.astype(BF)

            @pl.when(z != q)
            def _(h=h):
                att_remote(h, q).start()

            @pl.when(z == q)
            def _(h=h):
                att_own(h).start()

    def relay(s):
        @pl.when((s < n) & (z - s >= 0))
        def _():
            from_left(s).wait_recv()

        @pl.when((s + 1 < n) & has_right(s + 1))
        def _():
            to_right(s + 1).start()

        @pl.when((s < n) & (z + s < n))
        def _():
            from_right(s).wait_recv()

        @pl.when((s + 1 < n) & has_left(s + 1))
        def _():
            to_left(s + 1).start()

    def event(e, carry):
        s = (e + 1) // 2
        low = e % 2 == 1
        high = (e % 2 == 0) & (e > 0)

        @pl.when(e == 1)
        def _():
            relay(1)
            gather_forward()

        @pl.when(high & (z + s >= n))
        def _():
            relay(s + 1)

        c = jnp.where(low, z - s, z + s)
        bottom = jnp.maximum(z - s, 0)
        start = jnp.where(low, c + 1, jnp.where(high, bottom, c))
        stop = jnp.where(low, jnp.minimum(n, z + s), c)

        @pl.when((c >= 0) & (c < n))
        def _():
            enter(c)
            all_low = low & (c == 0)

            def masked_pair(a, t):
                pair(jnp.minimum(a, c), jnp.maximum(a, c), True)
                return t

            inner = c < prefix_chunks
            masked_from = jnp.where(inner & high, start, c)
            masked_to = jnp.where(inner & low, jnp.minimum(stop, prefix_chunks), c + 1)

            @pl.when(all_low)
            def _():
                lax.fori_loop(masked_from, masked_to, masked_pair, 0)
                finish(c)

            def full_pair(turn, t):
                length = stop - start
                own = z - start + 1
                a = jnp.where(low, start + (turn - start + own) % jnp.maximum(length, 1), turn)
                pair(jnp.maximum(a, c), jnp.minimum(a, c), False)

                @pl.when(all_low)
                def _():
                    finish(a)

                return t

            lax.fori_loop(start, stop, full_pair, 0)

            @pl.when(high)
            def _():
                relay(s + 1)

            @pl.when(jnp.logical_not(all_low))
            def _():
                lax.fori_loop(masked_from, masked_to, masked_pair, 0)

            ready = (bottom == 0) & high & (c >= prefix_chunks - 1)
            from_q = jnp.where(c == prefix_chunks - 1, 0, c)

            def finish_one(q, t):
                finish(q)
                return t

            lax.fori_loop(from_q, jnp.where(ready, c + 1, from_q), finish_one, 0)

        return carry

    lax.fori_loop(0, 2 * n - 1, event, 0)
    gather_finish()
    for s in range(1, n):

        @pl.when(has_right(s))
        def _(s=s):
            to_right(s).wait_send()

        @pl.when(has_left(s))
        def _(s=s):
            to_left(s).wait_send()

    for h in range(heads):
        att_own(h).wait()
        for k in range(1, n):
            d = lax.rem(z + k, n)
            att_remote(h, d).wait_send()
            remote(ob_ref.at[h, d], att_ref.at[h, d], os_sem.at[h, d], or_sem.at[h, d], {"tensor": d}).wait_recv()


def attend(prefix, x, gain, shift, w, bias, cos_t, sin_t, shard, n, m, bk=1024, sub=1024):
    rows, width = x.shape
    heads = w.shape[0] // (3 * HD)
    length = n * rows
    vmem = pl.BlockSpec(memory_space=pltpu.VMEM)
    dma = pltpu.SemaphoreType.DMA
    return pl.pallas_call(
        functools.partial(fwd_kernel, n, m, heads, rows, bk, sub),
        in_specs=[pl.BlockSpec(memory_space=pltpu.SMEM)] + [vmem] * 7 + [pl.BlockSpec(memory_space=pl.ANY)],
        out_specs=[vmem] * 5 + [pl.BlockSpec(memory_space=pl.ANY)],
        out_shape=[
            jax.ShapeDtypeStruct((n, rows, width), BF),
            jax.ShapeDtypeStruct((heads, n, 3, HD, rows), BF),
            jax.ShapeDtypeStruct((heads, n, HD, rows), BF),
            jax.ShapeDtypeStruct((heads, n, HD, rows), F32),
            jax.ShapeDtypeStruct((heads, n, 1, rows), F32),
            jax.ShapeDtypeStruct((m, n) + shard.shape, BF),
        ],
        scratch_shapes=[
            pltpu.VMEM((heads, n, 2 * HD, rows), BF),
            pltpu.VMEM((heads, length // bk, bk, 2 * HD), BF),
            pltpu.VMEM((heads, length // bk, HD + 16, bk), BF),
            pltpu.VMEM((heads, n, 1, rows), F32),
            pltpu.VMEM((heads, n, HD + 16, rows), F32),
            pltpu.VMEM((heads, n, HD, rows), BF),
            dma((n - 1,)),
            dma((n - 1,)),
            dma((n - 1,)),
            dma((n - 1,)),
            dma((heads, n)),
            dma((heads, n)),
            dma((heads,)),
        ]
        + gather_sems(n, m),
        compiler_params=pltpu.CompilerParams(
            collective_id=0, has_side_effects=True, vmem_limit_bytes=60 * 2**20
        ),
        cost_estimate=pl.CostEstimate(
            flops=int(heads * 4 * 256 * length * length * 0.7),
            bytes_accessed=heads * length * HD * 20,
            transcendentals=int(heads * length * length * 0.7),
        ),
        name="attend_forward",
    )(prefix, x, gain.reshape(1, width), shift.reshape(1, width), w, bias[:, None], cos_t, sin_t, shard)


def small_kernel(n, m, x_ref, o_ref, zbuf, mid, pbuf, zs, zr, ps, pr):
    z = lax.axis_index("tensor")
    d = lax.axis_index("dp")
    greet([("tensor", n), ("dp", m)])

    def stage(axis, me, count, src, buf, send, recv):
        buf[me] = src[...]
        for k in range(1, count):
            peer = lax.rem(me + k, count)
            remote(src, buf.at[me], send.at[k - 1], recv.at[me], {axis: peer}).start()
        for k in range(1, count):
            peer = lax.rem(me + k, count)
            copy = remote(src, buf.at[peer], send.at[k - 1], recv.at[peer], {axis: peer})
            copy.wait_send()
            copy.wait_recv()
        total = buf[0]
        for k in range(1, count):
            total = total + buf[k]
        return total

    mid[...] = stage("tensor", z, n, x_ref, zbuf, zs, zr)
    o_ref[...] = stage("dp", d, m, mid, pbuf, ps, pr)


def total_small(vectors, n, m):
    sizes = [v.size for v in vectors]
    flat = jnp.concatenate([v.reshape(-1) for v in vectors])
    flat = jnp.pad(flat, (0, -flat.size % 1024)).reshape(-1, 128)
    vmem = pl.BlockSpec(memory_space=pltpu.VMEM)
    dma = pltpu.SemaphoreType.DMA
    summed = pl.pallas_call(
        functools.partial(small_kernel, n, m),
        in_specs=[vmem],
        out_specs=vmem,
        out_shape=jax.ShapeDtypeStruct(flat.shape, F32),
        scratch_shapes=[
            pltpu.VMEM((n,) + flat.shape, F32),
            pltpu.VMEM(flat.shape, F32),
            pltpu.VMEM((m,) + flat.shape, F32),
            dma((n - 1,)),
            dma((n,)),
            dma((m - 1,)),
            dma((m,)),
        ],
        compiler_params=pltpu.CompilerParams(collective_id=1, has_side_effects=True),
        name="total_small",
    )(flat).reshape(-1)
    out, at = [], 0
    for v, size in zip(vectors, sizes):
        out.append(summed[at : at + size].reshape(v.shape))
        at += size
    return out


def unrotate(front, back, c, s):
    return front * c + back * s, back * c - front * s


def bit_orders(m):
    bits = list(range(m.bit_length() - 1))
    return [bits, bits[:1] + bits[:0:-1], bits]


def bwd_kernel(n, heads, rows, bk, sub, m, *refs):
    steps = m.bit_length() - 1
    (pref_ref, send_ref, qkv_ref, of_ref, lse_ref, cos_ref, sin_ref, normed_ref), refs = refs[:8], refs[8:]
    parts, refs = refs[:3], refs[3:]
    (g_ref, back_ref), refs = refs[:2], refs[2:]
    (rw_ref,), results, refs = refs[:1], refs[1:4], refs[4:]
    (do_ref, q2_ref, qn_ref, don_ref, dd_ref, dq_ref, dk_ref, dv_ref), refs = refs[:8], refs[8:]
    (wv_ref, ws_ref, wb_ref, wf_ref), refs = refs[:4], refs[4:]
    tracks = []
    for tag, order in enumerate(bit_orders(m)):
        held, came, (zbuf, fin) = refs[0], refs[1 : steps + 1], refs[steps + 1 : steps + 3]
        refs = refs[steps + 3 :]
        tracks.append((tag, order, parts[tag], held, came, zbuf, fin, results[tag]))
    (own_sem, s_sem, r_sem, kvs, kvr, qs, qr, kvo, qo), refs = refs[:9], refs[9:]
    (hs, hr, ho, p2s, p2r, p2o, p3s, p3r, p3o, w1s, w1r, w1o, w2s, w2r, w2o) = refs
    z = lax.axis_index("tensor")
    dp = lax.axis_index("dp")
    length = n * rows
    per = rows // bk
    prefix_chunks = -(-(length // 2) // rows)
    greet([("tensor", n), ("dp", m)])

    def spread(axis, me, count, pick, dst, send, recv, own, tag):
        pltpu.make_async_copy(pick(me), dst.at[me], own.at[tag]).start()
        for k in range(1, count):
            d = lax.rem(me + k, count)
            remote(pick(d), dst.at[me], send.at[tag, k - 1], recv.at[tag, me], {axis: d}).start()

    def arrived(axis, me, count, pick, dst, recv, send, own, tag):
        pltpu.make_async_copy(pick(me), dst.at[me], own.at[tag]).wait()
        for k in range(1, count):
            d = lax.rem(me + k, count)
            copy = remote(pick(d), dst.at[d], send.at[tag, k - 1], recv.at[tag, d], {axis: d})
            copy.wait_send()
            copy.wait_recv()

    def own_bit(b):
        return (dp // 2**b) % 2

    def slice_of(order, bit, j):
        index = bit * 2 ** order[0]
        for place, b in enumerate(order[1:]):
            index = index + ((j >> place) & 1) * 2**b
        return index

    def place(order, i, last):
        at = last * 2 ** (i - 1)
        for k in range(1, i):
            at = at + own_bit(order[k]) * 2 ** (k - 1)
        return at

    def halve_copies(i):
        for tag, order, part, held, came, zbuf, fin, res in tracks:
            bit = own_bit(order[i])
            partner = dp + (1 - 2 * bit) * 2 ** order[i]
            for j in range(m >> (i + 1)):
                src = part.at[slice_of(order, 1 - bit, j)] if i == 0 else held.at[place(order, i, 1 - bit) + 2**i * j]
                yield tag, j, bit, order, remote(src, came[i].at[j], hs.at[tag, i, j], hr.at[tag, i, j], {"dp": partner})

    def kept_copies():
        for tag, order, part, held, came, zbuf, fin, res in tracks:
            for j in range(m // 2):
                src = part.at[slice_of(order, own_bit(order[0]), j)]
                yield pltpu.make_async_copy(src, held.at[j], ho.at[tag, j])

    def halve_start(i):
        for _, _, _, _, copy in halve_copies(i):
            copy.start()

    def halve_sum(i):
        if i == 0:
            for copy in kept_copies():
                copy.wait()
        for tag, j, bit, order, copy in halve_copies(i):
            copy.wait_send()
            copy.wait_recv()
            held, came = tracks[tag][3], tracks[tag][4]
            at = j if i == 0 else place(order, i, bit) + 2**i * j
            for t in range(n):
                held[at, t] = (held[at, t].astype(F32) + came[i][j, t].astype(F32)).astype(BF)

    def line_start():
        for tag, order, part, held, came, zbuf, fin, res in tracks:
            spread("tensor", z, n, lambda d, held=held, order=order: held.at[place(order, steps - 1, own_bit(order[-1])), d], zbuf, p2s, p2r, p2o, tag)

    def line_sum():
        for tag, order, part, held, came, zbuf, fin, res in tracks:
            arrived("tensor", z, n, lambda d, held=held, order=order: held.at[place(order, steps - 1, own_bit(order[-1])), d], zbuf, p2r, p2s, p2o, tag)
            total = zbuf[0].astype(F32)
            for k in range(1, n):
                total = total + zbuf[k].astype(F32)
            fin[...] = total.astype(BF)
            spread("dp", dp, m, lambda d, fin=fin: fin, res, p3s, p3r, p3o, tag)

    def after_last():
        for tag, order, part, held, came, zbuf, fin, res in tracks:
            arrived("dp", dp, m, lambda d, fin=fin: fin, res, p3r, p3s, p3o, tag)

    for copy in kept_copies():
        copy.start()
    halve_start(0)
    points = (0, 3, 4) if steps == 3 else tuple(range(steps))

    def at_point(e):
        for i, point in enumerate(points):

            @pl.when(e == point)
            def _(i=i):
                halve_sum(i)
                if i + 1 < steps:
                    halve_start(i + 1)
                else:
                    line_start()

        @pl.when(e == 2 * n + 1)
        def _():
            line_sum()

    def weight_start(h):
        grad = dg(g_ref[h, 0], normed_ref[0], 1, 0)
        for t in range(1, n):
            grad = grad + dg(g_ref[h, t], normed_ref[t], 1, 0)
        wv_ref[...] = grad
        q = 3 * HD // m
        for i in range(m):
            ws_ref[h, i] = wv_ref[i * q : (i + 1) * q].astype(BF)
        spread("dp", dp, m, lambda d: ws_ref.at[h, d], wb_ref.at[h], w1s, w1r, w1o, h)

    def weight_sum(h):
        arrived("dp", dp, m, lambda d: ws_ref.at[h, d], wb_ref.at[h], w1r, w1s, w1o, h)
        total = wb_ref[h, 0].astype(F32)
        for k in range(1, m):
            total = total + wb_ref[h, k].astype(F32)
        wf_ref[h] = total.astype(BF)
        spread("dp", dp, m, lambda d: wf_ref.at[h], rw_ref.at[h], w2s, w2r, w2o, h)

    def weight_end(h):
        arrived("dp", dp, m, lambda d: wf_ref.at[h], rw_ref.at[h], w2r, w2s, w2o, h)

    def do_copy(h, k):
        d = lax.rem(z + k, n)
        return remote(send_ref.at[d, h], do_ref.at[h, z], s_sem.at[h, k - 1], r_sem.at[h, k - 1], {"tensor": d})

    def own_copy(h):
        return pltpu.make_async_copy(send_ref.at[z, h], do_ref.at[h, z], own_sem.at[h])

    def do_start(h):
        own_copy(h).start()
        for k in range(1, n):
            do_copy(h, k).start()

    do_start(0)
    prefix = pref_ref[0]
    kv_rows, q_rows = pl.ds(HD, 2 * HD), pl.ds(0, HD)

    def piece(h, t, part, source, send, recv):
        return remote(
            g_ref.at[h, t, part], back_ref.at[source, h, part], send.at[h, t], recv.at[h, source], {"tensor": t}
        )

    def own_piece(h, part, sem):
        return pltpu.make_async_copy(g_ref.at[h, z, part], back_ref.at[z, h, part], sem.at[h])

    def hand_out(h, t, part, send, recv, own):
        @pl.when(z != t)
        def _():
            piece(h, t, part, z, send, recv).start()

        @pl.when(z == t)
        def _():
            own_piece(h, part, own).start()

    def head(h, carry):
        own_copy(h).wait()
        for k in range(1, n):
            do_copy(h, k).wait_recv()

        @pl.when(h + 1 < heads)
        def _():
            do_start(h + 1)

        for c in range(n):
            q = qkv_ref[h, c, 0]
            q2_ref[c] = split_query(q)
            qn_ref[c] = q.astype(F32).T.astype(BF)
            dof = do_ref[h, c].astype(F32)
            don_ref[c] = dof.T.astype(BF)
            inner = jnp.sum(dof * of_ref[h, c], axis=0, keepdims=True)
            dd_ref[c] = jnp.concatenate([inner, lse_ref[h, c]], axis=0)
            dq_ref[c] = jnp.zeros((HD, rows), F32)

        def keys(turn, c1):
            t = lax.rem(z + 1 + turn, n)
            for o in range(0, rows, bk):
                kt = qkv_ref[h, t, 1, :, o : o + bk]
                kn = kt.astype(F32).T.astype(BF)
                k2 = jnp.concatenate([kn, kn], axis=1)
                vn = qkv_ref[h, t, 2, :, o : o + bk].astype(F32).T.astype(BF)
                dk_ref[...] = jnp.zeros(dk_ref.shape, F32)
                dv_ref[...] = jnp.zeros(dv_ref.shape, F32)

                def block(i, masked, o=o, kt=kt, k2=k2, vn=vn):
                    for s0 in range(0, rows, sub):
                        sl = slice(s0, s0 + sub)
                        p = jnp.exp2(dg(k2, q2_ref[i, :, sl], 1, 0) - dd_ref[i, 1:2, sl])
                        if masked:
                            p = jnp.where(visible(t * rows + o, i * rows + s0, bk, sub, prefix), p, 0.0)
                        dp = dg(vn, do_ref[h, i, :, sl], 1, 0)
                        dv_ref[...] += dg(p.astype(BF), don_ref[i, sl, :], 1, 0)
                        ds = (p * (dp - dd_ref[i, 0:1, sl])).astype(BF)
                        dk_ref[...] += dg(ds, qn_ref[i, sl, :], 1, 0)
                        dq_ref[i, :, sl] += dg(kt, ds, 1, 0)

                def masked_block(i, c2, block=block):
                    block(i, True)
                    return c2

                def full_block(i, c2, block=block):
                    block(i, False)
                    return c2

                lax.fori_loop(jnp.where(t < prefix_chunks, 0, t), t + 1, masked_block, 0)
                lax.fori_loop(t + 1, n, full_block, 0)
                dk = dk_ref[...].T * HD**-0.5
                at = pl.ds(pl.multiple_of(t * rows + o, bk), bk)
                a, b = unrotate(dk[: HD // 2], dk[HD // 2 :], cos_ref[:, at], sin_ref[:, at])
                g_ref[h, t, HD : HD + HD // 2, o : o + bk] = a.astype(BF)
                g_ref[h, t, HD + HD // 2 : 2 * HD, o : o + bk] = b.astype(BF)
                g_ref[h, t, 2 * HD : 3 * HD, o : o + bk] = dv_ref[...].T.astype(BF)
            hand_out(h, t, kv_rows, kvs, kvr, kvo)
            at_point(h * n + turn)
            return c1

        lax.fori_loop(0, n, keys, 0)
        for c in range(n):
            x = dq_ref[c] * HD**-0.5
            at = slice(c * rows, (c + 1) * rows)
            a, b = unrotate(x[: HD // 2], x[HD // 2 :], cos_ref[:, at], sin_ref[:, at])
            g_ref[h, c, : HD // 2, :] = a.astype(BF)
            g_ref[h, c, HD // 2 : HD, :] = b.astype(BF)
            hand_out(h, c, q_rows, qs, qr, qo)
        weight_start(h)

        @pl.when(h > 0)
        def _():
            weight_sum(h - 1)

        return carry

    lax.fori_loop(0, heads, head, 0)
    weight_sum(heads - 1)
    after_last()
    for h in range(heads):
        weight_end(h)
    for h in range(heads):
        own_piece(h, kv_rows, kvo).wait()
        own_piece(h, q_rows, qo).wait()
        for k in range(1, n):
            do_copy(h, k).wait_send()
            d = lax.rem(z + k, n)
            for part, send, recv in ((kv_rows, kvs, kvr), (q_rows, qs, qr)):
                copy = piece(h, d, part, d, send, recv)
                copy.wait_send()
                copy.wait_recv()


def attend_back(prefix, send, qkv, of, lse, cos_t, sin_t, normed, parts, bk=512, sub=256):
    n, heads, _, rows = send.shape
    m, width = parts[0].shape[0], parts[0].shape[-1]
    steps = m.bit_length() - 1
    size_w = 3 * HD // m
    length = n * rows
    vmem = pl.BlockSpec(memory_space=pltpu.VMEM)
    dma = pltpu.SemaphoreType.DMA
    buffers = []
    for part in parts:
        size = part.shape[2]
        for count in [m // 2] + [m >> (i + 1) for i in range(steps)]:
            buffers.append(pltpu.VMEM((count, n, size, width), BF))
        buffers += [pltpu.VMEM((n, size, width), BF), pltpu.VMEM((size, width), BF)]
    return pl.pallas_call(
        functools.partial(bwd_kernel, n, heads, rows, bk, sub, m),
        in_specs=[pl.BlockSpec(memory_space=pltpu.SMEM)] + [vmem] * 7 + [pl.BlockSpec(memory_space=pl.ANY)] * 3,
        out_specs=[vmem] * 6,
        out_shape=[
            jax.ShapeDtypeStruct((heads, n, 3 * HD, rows), BF),
            jax.ShapeDtypeStruct((n, heads, 3 * HD, rows), BF),
            jax.ShapeDtypeStruct((heads, m, size_w, width), BF),
        ]
        + [jax.ShapeDtypeStruct((m, part.shape[2], width), BF) for part in parts],
        scratch_shapes=[
            pltpu.VMEM((heads, n, HD, rows), BF),
            pltpu.VMEM((n, 2 * HD, rows), BF),
            pltpu.VMEM((n, rows, HD), BF),
            pltpu.VMEM((n, rows, HD), BF),
            pltpu.VMEM((n, 2, rows), F32),
            pltpu.VMEM((n, HD, rows), F32),
            pltpu.VMEM((bk, HD), F32),
            pltpu.VMEM((bk, HD), F32),
            pltpu.VMEM((3 * HD, width), F32),
            pltpu.VMEM((heads, m, size_w, width), BF),
            pltpu.VMEM((heads, m, size_w, width), BF),
            pltpu.VMEM((heads, size_w, width), BF),
        ]
        + buffers
        + [
            dma((heads,)),
            dma((heads, n - 1)),
            dma((heads, n - 1)),
            dma((heads, n)),
            dma((heads, n)),
            dma((heads, n)),
            dma((heads, n)),
            dma((heads,)),
            dma((heads,)),
            dma((3, steps, m // 2)),
            dma((3, steps, m // 2)),
            dma((3, m // 2)),
            dma((3, n - 1)),
            dma((3, n)),
            dma((3,)),
            dma((3, m - 1)),
            dma((3, m)),
            dma((3,)),
            dma((heads, m - 1)),
            dma((heads, m)),
            dma((heads,)),
            dma((heads, m - 1)),
            dma((heads, m)),
            dma((heads,)),
        ],
        compiler_params=pltpu.CompilerParams(
            collective_id=2, has_side_effects=True, vmem_limit_bytes=63 * 2**20
        ),
        cost_estimate=pl.CostEstimate(
            flops=int(heads * 10 * 256 * length * length * 0.7),
            bytes_accessed=heads * length * HD * 20,
            transcendentals=int(heads * length * length * 0.7),
        ),
        name="attend_backward",
    )(prefix, send, qkv, of, lse, cos_t, sin_t, normed, *parts)


EPS = 1e-05
ROPE_BASE = 10000.0
GELU_C = 0.7978845608028654


def layer_norm(values, norm_gain, norm_shift):
    center = values - jnp.mean(values, axis=-1, keepdims=True)
    spread = jnp.mean(center * center, axis=-1, keepdims=True)
    return center * lax.rsqrt(spread + EPS) * norm_gain + norm_shift


def rotary_tables(length):
    half_dim = HD // 2
    frequency = ROPE_BASE ** (-jnp.arange(half_dim, dtype=jnp.float32) / half_dim)
    angles = frequency[:, None] * jnp.arange(length, dtype=jnp.float32)[None, :]
    return (jnp.cos(angles), jnp.sin(angles))


def mlp_kernel(
    split, size, block, n, m, nm_ref, gm_ref, w_ref, upb_ref, shard_ref, out_ref, dnm_ref, dup_ref, ddown_ref, dupb_ref,
    every_ref, nmt_ref, gmt_ref, act_ref, gp_ref, *gather,
):
    step = pl.program_id(0)
    gather_start, gather_forward, gather_finish = gatherer(n, m, shard_ref, every_ref, *gather)

    @pl.when(step == 0)
    def _():
        greet([("tensor", n), ("dp", m)])
        gather_start()
        nmt_ref[...] = nm_ref[...].T
        gmt_ref[...] = gm_ref[...].T
        out_ref[...] = jnp.zeros(out_ref.shape, F32)
        dnm_ref[...] = jnp.zeros(dnm_ref.shape, F32)

    width = w_ref.shape[-1]
    up = w_ref[:, :size].reshape(split * size, width)
    down = w_ref[:, size : 2 * size].reshape(split * size, width)
    for r in range(0, nm_ref.shape[0], block):
        at = slice(r, r + block)
        pre = dg(nm_ref[at], up, 1, 0) + upb_ref[...]
        sq = pre * pre
        th = jnp.tanh(GELU_C * (pre + 0.044715 * sq * pre))
        half = 0.5 * (1.0 + th)
        act = (pre * half).astype(BF)
        slope = half + 0.5 * pre * (1.0 - th * th) * (GELU_C + (3.0 * 0.044715 * GELU_C) * sq)
        gp = (dg(gm_ref[at], down, 1, 1) * slope).astype(BF)
        act_ref[at] = act
        gp_ref[at] = gp
        out_ref[at] += dg(act, down, 1, 0)
        dnm_ref[at] += dg(gp, up, 1, 1)
    dup_ref[...] = dg(nmt_ref[...], gp_ref[...], 1, 0).astype(BF).reshape(split, size, width)
    ddown_ref[...] = dg(gmt_ref[...], act_ref[...], 1, 0).astype(BF).reshape(split, size, width)
    dupb_ref[...] = jnp.sum(gp_ref[...].astype(F32), axis=0, keepdims=True)

    @pl.when(step == 0)
    def _():
        gather_forward()

    @pl.when(step == n - 1)
    def _():
        gather_finish()


def mlp(nm, gm, weights, up_bias, size, shard, m, block=256):
    rows, width = nm.shape
    split, n, deep, _ = weights.shape
    f = split * size
    squeezed = pl.Squeezed()
    const = pl.BlockSpec((rows, width), lambda i: (0, 0))
    hidden = n * f
    return pl.pallas_call(
        functools.partial(mlp_kernel, split, size, block, n, m),
        grid=(n,),
        in_specs=[
            const,
            const,
            pl.BlockSpec((split, squeezed, deep, width), lambda i: (0, i, 0, 0)),
            pl.BlockSpec((1, f), lambda i: (0, i)),
            pl.BlockSpec(memory_space=pl.ANY),
        ],
        out_specs=[
            const,
            const,
            pl.BlockSpec((split, squeezed, size, width), lambda i: (0, i, 0, 0)),
            pl.BlockSpec((split, squeezed, size, width), lambda i: (0, i, 0, 0)),
            pl.BlockSpec((1, f), lambda i: (0, i)),
            pl.BlockSpec(memory_space=pl.ANY),
        ],
        out_shape=[
            jax.ShapeDtypeStruct((rows, width), F32),
            jax.ShapeDtypeStruct((rows, width), F32),
            jax.ShapeDtypeStruct((split, n, size, width), BF),
            jax.ShapeDtypeStruct((split, n, size, width), BF),
            jax.ShapeDtypeStruct((1, hidden), F32),
            jax.ShapeDtypeStruct((m, n) + shard.shape, BF),
        ],
        scratch_shapes=[pltpu.VMEM((width, rows), BF)] * 2 + [pltpu.VMEM((rows, f), BF)] * 2 + gather_sems(n, m),
        compiler_params=pltpu.CompilerParams(collective_id=3, has_side_effects=True, vmem_limit_bytes=60 * 2**20),
        cost_estimate=pl.CostEstimate(
            flops=12 * rows * width * hidden, bytes_accessed=8 * width * hidden + 12 * rows * width, transcendentals=rows * hidden
        ),
        name="mlp",
    )(nm, gm, weights, up_bias, shard)


def norm_backward(values, gain, grad):
    center = values - jnp.mean(values, axis=-1, keepdims=True)
    rstd = lax.rsqrt(jnp.mean(center * center, axis=-1, keepdims=True) + EPS)
    hat = center * rstd
    scaled = grad * gain
    result = rstd * (
        scaled - jnp.mean(scaled, axis=-1, keepdims=True) - hat * jnp.mean(scaled * hat, axis=-1, keepdims=True)
    )
    return result, grad * hat


def column_sum(value):
    return jnp.sum(value, axis=0, keepdims=True)


def middle_kernel(
    n, heads, coef_ref, grad_ref, middle_ref, mlp_ref, top_ref, embed_ref, history_ref, gain_ref, bias_ref, out_w_ref, att_ref,
    gm_ref, mixed_ref, send_ref, out_grad_ref, vec_ref, ga_ref,
):
    step = pl.program_id(0)
    block = grad_ref.shape[0]

    @pl.when(step == 0)
    def _():
        vec_ref[...] = jnp.zeros(vec_ref.shape, F32)

    dy, middle, top = grad_ref[...], middle_ref[...], top_ref[...].astype(F32)
    back, scaled = norm_backward(middle, gain_ref[...], dy)
    branch = coef_ref[4] * top
    gm = branch + back
    gm_ref[...] = gm
    ga = gm.astype(BF)
    ga_ref[pl.ds(pl.multiple_of(step * block, block), block), :] = ga
    block_out = middle + (mlp_ref[...] + bias_ref[...])
    embed = embed_ref[...].astype(F32)
    mixed = coef_ref[0] * embed + coef_ref[4] * block_out
    rows = [scaled, dy, ga.astype(F32), branch.astype(BF).astype(F32), top * embed, top * block_out]
    for k in range(3):
        past = history_ref[k].astype(F32)
        mixed = mixed + coef_ref[1 + k] * past
        rows.append(top * past)
    mixed_ref[...] = mixed.astype(BF)
    for k, value in enumerate(rows):
        vec_ref[k : k + 1] += column_sum(value)

    @pl.when(step == pl.num_programs(0) - 1)
    def _():
        for d in range(n):
            got = dg(out_w_ref[d], ga_ref[...], 1, 1).astype(BF)
            for h in range(heads):
                send_ref[d, h] = got[h * HD : (h + 1) * HD]
        for h in range(heads):
            got = dg(att_ref[h], ga_ref[...], 1, 0).astype(BF)
            for d in range(n):
                out_grad_ref[d, h * HD : (h + 1) * HD] = got[d * HD : (d + 1) * HD]


def middle_back(coefs, grad, middle, mlp_out, top, embed, history, gain, bias, out_w, attended, block=256):
    rows, width = grad.shape
    n, local, _ = out_w.shape
    heads = local // HD
    whole = lambda shape: pl.BlockSpec(shape, lambda i: (0,) * len(shape))
    by_row = pl.BlockSpec((block, width), lambda i: (i, 0))
    return pl.pallas_call(
        functools.partial(middle_kernel, n, heads),
        grid=(rows // block,),
        in_specs=[
            pl.BlockSpec(memory_space=pltpu.SMEM),
            by_row,
            by_row,
            by_row,
            by_row,
            by_row,
            pl.BlockSpec((3, block, width), lambda i: (0, i, 0)),
            whole((1, width)),
            whole((1, width)),
            whole((n, local, width)),
            whole((heads, n * HD, rows)),
        ],
        out_specs=[by_row, by_row, whole((n, heads, HD, rows)), whole((n, local, width)), whole((16, width))],
        out_shape=[
            jax.ShapeDtypeStruct((rows, width), F32),
            jax.ShapeDtypeStruct((rows, width), BF),
            jax.ShapeDtypeStruct((n, heads, HD, rows), BF),
            jax.ShapeDtypeStruct((n, local, width), BF),
            jax.ShapeDtypeStruct((16, width), F32),
        ],
        scratch_shapes=[pltpu.VMEM((rows, width), BF)],
        compiler_params=pltpu.CompilerParams(vmem_limit_bytes=48 * 2**20),
        cost_estimate=pl.CostEstimate(
            flops=4 * rows * width * width, bytes_accessed=30 * rows * width, transcendentals=rows
        ),
        name="middle_back",
    )(
        coefs,
        grad,
        middle,
        mlp_out,
        top,
        embed,
        history,
        gain.reshape(1, width),
        bias.reshape(1, width),
        out_w,
        attended.reshape(heads, n * HD, rows),
    )


def input_kernel(n, split, back_ref, w_ref, x_ref, gm_ref, gain_ref, out_ref, vec_ref):
    step = pl.program_id(0)

    @pl.when(step == 0)
    def _():
        vec_ref[...] = jnp.zeros(vec_ref.shape, F32)

    cols, width = w_ref.shape[-1], x_ref.shape[-1]
    total = None
    for d in range(n):
        w = w_ref[:, d].reshape(width, cols)
        term = dg(w, back_ref[d], 1, 0)
        total = term if total is None else total + term
    dy = total.T
    back, scaled = norm_backward(x_ref[...].astype(F32), gain_ref[...], dy)
    out_ref[...] = gm_ref[...] + back
    vec_ref[0:1] += column_sum(scaled)
    vec_ref[1:2] += column_sum(dy)


def input_back(back, w_every, x, grad_middle, gain, block=256):
    rows, width = x.shape
    n, cols, _ = back.shape
    split = w_every.shape[0]
    row_block = pl.BlockSpec((block, width), lambda i: (i, 0))
    return pl.pallas_call(
        functools.partial(input_kernel, n, split),
        grid=(rows // block,),
        in_specs=[
            pl.BlockSpec((n, cols, block), lambda i: (0, 0, i)),
            pl.BlockSpec(w_every.shape, lambda i: (0, 0, 0, 0)),
            row_block,
            row_block,
            pl.BlockSpec((1, width), lambda i: (0, 0)),
        ],
        out_specs=[row_block, pl.BlockSpec((8, width), lambda i: (0, 0))],
        out_shape=[jax.ShapeDtypeStruct((rows, width), F32), jax.ShapeDtypeStruct((8, width), F32)],
        compiler_params=pltpu.CompilerParams(vmem_limit_bytes=48 * 2**20),
        cost_estimate=pl.CostEstimate(
            flops=2 * rows * width * n * cols, bytes_accessed=12 * rows * width + 2 * n * cols * (rows + width), transcendentals=rows
        ),
        name="input_back",
    )(back, w_every, x, grad_middle, gain.reshape(1, width))


def shards(
    block_input,
    embedding,
    history,
    cotangent,
    first_gain,
    first_shift,
    qkv_weight,
    qkv_bias,
    out_weight,
    out_bias,
    second_gain,
    second_shift,
    up_weight,
    up_bias,
    down_weight,
    down_bias,
    depth_weights,
    prefix_length,
    history_index,
):
    rows, width = block_input.shape
    local = qkv_weight.shape[2]
    heads = local // HD
    n = lax.axis_size("tensor")
    m = lax.axis_size("dp")
    z = lax.axis_index("tensor")
    dp = lax.axis_index("dp")
    length = rows * n
    hidden = up_weight.shape[1]
    cos_t, sin_t = rotary_tables(length)

    w_t = qkv_weight.reshape(width, 3, heads, HD).transpose(2, 1, 3, 0).reshape(3 * local, width)
    w_f = qkv_weight.reshape(width, 3, heads, HD).transpose(0, 2, 1, 3).reshape(width, 3 * local)
    b_t = qkv_bias.reshape(3, heads, HD).transpose(1, 0, 2).reshape(3 * local).astype(F32)
    def mine(shard):
        size = shard.shape[0] // m
        return lax.dynamic_slice_in_dim(shard, dp * size, size, 0)

    size, out_size = width // m, local // m
    used = 2 * size + out_size
    fill = jnp.zeros((15 - used % 16, width), BF)
    early = jnp.concatenate([mine(up_weight), mine(down_weight), mine(out_weight), up_bias[None], fill], axis=0)
    normed, qkv_t, attended, of, lse, every = attend(
        prefix_length, block_input, first_gain, first_shift, w_t, b_t, cos_t, sin_t, early, n, m
    )
    out_all = every[:, :, 2 * size : used].transpose(1, 0, 2, 3).reshape(n, heads, HD, width)
    up_bias_all = every[0, :, used, :hidden].astype(F32).reshape(1, n * hidden)

    inputs_f = block_input.astype(F32)
    attn = None
    for h in range(heads):
        piece = dg(attended[h].reshape(n * HD, rows), out_all[:, h].reshape(n * HD, width), 0, 0)
        attn = piece if attn is None else attn + piece


    middle = inputs_f + (attn + out_bias.astype(F32))
    normed_mid_f = layer_norm(middle, second_gain, second_shift)
    grad_top = cotangent.astype(F32)
    grad_block = depth_weights[4] * grad_top
    grad_branch = grad_block.astype(BF)
    if size % 16 == 0:
        mlp_weights, part = every, size
    else:
        whole = every[:, :, : 2 * size].reshape(m, n, 2, size, width)
        mlp_weights, part = whole.transpose(1, 2, 0, 3, 4).reshape(1, n, 2 * hidden, width), hidden
    mlp_out, grad_normed_mid, up_grad, down_grad, up_bias_grad, w_every = mlp(
        normed_mid_f.astype(BF), grad_branch, mlp_weights, up_bias_all, part, mine(w_f), m
    )
    if size % 16 != 0:
        up_grad = up_grad.reshape(n, m, size, width).transpose(1, 0, 2, 3)
        down_grad = down_grad.reshape(n, m, size, width).transpose(1, 0, 2, 3)
    slot_ids = jnp.arange(3, dtype=jnp.int32)
    pick = (history_index[:, None] == slot_ids[None, :]).astype(F32)
    slot_coef = jnp.sum(depth_weights[1:4, None] * pick, axis=0)
    coefs = jnp.concatenate([depth_weights[:1], slot_coef, depth_weights[4:]])
    grad_middle, dwa_output, grad_send, out_grad, middle_sums = middle_back(
        coefs,
        grad_normed_mid,
        middle,
        mlp_out,
        cotangent,
        embedding,
        history,
        second_gain,
        down_bias.astype(F32),
        out_all.reshape(n, local, width),
        attended,
    )
    middle_sums = middle_sums[:9]
    out_grad = out_grad.reshape(n, m, out_size, width).transpose(1, 0, 2, 3)
    grad_own, back, qkv_sum, up_sum, down_sum, out_sum = attend_back(
        prefix_length, grad_send, qkv_t, of, lse, cos_t, sin_t, normed, (up_grad, down_grad, out_grad)
    )
    if size % 16 != 0:
        w_every = w_every.transpose(1, 0, 2, 3).reshape(1, n, width, 3 * local)
    qkv_bias_grad = jnp.sum(grad_own.astype(F32), axis=(1, 3)).reshape(-1)
    grad_input, input_sums = input_back(
        back.reshape(n, 3 * local, rows), w_every, block_input, grad_middle, first_gain
    )
    up_grad = up_sum.reshape(width, hidden).astype(F32)
    down_grad = down_sum.reshape(width, hidden).T.astype(F32)
    out_grad = out_sum.reshape(local, width).astype(F32)
    qkv_grad = qkv_sum.reshape(heads, 3, HD, width).transpose(3, 1, 0, 2).reshape(width, 3, local).astype(F32)

    spread = jnp.zeros((n, 3 * local), F32)
    spread = lax.dynamic_update_slice_in_dim(spread, qkv_bias_grad[None], z, 0)
    middle_sums, up_bias_grad, qkv_bias_grad, input_sums = total_small(
        [middle_sums, up_bias_grad[0], spread, input_sums[:2]], n, m
    )
    second_gain_grad, second_shift_grad, out_bias_grad, down_bias_grad = [middle_sums[k] for k in range(4)]
    depth_sums = jnp.sum(middle_sums[4:], axis=1)
    grad_depth = jnp.concatenate(
        [depth_sums[:1], jnp.sum(pick * depth_sums[None, 2:], axis=1), depth_sums[1:2]]
    )
    first_gain_grad, first_shift_grad = input_sums[0], input_sums[1]
    up_bias_grad = lax.dynamic_slice_in_dim(up_bias_grad, z * hidden, hidden, 0)
    qkv_bias_grad = lax.dynamic_index_in_dim(qkv_bias_grad, z, 0, keepdims=False)
    qkv_bias_grad = qkv_bias_grad.reshape(heads, 3, HD).transpose(1, 0, 2).reshape(3, local)
    return (
        dwa_output,
        grad_input,
        first_gain_grad,
        first_shift_grad,
        qkv_grad,
        qkv_bias_grad,
        out_grad,
        out_bias_grad,
        second_gain_grad,
        second_shift_grad,
        up_grad,
        up_bias_grad,
        down_grad,
        down_bias_grad,
        grad_depth,
    )


def solution(mesh):
    both = ("dp", "tensor")
    return jax.shard_map(
        shards,
        mesh=mesh,
        in_specs=(
            P(both, None),
            P(both, None),
            P(None, both, None),
            P(both, None),
            P(),
            P(),
            P(None, None, "tensor"),
            P(None, "tensor"),
            P("tensor", None),
            P(),
            P(),
            P(),
            P(None, "tensor"),
            P("tensor"),
            P("tensor", None),
            P(),
            P(),
            P("dp"),
            P(),
        ),
        out_specs=(
            P(both, None),
            P(both, None),
            P(),
            P(),
            P(None, None, "tensor"),
            P(None, "tensor"),
            P("tensor", None),
            P(),
            P(),
            P(),
            P(None, "tensor"),
            P("tensor"),
            P("tensor", None),
            P(),
            P(),
        ),
        check_vma=False,
    )
```
